32 devices in a mesh: dp: 8 (over y, x, core), fsdp: 4 (over z).
Axes of the slice: x: 2, y: 2, z: 4, core: 2. Of those that a mesh axis runs over, the one named last changes fastest.
Arguments:
- tokens: bfloat16 [32768, 1024], P(('dp', 'fsdp')), may hold values from -6 to 6
- prefix_len: int32 [32], P(('dp', 'fsdp')), may hold values from 64 to 256
- padding_len: int32 [32], P(('dp', 'fsdp')), may hold values from 0 to 384
- first_gain: bfloat16 [1024], P(('dp', 'fsdp')), may hold values from 0.5 to 1.5
- first_shift: bfloat16 [1024], P(('dp', 'fsdp')), may hold values from -4 to 4
- inproj_weight: bfloat16 [1024, 3072], P(('dp', 'fsdp')), may hold values from -0.1875 to 0.1875
- query_bias: bfloat16 [1024], P(('dp', 'fsdp')), may hold values from -4 to 4
- value_bias: bfloat16 [1024], P(('dp', 'fsdp')), may hold values from -4 to 4
- outproj_weight: bfloat16 [1024, 1024], P(('dp', 'fsdp')), may hold values from -1.5 to 1.5
- outproj_bias: bfloat16 [1024], P(('dp', 'fsdp')), may hold values from -4 to 4
- second_gain: bfloat16 [1024], P(('dp', 'fsdp')), may hold values from 0.5 to 1.5
- second_shift: bfloat16 [1024], P(('dp', 'fsdp')), may hold values from -4 to 4
- up_weight: bfloat16 [1024, 4096], P(('dp', 'fsdp')), may hold values from -0.1875 to 0.1875
- up_bias: bfloat16 [4096], P(('dp', 'fsdp')), may hold values from -4 to 4
- down_weight: bfloat16 [4096, 1024], P(('dp', 'fsdp')), may hold values from -0.09375 to 0.09375
- down_bias: bfloat16 [1024], P(('dp', 'fsdp')), may hold values from -4 to 4
- grad_out: bfloat16 [32768, 1024], P(('dp', 'fsdp')), may hold values from -6 to 6
Outputs:
- out_tokens: bfloat16 [32768, 1024], P(('dp', 'fsdp'))
- tokens_grad: bfloat16 [32768, 1024], P(('dp', 'fsdp'))
- first_gain_grad: float32 [1024], P(('dp', 'fsdp'))
- first_shift_grad: float32 [1024], P(('dp', 'fsdp'))
- inproj_grad: float32 [1024, 3072], P(('dp', 'fsdp'))
- query_bias_grad: float32 [1024], P(('dp', 'fsdp'))
- value_bias_grad: float32 [1024], P(('dp', 'fsdp'))
- outproj_grad: float32 [1024, 1024], P(('dp', 'fsdp'))
- outbias_grad: float32 [1024], P(('dp', 'fsdp'))
- second_gain_grad: float32 [1024], P(('dp', 'fsdp'))
- second_shift_grad: float32 [1024], P(('dp', 'fsdp'))
- up_grad: float32 [1024, 4096], P(('dp', 'fsdp'))
- upbias_grad: float32 [4096], P(('dp', 'fsdp'))
- down_grad: float32 [4096, 1024], P(('dp', 'fsdp'))
- downbias_grad: float32 [1024], P(('dp', 'fsdp'))
The draws below stay inside these ranges and needn't reach their ends.
All inputs are finite; a program needn't handle non-finite values.
Results may differ from the reference program's by a relative error of at most 0.013.
Values may be sent and summed in bfloat16 or wider, within the bound.
No kernel may reach another device: no remote copies, remote signals or barrier semaphores. Data moves between devices by JAX's collectives and lax.ppermute only.
A program may use at most 320 MiB of HBM per device.

```python
import math
import jax
import jax.numpy as jnp
from jax import lax

D = 1024
HEADS = 16
HEAD_DIM = 64
FF = 4096
LENGTH = 1024
SEQS = 32
TOKENS = 32768


def place_ends(values, stream_key, low, high):
    spot = [jax.random.randint(jax.random.fold_in(stream_key, axis), (), 0, length) for axis, length in enumerate(values.shape)]
    longest = values.shape.index(max(values.shape))
    beside = spot[:longest] + [(spot[longest] + 1) % values.shape[longest]] + spot[longest + 1:]
    return values.at[tuple(spot)].set(low).at[tuple(beside)].set(high)


def raised(entries, key, source, target, blocks, factor):
    def block_of(dim):
        return (jnp.arange(entries.shape[dim]) // (entries.shape[dim] // blocks)).reshape((-1,) + (1,) * (entries.ndim - 1 - dim))

    near = jax.random.permutation(key, blocks)[block_of(target)]
    far = (block_of(target) + blocks // 2) % blocks
    return jnp.where((block_of(source) == near) | (block_of(source) == far), factor * entries, entries)


def shard_levels(rng, extent, shards, low, high):
    def one(position, shards_of):
        draws = jax.random.uniform(jax.random.fold_in(jax.random.fold_in(rng, 6), position), (shards_of,), jnp.float32, low / len(shards), high / len(shards))
        return jnp.repeat(jnp.exp(draws), extent[position] // shards_of).reshape((-1,) + (1,) * (len(extent) - position - 1))

    loudness = one(*shards[0])
    for cut in shards[1:]:
        loudness = loudness * one(*cut)
    return loudness


def gaussian(key, shape, scale, most, split=(), held_as=jnp.bfloat16):
    drawn = scale * jax.random.normal(key, shape, jnp.float32)
    if split:
        drawn = drawn * shard_levels(key, shape, split, -0.22, 0.18)
    return jnp.clip(drawn, -most, most).astype(held_as)


def noise_with(own_key, shape, width, reach, split, heavy, kind=jnp.bfloat16):
    values = width * jax.random.normal(own_key, shape, jnp.float32)
    if split:
        values = values * shard_levels(own_key, shape, split, -0.22, 0.18)
    return jnp.clip(raised(values, jax.random.fold_in(own_key, 3), *heavy), -reach, reach).astype(kind)


def setup_inputs(seed: int = 0) -> dict:
    splits = jax.random.split(jax.random.key(seed), 18)
    return {
        "tokens": gaussian(splits[0], (TOKENS, D), 1.0, 6.0, ((0, 32),)),
        "prefix_len": place_ends(jax.random.randint(splits[1], (SEQS,), LENGTH // 16, LENGTH // 4 + 1), jax.random.fold_in(splits[1], 1), LENGTH // 16, (LENGTH // 4 + 1) - 1).astype(jnp.int32),
        "padding_len": place_ends(jax.random.randint(splits[2], (SEQS,), 0, 3 * LENGTH // 8 + 1), jax.random.fold_in(splits[2], 1), 0, (3 * LENGTH // 8 + 1) - 1).astype(jnp.int32),
        "first_gain": jnp.clip(1.0 + 0.1 * jax.random.normal(splits[3], (D,), jnp.float32), 0.5, 1.5).astype(jnp.bfloat16),
        "first_shift": gaussian(splits[4], (D,), 0.3, 4.0, ((0, 32),)),
        "inproj_weight": gaussian(splits[5], (D, 3 * D), D ** -0.5, 0.1875, ((0, 32),)),
        "query_bias": gaussian(splits[6], (D,), 0.3, 4.0, ((0, 32),)),
        "value_bias": gaussian(splits[7], (D,), 0.3, 4.0, ((0, 32),)),
        "outproj_weight": gaussian(splits[8], (D, D), (D // 64) ** -0.5, 1.5, ((0, 32),)),
        "outproj_bias": gaussian(splits[9], (D,), 0.3, 4.0, ((0, 32),)),
        "second_gain": jnp.clip(1.0 + 0.1 * jax.random.normal(splits[10], (D,), jnp.float32), 0.5, 1.5).astype(jnp.bfloat16),
        "second_shift": gaussian(splits[11], (D,), 0.3, 4.0, ((0, 32),)),
        "up_weight": gaussian(splits[12], (D, FF), D ** -0.5, 0.1875, ((0, 32),)),
        "up_bias": gaussian(splits[13], (FF,), 0.3, 4.0, ((0, 32),)),
        "down_weight": gaussian(splits[14], (FF, D), FF ** -0.5, 0.09375, ((0, 32),)),
        "down_bias": gaussian(splits[15], (D,), 0.3, 4.0, ((0, 32),)),
        "grad_out": noise_with(splits[16], (TOKENS, D), 1.0, 6.0, ((0, 32),), (0, 1, 32, 2.75)),
    }


EPSILON = 1e-05
NEGATIVE = -1000000000.0
HIGH = lax.Precision.HIGHEST

@jax.custom_vjp
def low(v):
    return lax.optimization_barrier(v.astype(jnp.bfloat16)).astype(jnp.float32)

@jax.custom_vjp
def low_back(v):
    return v

def low_keep(v):
    return (low(v), None)

def low_pass(kept, grad):
    return (grad,)

def back_keep(v):
    return (v, None)

def back_low(kept, grad):
    return (low(grad),)
low.defvjp(low_keep, low_pass)
low_back.defvjp(back_keep, back_low)

def layer_norm(values, gain, shift):
    center = values - lax.optimization_barrier(jnp.mean(values, axis=-1, keepdims=True))
    spread = lax.optimization_barrier(jnp.mean(center * center, axis=-1, keepdims=True))
    return center * lax.rsqrt(spread + EPSILON) * gain + shift

def attend(item):
    query, key_rows, value_rows, prefix, padding = item
    scores = jnp.einsum('qhd,khd->hqk', query, key_rows, precision=HIGH) * (1.0 / math.sqrt(HEAD_DIM))
    place = jnp.arange(LENGTH, dtype=jnp.int32)
    allowed = ((place[None, :] < prefix) | (place[None, :] <= place[:, None])) & (place[None, :] < LENGTH - padding)
    scores = low_back(jnp.where(allowed[None], scores, NEGATIVE))
    highest = lax.optimization_barrier(jnp.max(scores, axis=-1, keepdims=True))
    exponent = jnp.exp(scores - highest)
    probability = low(exponent / lax.optimization_barrier(jnp.sum(exponent, axis=-1, keepdims=True)))
    return jnp.einsum('hqk,khd->qhd', probability, value_rows, precision=HIGH).reshape(LENGTH, D)

def reference(tokens, prefix_len, padding_len, first_gain, first_shift, inproj_weight, query_bias, value_bias, outproj_weight, outproj_bias, second_gain, second_shift, up_weight, up_bias, down_weight, down_bias, grad_out):
    params = [p.astype(jnp.float32) for p in (first_gain, first_shift, inproj_weight, query_bias, value_bias, outproj_weight, outproj_bias, second_gain, second_shift, up_weight, up_bias, down_weight, down_bias)]

    def forward(xfloat, gain_one, shift_one, w_inproj, bias_query, bias_value, w_outproj, bias_out, gain_two, shift_two, w_upper, bias_upper, w_lower, bias_lower):
        normed_one = low(layer_norm(xfloat, gain_one, shift_one))
        projected = jnp.dot(normed_one, w_inproj, precision=HIGH)
        shape4 = (SEQS, LENGTH, HEADS, HEAD_DIM)
        queries = low(low_back(projected[:, :D] + bias_query)).reshape(shape4)
        keys_all = low(low_back(projected[:, D:2 * D])).reshape(shape4)
        values_all = low(low_back(projected[:, 2 * D:] + bias_value)).reshape(shape4)
        context = lax.map(jax.checkpoint(attend), (queries, keys_all, values_all, prefix_len, padding_len))
        context = low(low_back(context.reshape(TOKENS, D)))
        branch = low_back(jnp.dot(context, w_outproj, precision=HIGH) + bias_out)
        resid = xfloat + branch
        normed_two = low(layer_norm(resid, gain_two, shift_two))
        upper = low_back(jnp.dot(normed_two, w_upper, precision=HIGH) + bias_upper)
        active = low(jax.nn.gelu(upper, approximate=False))
        return resid + jnp.dot(active, w_lower, precision=HIGH) + bias_lower
    result, pullback = jax.vjp(forward, tokens.astype(jnp.float32), *params)
    grads = pullback(grad_out.astype(jnp.float32))
    return (result.astype(jnp.bfloat16), grads[0].astype(jnp.bfloat16), grads[1], grads[2], grads[3], grads[4], grads[5], grads[6], grads[7], grads[8], grads[9], grads[10], grads[11], grads[12], grads[13])
```

```python
import functools, math
import jax, jax.numpy as jnp
from jax import lax
from jax.sharding import PartitionSpec as P
from jax.experimental import pallas as pl
from jax.experimental.pallas import tpu as pltpu
HEADS=16
EPSILON = 1e-05
NEGATIVE = -1000000000.0
bf16=jnp.bfloat16; f32=jnp.float32
VMEM_LIMIT=60*1024*1024
def cp(n=1): return pltpu.CompilerParams(dimension_semantics=("arbitrary",)*n, vmem_limit_bytes=VMEM_LIMIT)
def dot(a,b): return lax.dot_general(a,b,(((1,),(0,)),((),())),preferred_element_type=f32)
def dot_nt(a,b): return lax.dot_general(a,b,(((1,),(1,)),((),())),preferred_element_type=f32)
def dot_tn(a,b): return lax.dot_general(a,b,(((0,),(0,)),((),())),preferred_element_type=f32)

def project_kernel(tokens_ref, gain_ref, shift_ref, weight_ref, bias_ref, normed_ref, out_ref, low_ref):
    step = pl.program_id(0)
    @pl.when(step == 0)
    def _():
        x = tokens_ref[...].astype(f32)
        center = x - jnp.mean(x, axis=-1, keepdims=True)
        spread = jnp.mean(center * center, axis=-1, keepdims=True)
        normed = center * lax.rsqrt(spread + EPSILON) * gain_ref[...].astype(f32) + shift_ref[...].astype(f32)
        low_ref[...] = normed.astype(bf16)
        normed_ref[...] = normed.astype(bf16)
    tn = out_ref.shape[1]
    third = pl.num_programs(0) // 3
    factor = jnp.where(step < third, 0.125, 1.0)
    out = dot(low_ref[...], weight_ref[...]) + bias_ref[...].astype(f32)
    out_ref[...] = (out * factor).astype(bf16)

def project(tokens, gain, shift, weight, bias, tn=512):
    R, D = tokens.shape
    N = weight.shape[1]
    full = pl.BlockSpec((R, D), lambda j: (0, 0))
    row = pl.BlockSpec((1, D), lambda j: (0, 0))
    return pl.pallas_call(
        project_kernel, grid=(N // tn,),
        in_specs=[full, row, row, pl.BlockSpec((D, tn), lambda j: (0, j)), pl.BlockSpec((1, tn), lambda j: (0, j))],
        out_specs=[full, pl.BlockSpec((R, tn), lambda j: (0, j))],
        out_shape=[jax.ShapeDtypeStruct((R, D), bf16), jax.ShapeDtypeStruct((R, N), bf16)],
        scratch_shapes=[pltpu.VMEM((R, D), bf16)],
        compiler_params=cp(), name="project",
        cost_estimate=pl.CostEstimate(flops=2*R*D*N, bytes_accessed=2*(D*N+R*N+2*R*D), transcendentals=0),
    )(tokens, gain, shift, weight, bias)

def mask_rows(start, bq, lo, hi, prefix, limit):
    q = start + lax.broadcasted_iota(jnp.int32, (bq, hi - lo), 0)
    k = lo + lax.broadcasted_iota(jnp.int32, (bq, hi - lo), 1)
    return ((k < prefix) | (k <= q)) & (k < limit)

def attend_kernel(prefix_ref, padding_ref, q_ref, k_ref, v_ref, out_ref, lse_ref, stat_ref, *, bq):
    L = q_ref.shape[0]
    step = pl.program_id(0)
    prefix = prefix_ref[0]
    limit = L - padding_ref[0]
    lane = lax.broadcasted_iota(jnp.int32, (1, 128), 1)
    stat_lane = lax.broadcasted_iota(jnp.int32, (bq, 128), 1)
    @pl.when(step == 0)
    def _():
        stat_ref[...] = jnp.zeros_like(stat_ref)
    for start in range(0, L, bq):
        stop = start + bq
        parts = []
        stat = stat_ref[start:stop, :]
        for half in range(2):
            mine = (lane < 64) if half == 0 else (lane >= 64)
            q = jnp.where(mine, q_ref[start:stop, :], 0).astype(bf16)
            s = dot_nt(q, k_ref[:stop, :])
            s = jnp.where(mask_rows(start, bq, 0, stop, prefix, limit), s, NEGATIVE)
            m = jnp.max(s, axis=-1, keepdims=True)
            e = jnp.exp(s - m)
            t = jnp.sum(e, axis=-1, keepdims=True)
            p = (e * (1.0 / t)).astype(bf16)
            parts.append(dot(p, v_ref[:stop, :]))
            stat = jnp.where(stat_lane == 2 * step + half, m + jnp.log(t), stat)
        stat_ref[start:stop, :] = stat
        out_ref[start:stop, :] = jnp.where(lane < 64, parts[0], parts[1]).astype(bf16)
    @pl.when(step == pl.num_programs(0) - 1)
    def _():
        lse_ref[...] = jnp.transpose(stat_ref[...])

def attend(prefix, padding, qkv, bq=256):
    L = qkv.shape[0]
    D = qkv.shape[1] // 3
    n = D // 128
    smem = pl.BlockSpec(memory_space=pltpu.SMEM)
    col = lambda off: pl.BlockSpec((L, 128), lambda j: (0, j + off))
    return pl.pallas_call(
        functools.partial(attend_kernel, bq=bq), grid=(n,),
        in_specs=[smem, smem, col(0), col(n), col(2 * n)],
        out_specs=[col(0), pl.BlockSpec((128, L), lambda j: (0, 0))],
        out_shape=[jax.ShapeDtypeStruct((L, D), bf16), jax.ShapeDtypeStruct((128, L), f32)],
        scratch_shapes=[pltpu.VMEM((L, 128), f32)],
        compiler_params=cp(), name="attend",
        cost_estimate=pl.CostEstimate(flops=4*L*L*D, bytes_accessed=8*L*D, transcendentals=L*L*n),
    )(prefix, padding, qkv, qkv, qkv)

def branch_kernel(ctx_ref, weight_ref, tokens_ref, bias_ref, gain_ref, shift_ref, resid_ref, normed_ref):
    resid = tokens_ref[...].astype(f32) + (dot(ctx_ref[...], weight_ref[...]) + bias_ref[...].astype(f32))
    center = resid - jnp.mean(resid, axis=-1, keepdims=True)
    spread = jnp.mean(center * center, axis=-1, keepdims=True)
    normed = center * lax.rsqrt(spread + EPSILON) * gain_ref[...].astype(f32) + shift_ref[...].astype(f32)
    resid_ref[...] = resid
    normed_ref[...] = normed.astype(bf16)

def branch(ctx, weight, tokens, bias, gain, shift, tm=256):
    R, D = ctx.shape
    rows = pl.BlockSpec((tm, D), lambda i: (i, 0))
    vec = pl.BlockSpec((1, D), lambda i: (0, 0))
    return pl.pallas_call(
        branch_kernel, grid=(R // tm,),
        in_specs=[rows, pl.BlockSpec((D, D), lambda i: (0, 0)), rows, vec, vec, vec],
        out_specs=[rows, rows],
        out_shape=[jax.ShapeDtypeStruct((R, D), f32), jax.ShapeDtypeStruct((R, D), bf16)],
        compiler_params=cp(), name="branch",
        cost_estimate=pl.CostEstimate(flops=2*R*D*D, bytes_accessed=2*D*D+10*R*D, transcendentals=0),
    )(ctx, weight, tokens, bias, gain, shift)

def ffn_kernel(normed_ref, grad_ref, up_ref, bias_ref, down_ref, out_ref, dn_ref, upg_ref, downg_ref, biasg_ref, *, tr):
    step = pl.program_id(0)
    R = normed_ref.shape[0]
    n2 = normed_ref[...]
    go = grad_ref[...]
    up = up_ref[...]
    down = down_ref[...]
    u = dot(n2, up) + bias_ref[...].astype(f32)
    cdf = 0.5 * (1.0 + lax.erf(u * math.sqrt(0.5)))
    a = (u * cdf).astype(bf16)
    slope = cdf + u * (jnp.exp(-0.5 * u * u) * (1.0 / math.sqrt(2 * math.pi)))
    da = dot_nt(go, down)
    du32 = da * slope
    du = du32.astype(bf16)
    @pl.when(step == 0)
    def _():
        out_ref[...] = jnp.zeros_like(out_ref)
        dn_ref[...] = jnp.zeros_like(dn_ref)
    out_ref[...] += dot(a, down)
    dn_ref[...] += dot_nt(du, up)
    upg_ref[...] = dot_tn(n2, du).astype(bf16)
    downg_ref[...] = dot_tn(a, go).astype(bf16)
    biasg_ref[...] = jnp.sum(du.astype(f32), axis=0, keepdims=True)

def ffn(normed, grad, up, bias, down, tf=512):
    R, D = normed.shape
    F = up.shape[1]
    full = pl.BlockSpec((R, D), lambda j: (0, 0))
    return pl.pallas_call(
        functools.partial(ffn_kernel, tr=R), grid=(F // tf,),
        in_specs=[full, full, pl.BlockSpec((D, tf), lambda j: (0, j)), pl.BlockSpec((1, tf), lambda j: (0, j)), pl.BlockSpec((tf, D), lambda j: (j, 0))],
        out_specs=[full, full, pl.BlockSpec((D, tf), lambda j: (0, j)), pl.BlockSpec((tf, D), lambda j: (j, 0)), pl.BlockSpec((1, tf), lambda j: (0, j))],
        out_shape=[jax.ShapeDtypeStruct((R, D), f32), jax.ShapeDtypeStruct((R, D), f32), jax.ShapeDtypeStruct((D, F), bf16), jax.ShapeDtypeStruct((F, D), bf16), jax.ShapeDtypeStruct((1, F), f32)],
        compiler_params=cp(), name="ffn",
        cost_estimate=pl.CostEstimate(flops=12*R*D*F, bytes_accessed=8*D*F+12*R*D, transcendentals=2*R*F),
    )(normed, grad, up, bias, down)

def middle_kernel(resid_ref, outacc_ref, dn_ref, go_ref, gain_ref, dbias_ref, weight_ref, ctx_ref,
                  out_ref, dres_ref, dctx_ref, wg_ref, small_ref, low_ref):
    i = pl.program_id(0)
    tm = resid_ref.shape[0]
    resid = resid_ref[...]
    out_ref[...] = (resid + outacc_ref[...] + dbias_ref[...].astype(f32)).astype(bf16)
    center = resid - jnp.mean(resid, axis=-1, keepdims=True)
    spread = jnp.mean(center * center, axis=-1, keepdims=True)
    r = lax.rsqrt(spread + EPSILON)
    nhat = center * r
    dn = dn_ref[...]
    go = go_ref[...].astype(f32)
    e = dn * gain_ref[...].astype(f32)
    d_res = go + r * (e - jnp.mean(e, axis=-1, keepdims=True) - nhat * jnp.mean(e * nhat, axis=-1, keepdims=True))
    dres_ref[...] = d_res
    low = d_res.astype(bf16)
    low_ref[pl.ds(i * tm, tm), :] = low
    dctx_ref[...] = dot_nt(low, weight_ref[...]).astype(bf16)
    @pl.when(i == 0)
    def _():
        small_ref[...] = jnp.zeros_like(small_ref)
    small_ref[0:1, :] += jnp.sum(dn * nhat, axis=0, keepdims=True)
    small_ref[1:2, :] += jnp.sum(dn, axis=0, keepdims=True)
    small_ref[2:3, :] += jnp.sum(low.astype(f32), axis=0, keepdims=True)
    small_ref[3:4, :] += jnp.sum(go, axis=0, keepdims=True)
    @pl.when(i == pl.num_programs(0) - 1)
    def _():
        wg_ref[...] = dot_tn(ctx_ref[...], low_ref[...]).astype(bf16)

def middle(resid, outacc, dn, go, gain, dbias, weight, ctx, tm=256):
    R, D = resid.shape
    rows = pl.BlockSpec((tm, D), lambda i: (i, 0))
    vec = pl.BlockSpec((1, D), lambda i: (0, 0))
    sq = pl.BlockSpec((D, D), lambda i: (0, 0))
    full = pl.BlockSpec((R, D), lambda i: (0, 0))
    return pl.pallas_call(
        middle_kernel, grid=(R // tm,),
        in_specs=[rows, rows, rows, rows, vec, vec, sq, full],
        out_specs=[rows, rows, rows, sq, pl.BlockSpec((8, D), lambda i: (0, 0))],
        out_shape=[jax.ShapeDtypeStruct((R, D), bf16), jax.ShapeDtypeStruct((R, D), f32), jax.ShapeDtypeStruct((R, D), bf16),
                   jax.ShapeDtypeStruct((D, D), bf16), jax.ShapeDtypeStruct((8, D), f32)],
        scratch_shapes=[pltpu.VMEM((R, D), bf16)],
        compiler_params=cp(), name="middle",
        cost_estimate=pl.CostEstimate(flops=4*R*D*D, bytes_accessed=4*D*D+26*R*D, transcendentals=0),
    )(resid, outacc, dn, go, gain, dbias, weight, ctx)

def attend_back_kernel(prefix_ref, padding_ref, q_ref, k_ref, v_ref, do_ref, lse_ref, dq_ref, dk_ref, dv_ref, small_ref, dka_ref, dva_ref, *, bq):
    L = q_ref.shape[0]
    step = pl.program_id(0)
    prefix = prefix_ref[0]
    limit = L - padding_ref[0]
    lane = lax.broadcasted_iota(jnp.int32, (1, 128), 1)
    dka_ref[...] = jnp.zeros_like(dka_ref)
    dva_ref[...] = jnp.zeros_like(dva_ref)
    kT = jnp.transpose(k_ref[...])
    for start in range(0, L, bq):
        stop = start + bq
        dqT = []
        for half in range(2):
            mine = (lane < 64) if half == 0 else (lane >= 64)
            q = jnp.where(mine, q_ref[start:stop, :], 0).astype(bf16)
            do = jnp.where(mine, do_ref[start:stop, :], 0).astype(bf16)
            s = dot_nt(k_ref[:stop, :], q)
            kk = lax.broadcasted_iota(jnp.int32, (stop, bq), 0)
            qq = start + lax.broadcasted_iota(jnp.int32, (stop, bq), 1)
            ok = ((kk < prefix) | (kk <= qq)) & (kk < limit)
            lse = lse_ref[pl.ds(2 * step + half, 1), start:stop]
            p = jnp.where(ok, jnp.exp(s - lse), 0.0)
            dp = dot_nt(v_ref[:stop, :], do)
            inner = jnp.sum(p * dp, axis=0, keepdims=True)
            ds = (p * (dp - inner)).astype(bf16)
            dva_ref[:stop, :] += dot(p.astype(bf16), do)
            dka_ref[:stop, :] += dot(ds, q)
            dqT.append(dot(kT[64 * half:64 * half + 64, :stop], ds))
        dq = jnp.transpose(jnp.concatenate(dqT, axis=0)) * 0.125
        dq_ref[start:stop, :] = dq.astype(bf16)
    dk_ref[...] = dka_ref[...].astype(bf16)
    dv_ref[...] = dva_ref[...].astype(bf16)
    small_ref[0:1, :] = jnp.sum(dq_ref[...].astype(f32), axis=0, keepdims=True)
    small_ref[1:2, :] = jnp.sum(dv_ref[...].astype(f32), axis=0, keepdims=True)

def attend_back(prefix, padding, qkv, dctx, lse, bq=256):
    L = qkv.shape[0]
    D = dctx.shape[1]
    n = D // 128
    smem = pl.BlockSpec(memory_space=pltpu.SMEM)
    col = lambda off: pl.BlockSpec((L, 128), lambda j: (0, j + off))
    o = jax.ShapeDtypeStruct((L, D), bf16)
    return pl.pallas_call(
        functools.partial(attend_back_kernel, bq=bq), grid=(n,),
        in_specs=[smem, smem, col(0), col(n), col(2 * n), col(0), pl.BlockSpec((128, L), lambda j: (0, 0))],
        out_specs=[col(0), col(0), col(0), pl.BlockSpec((8, 128), lambda j: (0, j))],
        out_shape=[o, o, o, jax.ShapeDtypeStruct((8, D), f32)],
        scratch_shapes=[pltpu.VMEM((L, 128), f32), pltpu.VMEM((L, 128), f32)],
        compiler_params=cp(), name="attend_back",
        cost_estimate=pl.CostEstimate(flops=10*L*L*D, bytes_accessed=14*L*D, transcendentals=L*L*n),
    )(prefix, padding, qkv, qkv, qkv, dctx, lse)

def inproj_grad_kernel(n_ref, d_ref, o_ref):
    o_ref[...] = dot_tn(n_ref[...], d_ref[...]).astype(bf16)

def inproj_grad(n1, d, tn=256):
    R, D = n1.shape
    N = d.shape[1]
    return pl.pallas_call(
        inproj_grad_kernel, grid=(N // tn,),
        in_specs=[pl.BlockSpec((R, D), lambda j: (0, 0)), pl.BlockSpec((R, tn), lambda j: (0, j))],
        out_specs=pl.BlockSpec((D, tn), lambda j: (0, j)),
        out_shape=jax.ShapeDtypeStruct((D, N), bf16),
        compiler_params=cp(), name="inproj_grad",
        cost_estimate=pl.CostEstimate(flops=2*R*D*N, bytes_accessed=2*(D*N+R*N+R*D), transcendentals=0),
    )(n1, d)

def last_kernel(dq_ref, dk_ref, dv_ref, w_ref, tokens_ref, dres_ref, gain_ref, out_ref, small_ref):
    i = pl.program_id(0)
    D = tokens_ref.shape[1]
    dn = dot_nt(dq_ref[...], w_ref[:, :D]) + dot_nt(dk_ref[...], w_ref[:, D:2*D]) + dot_nt(dv_ref[...], w_ref[:, 2*D:])
    x = tokens_ref[...].astype(f32)
    center = x - jnp.mean(x, axis=-1, keepdims=True)
    spread = jnp.mean(center * center, axis=-1, keepdims=True)
    r = lax.rsqrt(spread + EPSILON)
    nhat = center * r
    e = dn * gain_ref[...].astype(f32)
    d = dres_ref[...] + r * (e - jnp.mean(e, axis=-1, keepdims=True) - nhat * jnp.mean(e * nhat, axis=-1, keepdims=True))
    out_ref[...] = d.astype(bf16)
    @pl.when(i == 0)
    def _():
        small_ref[...] = jnp.zeros_like(small_ref)
    small_ref[0:1, :] += jnp.sum(dn * nhat, axis=0, keepdims=True)
    small_ref[1:2, :] += jnp.sum(dn, axis=0, keepdims=True)

def last(dq, dk, dv, w, tokens, dres, gain, tm=256):
    R, D = tokens.shape
    rows = pl.BlockSpec((tm, D), lambda i: (i, 0))
    return pl.pallas_call(
        last_kernel, grid=(R // tm,),
        in_specs=[rows, rows, rows, pl.BlockSpec((D, 3 * D), lambda i: (0, 0)), rows, rows, pl.BlockSpec((1, D), lambda i: (0, 0))],
        out_specs=[rows, pl.BlockSpec((8, D), lambda i: (0, 0))],
        out_shape=[jax.ShapeDtypeStruct((R, D), bf16), jax.ShapeDtypeStruct((8, D), f32)],
        compiler_params=cp(), name="last",
        cost_estimate=pl.CostEstimate(flops=6*R*D*D, bytes_accessed=6*D*D+14*R*D, transcendentals=0),
    )(dq, dk, dv, w, tokens, dres, gain)


def own_index(axes):
    return lax.axis_index(axes)

def swap_stages(sizes):
    total = math.prod(sizes)
    return [total >> (b + 1) for b in range(total.bit_length() - 1)]

def gather_small(buf, axes, total):
    me = lax.axis_index(axes)
    stride = 1
    while stride < total:
        pairs = [(i, i ^ stride) for i in range(total)]
        other = lax.ppermute(buf, axes, pairs)
        low = (me & stride) == 0
        buf = jnp.where(low, jnp.concatenate([buf, other]), jnp.concatenate([other, buf]))
        stride *= 2
    return buf

def scatter_small(buf, axes, total):
    me = lax.axis_index(axes)
    stride = total // 2
    while stride:
        pairs = [(i, i ^ stride) for i in range(total)]
        low = (me & stride) == 0
        lower, upper = buf[:stride], buf[stride:]
        other = lax.ppermute(jnp.where(low, upper, lower), axes, pairs)
        buf = jnp.where(low, lower, upper) + other
        stride //= 2
    return buf

def body(plan, tokens, prefix_len, padding_len, first_gain, first_shift, inproj_weight, query_bias, value_bias,
         outproj_weight, outproj_bias, second_gain, second_shift, up_weight, up_bias, down_weight, down_bias, grad_out):
    axes, sizes, core, yx, z = plan
    total = math.prod(sizes)
    R, D = tokens.shape
    gather = lambda w: lax.all_gather(w, axes, axis=0, tiled=True)
    small = jnp.concatenate([first_gain, first_shift, query_bias, value_bias, outproj_bias, second_gain, second_shift, down_bias, up_bias])
    n = first_gain.shape[0]
    small = gather_small(small[None], axes, total)
    vec = lambda i: small[:, i * n:(i + 1) * n].reshape(1, D)
    gain1, shift1, qbias, vbias, obias, gain2, shift2, dbias = [vec(i) for i in range(8)]
    ubias = small[:, 8 * n:].reshape(1, -1)
    w_in = gather(inproj_weight)
    w_out = gather(outproj_weight)
    w_up = gather(up_weight)
    w_down = gather(down_weight)
    bias = jnp.concatenate([qbias, jnp.zeros_like(qbias), vbias], axis=1)
    n1, qkv = project(tokens, gain1, shift1, w_in, bias)
    ctx, lse = attend(prefix_len, padding_len, qkv)
    resid, n2 = branch(ctx, w_out, tokens, obias, gain2, shift2)
    acc, dn2, up_g, down_g, ubias_g = ffn(n2, grad_out, w_up, ubias, w_down)
    out, dres, dctx, out_g, mid = middle(resid, acc, dn2, grad_out, gain2, dbias, w_out, ctx)
    dq, dk, dv, att = attend_back(prefix_len, padding_len, qkv, dctx, lse)
    in_g = jnp.concatenate([inproj_grad(n1, d) for d in (dq, dk, dv)], axis=1)
    tokens_grad, end = last(dq, dk, dv, w_in, tokens, dres, gain1)

    def scatter(g):
        rows = g.shape[0] // total
        cols = g.shape[1]
        if core:
            outer = math.prod(sizes[:sizes_index(axes, core)])
            inner = total // 2 // outer
            g = g.reshape(outer, 2, inner * rows * cols // 1024, 1024).transpose(1, 0, 2, 3)
            g = lax.psum_scatter(g, core, scatter_dimension=0, tiled=True)
            g = g.reshape(total // 2 * rows, cols)
            g = lax.psum_scatter(g, yx, scatter_dimension=0, tiled=True)
            g = lax.psum_scatter(g, z, scatter_dimension=0, tiled=True)
        else:
            g = lax.psum_scatter(g, axes, scatter_dimension=0, tiled=True)
        return g.astype(f32)
    down_grad, up_grad, out_grad, in_grad = scatter(down_g), scatter(up_g), scatter(out_g), scatter(in_g)
    rows8 = lambda *v: jnp.concatenate([a.reshape(total, -1) for a in v], axis=1)
    early = scatter_small(rows8(att[0], att[1], mid[2], mid[0], mid[1], mid[3], ubias_g[0]), axes, total)[0]
    late = scatter_small(rows8(end[0], end[1]), axes, total)[0]
    e = [early[i * n:(i + 1) * n] for i in range(6)]
    return (out, tokens_grad, late[:n], late[n:], in_grad, e[0], e[1], out_grad, e[2], e[3], e[4], up_grad, early[6 * n:], down_grad, e[5])

def sizes_index(axes, name):
    return axes.index(name)

def solution(mesh):
    shape = dict(mesh.shape)
    if shape == {"dp": 8, "fsdp": 4}:
        mesh = jax.sharding.Mesh(mesh.devices.reshape(2, 2, 2, 4), ("y", "x", "core", "fsdp"))
        plan = (("y", "x", "core", "fsdp"), (2, 2, 2, 4), "core", ("y", "x"), "fsdp")
    else:
        plan = (("dp", "fsdp"), tuple(mesh.shape[a] for a in ("dp", "fsdp")), None, None, None)
    axes = plan[0]
    rows, flat = P(axes, None), P(axes)
    ins = (rows, flat, flat, flat, flat, rows, flat, flat, rows, flat, flat, flat, rows, flat, rows, flat, rows)
    outs = (rows, rows, flat, flat, rows, flat, flat, rows, flat, flat, flat, rows, flat, rows, flat)
    return jax.shard_map(functools.partial(body, plan), mesh=mesh, in_specs=ins, out_specs=outs, check_vma=False)
```

```python
import functools, math
import jax, jax.numpy as jnp
from jax import lax
from jax.sharding import PartitionSpec as P
from jax.experimental import pallas as pl
from jax.experimental.pallas import tpu as pltpu
HEADS=16
EPSILON = 1e-05
NEGATIVE = -1000000000.0
bf16=jnp.bfloat16; f32=jnp.float32
VMEM_LIMIT=60*1024*1024
HINT=pl.CostEstimate(flops=1000, bytes_accessed=1000, transcendentals=0)
def cp(n=1): return pltpu.CompilerParams(dimension_semantics=("arbitrary",)*n, vmem_limit_bytes=VMEM_LIMIT)
def dot(a,b): return lax.dot_general(a,b,(((1,),(0,)),((),())),preferred_element_type=f32)
def dot_nt(a,b): return lax.dot_general(a,b,(((1,),(1,)),((),())),preferred_element_type=f32)
def dot_tn(a,b): return lax.dot_general(a,b,(((0,),(0,)),((),())),preferred_element_type=f32)

def project_kernel(order_ref, tokens_ref, gain_ref, shift_ref, bias_ref, *refs):
    *pieces, normed_ref, out_ref, weight_ref = refs
    step = pl.program_id(0)
    @pl.when(step == 0)
    def _():
        x = tokens_ref[...].astype(f32)
        center = x - jnp.mean(x, axis=-1, keepdims=True)
        spread = jnp.mean(center * center, axis=-1, keepdims=True)
        normed = center * lax.rsqrt(spread + EPSILON) * gain_ref[...].astype(f32) + shift_ref[...].astype(f32)
        normed_ref[...] = normed.astype(bf16)
    n, rows, tn = pieces[0].shape
    for p, piece in enumerate(pieces):
        for i in range(n):
            weight_ref[pl.ds(pl.multiple_of(order_ref[p * n + i] * rows, rows), rows), :] = piece[i]
    third = pl.num_programs(0) // 3
    factor = jnp.where(step < third, 0.125, 1.0)
    out = dot(normed_ref[...], weight_ref[...]) + bias_ref[...].astype(f32)
    out_ref[...] = (out * factor).astype(bf16)

def project(order, tokens, gain, shift, bias, pieces, tn=512):
    R, D = tokens.shape
    n, rows, N = pieces[0].shape
    full = pl.BlockSpec((R, D), lambda j: (0, 0))
    row = pl.BlockSpec((1, D), lambda j: (0, 0))
    cols = pl.BlockSpec((R, tn), lambda j: (0, j))
    return pl.pallas_call(
        project_kernel, grid=(N // tn,),
        in_specs=[pl.BlockSpec(memory_space=pltpu.SMEM), full, row, row, pl.BlockSpec((1, tn), lambda j: (0, j))]
        + [pl.BlockSpec((n, rows, tn), lambda j: (0, 0, j))] * len(pieces),
        out_specs=[full, cols, pl.BlockSpec((D, tn), lambda j: (0, j))],
        out_shape=[jax.ShapeDtypeStruct((R, D), bf16), jax.ShapeDtypeStruct((R, N), bf16), jax.ShapeDtypeStruct((D, N), bf16)],
        compiler_params=cp(), name="project",
        cost_estimate=HINT,
    )(order, tokens, gain, shift, bias, *pieces)

def mask_rows(start, bq, lo, hi, prefix, limit):
    q = start + lax.broadcasted_iota(jnp.int32, (bq, hi - lo), 0)
    k = lo + lax.broadcasted_iota(jnp.int32, (bq, hi - lo), 1)
    return ((k < prefix) | (k <= q)) & (k < limit)

def attend_kernel(prefix_ref, padding_ref, q_ref, k_ref, v_ref, out_ref, lse_ref, stat_ref, *, bq):
    L = q_ref.shape[0]
    step = pl.program_id(0)
    prefix = prefix_ref[0]
    limit = L - padding_ref[0]
    lane = lax.broadcasted_iota(jnp.int32, (1, 128), 1)
    stat_lane = lax.broadcasted_iota(jnp.int32, (bq, 128), 1)
    @pl.when(step == 0)
    def _():
        stat_ref[...] = jnp.zeros_like(stat_ref)
    for start in range(0, L, bq):
        stop = start + bq
        parts = []
        stat = stat_ref[start:stop, :]
        for half in range(2):
            mine = (lane < 64) if half == 0 else (lane >= 64)
            q = jnp.where(mine, q_ref[start:stop, :], 0).astype(bf16)
            s = dot_nt(q, k_ref[:stop, :])
            s = jnp.where(mask_rows(start, bq, 0, stop, prefix, limit), s, NEGATIVE)
            m = jnp.max(s, axis=-1, keepdims=True)
            e = jnp.exp(s - m)
            t = jnp.sum(e, axis=-1, keepdims=True)
            p = (e * (1.0 / t)).astype(bf16)
            parts.append(dot(p, v_ref[:stop, :]))
            stat = jnp.where(stat_lane == 2 * step + half, m + jnp.log(t), stat)
        stat_ref[start:stop, :] = stat
        out_ref[start:stop, :] = jnp.where(lane < 64, parts[0], parts[1]).astype(bf16)
    @pl.when(step == pl.num_programs(0) - 1)
    def _():
        lse_ref[...] = jnp.transpose(stat_ref[...])

def attend(prefix, padding, qkv, bq=256):
    L = qkv.shape[0]
    D = qkv.shape[1] // 3
    n = D // 128
    smem = pl.BlockSpec(memory_space=pltpu.SMEM)
    col = lambda off: pl.BlockSpec((L, 128), lambda j: (0, j + off))
    return pl.pallas_call(
        functools.partial(attend_kernel, bq=bq), grid=(n,),
        in_specs=[smem, smem, col(0), col(n), col(2 * n)],
        out_specs=[col(0), pl.BlockSpec((128, L), lambda j: (0, 0))],
        out_shape=[jax.ShapeDtypeStruct((L, D), bf16), jax.ShapeDtypeStruct((128, L), f32)],
        scratch_shapes=[pltpu.VMEM((L, 128), f32)],
        compiler_params=cp(), name="attend",
        cost_estimate=HINT,
    )(prefix, padding, qkv, qkv, qkv)

def branch_kernel(ctx_ref, weight_ref, tokens_ref, bias_ref, gain_ref, shift_ref, resid_ref, normed_ref):
    resid = tokens_ref[...].astype(f32) + (dot(ctx_ref[...], weight_ref[...]) + bias_ref[...].astype(f32))
    center = resid - jnp.mean(resid, axis=-1, keepdims=True)
    spread = jnp.mean(center * center, axis=-1, keepdims=True)
    normed = center * lax.rsqrt(spread + EPSILON) * gain_ref[...].astype(f32) + shift_ref[...].astype(f32)
    resid_ref[...] = resid
    normed_ref[...] = normed.astype(bf16)

def branch(ctx, weight, tokens, bias, gain, shift, tm=256):
    R, D = ctx.shape
    rows = pl.BlockSpec((tm, D), lambda i: (i, 0))
    vec = pl.BlockSpec((1, D), lambda i: (0, 0))
    return pl.pallas_call(
        branch_kernel, grid=(R // tm,),
        in_specs=[rows, pl.BlockSpec((D, D), lambda i: (0, 0)), rows, vec, vec, vec],
        out_specs=[rows, rows],
        out_shape=[jax.ShapeDtypeStruct((R, D), f32), jax.ShapeDtypeStruct((R, D), bf16)],
        compiler_params=cp(), name="branch",
        cost_estimate=HINT,
    )(ctx, weight, tokens, bias, gain, shift)

def ffn_kernel(pos_ref, normed_ref, grad_ref, up_ref, bias_ref, down_ref, *refs, shards, per, F, chained):
    out_in, dn_in = refs[:2] if chained else (None, None)
    out_ref, dn_ref, keep_ref, send_ref, biasg_ref, ups_ref, dns_ref, up_sem, dn_sem, acc_sem = refs[2 if chained else 0:]
    step = pl.program_id(0)
    last = pl.num_programs(0) - 1
    D = normed_ref.shape[1]
    tf = up_ref.shape[1]
    half = shards // 2
    rows = D // shards
    slot = lax.rem(step, 2)
    block = lax.div(step, per)
    bslot = lax.rem(block, 2)

    def up_copies(slot, step):
        cols = pl.ds(pl.multiple_of(step * tf, tf), tf)
        return [pltpu.make_async_copy(ups_ref.at[slot, pl.ds(0, half)], keep_ref.at[:, :, cols], up_sem.at[slot, 0]),
                pltpu.make_async_copy(ups_ref.at[slot, pl.ds(half, half)], send_ref.at[:, :, cols], up_sem.at[slot, 1])]

    def down_copies(bslot, block):
        cols = pl.ds(pl.multiple_of(F + block * D, D), D)
        return [pltpu.make_async_copy(dns_ref.at[bslot, pl.ds(0, half)], keep_ref.at[:, :, cols], dn_sem.at[bslot, 0]),
                pltpu.make_async_copy(dns_ref.at[bslot, pl.ds(half, half)], send_ref.at[:, :, cols], dn_sem.at[bslot, 1])]

    earlier = [pltpu.make_async_copy(out_in, out_ref, acc_sem.at[0]), pltpu.make_async_copy(dn_in, dn_ref, acc_sem.at[1])] if chained else []

    @pl.when(step == 0)
    def _():
        if chained:
            for c in earlier:
                c.start()
        else:
            out_ref[...] = jnp.zeros_like(out_ref)
            dn_ref[...] = jnp.zeros_like(dn_ref)
    n2 = normed_ref[...]
    go = grad_ref[...]
    up = up_ref[...]
    down = down_ref[...]
    u = dot(n2, up) + bias_ref[...].astype(f32)
    cdf = 0.5 * (1.0 + lax.erf(u * math.sqrt(0.5)))
    a = (u * cdf).astype(bf16)
    slope = cdf + u * (jnp.exp(-0.5 * u * u) * (1.0 / math.sqrt(2 * math.pi)))
    du = (dot_nt(go, down) * slope).astype(bf16)
    if chained:
        @pl.when(step == 0)
        def _():
            for c in earlier:
                c.wait()
    out_ref[...] += dot(a, down)
    dn_ref[...] += dot_nt(du, up)
    biasg_ref[...] = jnp.sum(du.astype(f32), axis=0, keepdims=True)
    upg = dot_tn(n2, du).astype(bf16)
    downg = dot_tn(a, go).astype(bf16)

    @pl.when(step >= 2)
    def _():
        for c in up_copies(slot, step - 2):
            c.wait()
    for i in range(shards):
        ups_ref[slot, pos_ref[i]] = upg[i * rows:(i + 1) * rows]
    for c in up_copies(slot, step):
        c.start()

    @pl.when((step >= 2 * per) & (lax.rem(step, per) == 0))
    def _():
        for c in down_copies(bslot, block - 2):
            c.wait()
    here = tf // rows
    first = lax.rem(step, per) * here
    for i in range(here):
        dns_ref[bslot, pos_ref[first + i]] = downg[i * rows:(i + 1) * rows]

    @pl.when(lax.rem(step, per) == per - 1)
    def _():
        for c in down_copies(bslot, block):
            c.start()

    @pl.when(step == last)
    def _():
        for c in up_copies(1 - slot, step - 1) + up_copies(slot, step) + down_copies(1 - bslot, block - 1) + down_copies(bslot, block):
            c.wait()

def ffn(pos, normed, grad, wide, bias, first, blocks, extra=0, earlier=(), tf=512):
    R, D = normed.shape
    F = blocks * D
    shards = pos.shape[0]
    rows = D // shards
    per = D // tf
    every = (wide.shape[1] // D - 1) // 2
    full = pl.BlockSpec((R, D), lambda j: (0, 0))
    hbm = pl.BlockSpec(memory_space=pl.ANY)
    part = jax.ShapeDtypeStruct((shards // 2, rows, 2 * F + extra), bf16)
    return pl.pallas_call(
        functools.partial(ffn_kernel, shards=shards, per=per, F=F, chained=bool(earlier)), grid=(F // tf,),
        in_specs=[pl.BlockSpec(memory_space=pltpu.SMEM), full, full,
                  pl.BlockSpec((D, tf), lambda j: (0, j + (1 + first) * per)), pl.BlockSpec((1, tf), lambda j: (0, j + first * per)),
                  pl.BlockSpec((tf, D), lambda j: (lax.rem(j, per), 1 + every + first + lax.div(j, per)))] + [hbm] * len(earlier),
        out_specs=[full, full, hbm, hbm, pl.BlockSpec((1, tf), lambda j: (0, j))],
        out_shape=[jax.ShapeDtypeStruct((R, D), f32), jax.ShapeDtypeStruct((R, D), f32), part, part, jax.ShapeDtypeStruct((1, F), f32)],
        scratch_shapes=[pltpu.VMEM((2, shards, rows, tf), bf16), pltpu.VMEM((2, shards, rows, D), bf16),
                        pltpu.SemaphoreType.DMA((2, 2)), pltpu.SemaphoreType.DMA((2, 2)), pltpu.SemaphoreType.DMA((2,))],
        compiler_params=cp(), name="ffn",
        cost_estimate=HINT,
    )(pos, normed, grad, wide, bias, wide, *earlier)

def middle_kernel(resid_ref, outacc_ref, dn_ref, go_ref, gain_ref, dbias_ref, weight_ref,
                  out_ref, dres_ref, low_ref, dctx_ref, small_ref):
    i = pl.program_id(0)
    resid = resid_ref[...]
    out_ref[...] = (resid + outacc_ref[...] + dbias_ref[...].astype(f32)).astype(bf16)
    center = resid - jnp.mean(resid, axis=-1, keepdims=True)
    spread = jnp.mean(center * center, axis=-1, keepdims=True)
    r = lax.rsqrt(spread + EPSILON)
    nhat = center * r
    dn = dn_ref[...]
    go = go_ref[...].astype(f32)
    e = dn * gain_ref[...].astype(f32)
    d_res = go + r * (e - jnp.mean(e, axis=-1, keepdims=True) - nhat * jnp.mean(e * nhat, axis=-1, keepdims=True))
    dres_ref[...] = d_res
    low = d_res.astype(bf16)
    low_ref[...] = low
    dctx_ref[...] = dot_nt(low, weight_ref[...]).astype(bf16)
    @pl.when(i == 0)
    def _():
        small_ref[...] = jnp.zeros_like(small_ref)
    small_ref[0:1, :] += jnp.sum(dn * nhat, axis=0, keepdims=True)
    small_ref[1:2, :] += jnp.sum(dn, axis=0, keepdims=True)
    small_ref[2:3, :] += jnp.sum(low.astype(f32), axis=0, keepdims=True)
    small_ref[3:4, :] += jnp.sum(go, axis=0, keepdims=True)

def middle(resid, outacc, dn, go, gain, dbias, weight, tm=256):
    R, D = resid.shape
    rows = pl.BlockSpec((tm, D), lambda i: (i, 0))
    vec = pl.BlockSpec((1, D), lambda i: (0, 0))
    low = jax.ShapeDtypeStruct((R, D), bf16)
    return pl.pallas_call(
        middle_kernel, grid=(R // tm,),
        in_specs=[rows, rows, rows, rows, vec, vec, pl.BlockSpec((D, D), lambda i: (0, 0))],
        out_specs=[rows, rows, rows, rows, pl.BlockSpec((8, D), lambda i: (0, 0))],
        out_shape=[low, jax.ShapeDtypeStruct((R, D), f32), low, low, jax.ShapeDtypeStruct((8, D), f32)],
        compiler_params=cp(), name="middle",
        cost_estimate=HINT,
    )(resid, outacc, dn, go, gain, dbias, weight)

def attend_back_kernel(prefix_ref, padding_ref, q_ref, k_ref, v_ref, do_ref, lse_ref, *refs, bq, first):
    dq_ref, dk_ref, dv_ref, small_ref, dka_ref, dva_ref = refs[-6:]
    L = q_ref.shape[0]
    step = pl.program_id(0) + first
    prefix = prefix_ref[0]
    limit = L - padding_ref[0]
    lane = lax.broadcasted_iota(jnp.int32, (1, 128), 1)
    dka_ref[...] = jnp.zeros_like(dka_ref)
    dva_ref[...] = jnp.zeros_like(dva_ref)
    kT = jnp.transpose(k_ref[...])
    for start in range(0, L, bq):
        stop = start + bq
        dqT = []
        for half in range(2):
            mine = (lane < 64) if half == 0 else (lane >= 64)
            q = jnp.where(mine, q_ref[start:stop, :], 0).astype(bf16)
            do = jnp.where(mine, do_ref[start:stop, :], 0).astype(bf16)
            s = dot_nt(k_ref[:stop, :], q)
            kk = lax.broadcasted_iota(jnp.int32, (stop, bq), 0)
            qq = start + lax.broadcasted_iota(jnp.int32, (stop, bq), 1)
            ok = ((kk < prefix) | (kk <= qq)) & (kk < limit)
            lse = lse_ref[pl.ds(2 * step + half, 1), start:stop]
            p = jnp.where(ok, jnp.exp(s - lse), 0.0)
            dp = dot_nt(v_ref[:stop, :], do)
            inner = jnp.sum(p * dp, axis=0, keepdims=True)
            ds = (p * (dp - inner)).astype(bf16)
            dva_ref[:stop, :] += dot(p.astype(bf16), do)
            dka_ref[:stop, :] += dot(ds, q)
            dqT.append(dot(kT[64 * half:64 * half + 64, :stop], ds))
        dq = jnp.transpose(jnp.concatenate(dqT, axis=0)) * 0.125
        dq_ref[start:stop, :] = dq.astype(bf16)
    dk_ref[...] = dka_ref[...].astype(bf16)
    dv_ref[...] = dva_ref[...].astype(bf16)
    small_ref[0:1, :] = jnp.sum(dq_ref[...].astype(f32), axis=0, keepdims=True)
    small_ref[1:2, :] = jnp.sum(dv_ref[...].astype(f32), axis=0, keepdims=True)

def attend_back(prefix, padding, qkv, dctx, lse, first, count, width, earlier=(), bq=256):
    L = qkv.shape[0]
    D = dctx.shape[1]
    n = D // 128
    at = first % (width // 128)
    smem = pl.BlockSpec(memory_space=pltpu.SMEM)
    col = lambda off: pl.BlockSpec((L, 128), lambda j: (0, j + off))
    o = jax.ShapeDtypeStruct((L, width), bf16)
    return pl.pallas_call(
        functools.partial(attend_back_kernel, bq=bq, first=first), grid=(count,),
        in_specs=[smem, smem, col(first), col(n + first), col(2 * n + first), col(first), pl.BlockSpec((128, L), lambda j: (0, 0))]
        + [pl.BlockSpec(memory_space=pl.ANY)] * len(earlier),
        out_specs=[col(at), col(at), col(at), pl.BlockSpec((8, 128), lambda j: (0, j + at))],
        out_shape=[o, o, o, jax.ShapeDtypeStruct((8, width), f32)],
        scratch_shapes=[pltpu.VMEM((L, 128), f32), pltpu.VMEM((L, 128), f32)],
        input_output_aliases={7 + i: i for i in range(len(earlier))},
        compiler_params=cp(), name="attend_back",
        cost_estimate=HINT,
    )(prefix, padding, qkv, qkv, qkv, dctx, lse, *earlier)

def weight_grad_kernel(pos_ref, *refs, sources, extra):
    left = refs[:max(sources) + 1]
    refs = refs[len(left):]
    right = refs[:len(sources)]
    refs = refs[len(right):]
    small_ref = refs[0] if extra else None
    keep_ref, send_ref, wide_ref = refs[1 if extra else 0:]
    shards = wide_ref.shape[0]
    half = shards // 2
    rows = left[0].shape[1] // shards
    for g, (source, d_ref) in enumerate(zip(sources, right)):
        value = dot_tn(left[source][...], d_ref[...]).astype(bf16)
        for i in range(shards):
            wide_ref[pos_ref[i], g * rows:(g + 1) * rows, :] = value[i * rows:(i + 1) * rows]
    if extra:
        for i in range(shards):
            wide_ref[pos_ref[i], len(sources) * rows:, :] = jnp.broadcast_to(small_ref[i:i + 1, :], (extra, small_ref.shape[1])).astype(bf16)
    keep_ref[...] = wide_ref[:half]
    send_ref[...] = wide_ref[half:]

def weight_grad(pos, left, right, sources, small=None, width=512, tn=256):
    R, D = left[0].shape
    shards = pos.shape[0]
    rows = D // shards
    extra = min(rows, 16) if small is not None else 0
    high = len(right) * rows + extra
    part = pl.BlockSpec((shards // 2, high, tn), lambda j: (0, 0, j))
    half = jax.ShapeDtypeStruct((shards // 2, high, width), bf16)
    more = [small] if extra else []
    cols = lambda first: pl.BlockSpec((R, tn), lambda j: (0, j + first))
    return pl.pallas_call(
        functools.partial(weight_grad_kernel, sources=sources, extra=extra), grid=(width // tn,),
        in_specs=[pl.BlockSpec(memory_space=pltpu.SMEM)] + [pl.BlockSpec((R, D), lambda j: (0, 0))] * len(left)
        + [cols(first) for _, first in right] + [pl.BlockSpec((shards, tn), lambda j: (0, j))] * len(more),
        out_specs=[part, part], out_shape=[half, half],
        scratch_shapes=[pltpu.VMEM((shards, high, tn), bf16)],
        compiler_params=cp(), name="weight_grad",
        cost_estimate=HINT,
    )(pos, *left, *[r for r, _ in right], *more)

def last_kernel(w_ref, tokens_ref, dres_ref, gain_ref, *refs, count):
    parts = refs[:count]
    out_ref, small_ref = refs[-2:]
    i = pl.program_id(0)
    D = tokens_ref.shape[1]
    count = len(parts) // 3
    dn = None
    for p, part in enumerate(parts):
        width = part.shape[1]
        at = (p // count) * D + (p % count) * width
        term = dot_nt(part[...], w_ref[:, at:at + width])
        dn = term if dn is None else dn + term
    x = tokens_ref[...].astype(f32)
    center = x - jnp.mean(x, axis=-1, keepdims=True)
    spread = jnp.mean(center * center, axis=-1, keepdims=True)
    r = lax.rsqrt(spread + EPSILON)
    nhat = center * r
    e = dn * gain_ref[...].astype(f32)
    d = dres_ref[...] + r * (e - jnp.mean(e, axis=-1, keepdims=True) - nhat * jnp.mean(e * nhat, axis=-1, keepdims=True))
    out_ref[...] = d.astype(bf16)
    @pl.when(i == 0)
    def _():
        small_ref[...] = jnp.zeros_like(small_ref)
    small_ref[0:1, :] += jnp.sum(dn * nhat, axis=0, keepdims=True)
    small_ref[1:2, :] += jnp.sum(dn, axis=0, keepdims=True)

def last(parts, w, tokens, dres, gain, first, steps, earlier=(), tm=256):
    R, D = tokens.shape
    rows = lambda width: pl.BlockSpec((tm, width), lambda i: (i + first, 0))
    return pl.pallas_call(
        functools.partial(last_kernel, count=len(parts)), grid=(steps,),
        in_specs=[pl.BlockSpec((D, 3 * D), lambda i: (0, 0)), rows(D), rows(D), pl.BlockSpec((1, D), lambda i: (0, 0))]
        + [rows(p.shape[1]) for p in parts] + [pl.BlockSpec(memory_space=pl.ANY)] * len(earlier),
        out_specs=[rows(D), pl.BlockSpec((8, D), lambda i: (0, 0))],
        out_shape=[jax.ShapeDtypeStruct((R, D), bf16), jax.ShapeDtypeStruct((8, D), f32)],
        input_output_aliases={4 + len(parts): 0} if earlier else {},
        compiler_params=cp(), name="last",
        cost_estimate=HINT,
    )(w, tokens, dres, gain, *parts, *earlier)


class Plan:
    def __init__(self, dp, fsdp):
        self.total = dp * fsdp
        bits = self.total.bit_length() - 1
        low = fsdp.bit_length() - 1
        if fsdp == 4:
            self.core, z, rest = low, list(range(low)), list(range(low + 1, bits))
        else:
            self.core, z, rest = 0, list(range(1, low)), list(range(low, bits))
        a, b = rest[:len(rest) // 2], rest[len(rest) // 2:]
        self.stages = [(a, b), (b, a), (z, z)]
        self.third = len(z) == low

    def masks(self, stage, core):
        bits = self.stages[stage][core]
        return [sum(1 << b for k, b in enumerate(bits) if j >> k & 1) for j in range(1 << len(bits))]

    def pairs(self, stage, j):
        return [(i, i ^ self.masks(stage, i >> self.core & 1)[j]) for i in range(self.total)]

    def size(self, stage):
        return 1 << len(self.stages[stage][0])

    def places(self, me, fixed=False):
        shard = lax.iota(jnp.int32, self.total)
        rel = shard ^ me
        core = (shard >> self.core) & 1
        pos = (rel >> self.core) & 1
        for k, (a, b) in enumerate(self.stages):
            pick = lambda bits, v: sum((((v >> bit) & 1) << k) for k, bit in enumerate(bits))
            own = pick(a, shard) if fixed and k == 2 else jnp.where(core == 0, pick(a, rel), pick(b, rel))
            pos = (pos << len(a)) + own
        return pos

AXES = ("dp", "fsdp")

def swap_core(plan, x):
    return lax.ppermute(x, AXES, [(i, i ^ (1 << plan.core)) for i in range(plan.total)])

def exchange(plan, x, stage, j):
    return lax.ppermute(x, AXES, plan.pairs(stage, j))

def gather_pieces(plan, shard, beside):
    arrived = tie(beside, *[exchange(plan, shard, 2, j) for j in range(1, plan.size(2))])[1:]
    column = jnp.stack([shard] + arrived)
    pieces = [column] + [exchange(plan, column, 1, j) for j in range(1, plan.size(1))]
    pieces = pieces + [exchange(plan, p, 0, j) for j in range(1, plan.size(0)) for p in pieces]
    return pieces + [swap_core(plan, p) for p in pieces]

def step(x, after, *reductions):
    x, _ = tie(x, after, *reductions)
    reductions = [r for r in reductions if r.stage < 3]
    if reductions:
        for r in reductions:
            r.add()
        x, = tie(x, *reductions)
        for r in reductions:
            r.go()
    return x

class Reduction:
    def __init__(self, plan, keep, send):
        self.plan, self.stage, self.size = plan, 0, keep.shape[0]
        self.terms = [keep, swap_core(plan, send)]
        self.sent = []

    def cut(self, j):
        part = self.size // self.plan.size(self.stage)
        return sum(t[j * part:(j + 1) * part].astype(f32) for t in self.terms).astype(bf16)

    def add(self):
        self.sent = [self.cut(j) for j in range(1, self.plan.size(self.stage))]

    def go(self):
        self.terms = self.terms + [exchange(self.plan, s, self.stage, j + 1) for j, s in enumerate(self.sent)]
        self.sent = []
        self.size //= self.plan.size(self.stage)
        self.stage += 1

    def finish(self):
        while self.stage < 3:
            self.add()
            self.go()
        return sum(t[0].astype(f32) for t in self.terms)

    def scatter(self):
        if not self.plan.third:
            return self.finish()
        whole = sum(t[:self.size].astype(f32) for t in self.terms).astype(bf16)
        return lax.psum_scatter(whole, "fsdp", scatter_dimension=0, tiled=False).astype(f32)

def tie(*trees):
    flat = []
    for t in trees:
        flat += t.terms + t.sent if isinstance(t, Reduction) else [t]
    flat = list(lax.optimization_barrier(tuple(flat)))
    out = []
    for t in trees:
        if isinstance(t, Reduction):
            t.terms = [flat.pop(0) for _ in t.terms]
            t.sent = [flat.pop(0) for _ in t.sent]
        else:
            out.append(flat.pop(0))
    return out

def gather_small(plan, buf):
    me = lax.axis_index(AXES)
    stride = 1
    while stride < plan.total:
        other = lax.ppermute(buf, AXES, [(i, i ^ stride) for i in range(plan.total)])
        low = (me & stride) == 0
        buf = jnp.where(low, jnp.concatenate([buf, other]), jnp.concatenate([other, buf]))
        stride *= 2
    return buf

def scatter_small(plan, buf):
    me = lax.axis_index(AXES)
    stride = plan.total // 2
    while stride:
        low = (me & stride) == 0
        lower, upper = buf[:stride], buf[stride:]
        other = lax.ppermute(jnp.where(low, upper, lower), AXES, [(i, i ^ stride) for i in range(plan.total)])
        buf = jnp.where(low, lower, upper) + other
        stride //= 2
    return buf[0]

def body(plan, tokens, prefix_len, padding_len, first_gain, first_shift, inproj_weight, query_bias, value_bias,
         outproj_weight, outproj_bias, second_gain, second_shift, up_weight, up_bias, down_weight, down_bias, grad_out):
    total = plan.total
    R, D = tokens.shape
    F = up_weight.shape[1]
    rows = D // total
    blocks = F // D
    me = lax.axis_index(AXES)
    pos = plan.places(me)
    shard = lax.iota(jnp.int32, total)
    order = jnp.sum(jnp.where(pos[None, :] == shard[:, None], shard[None, :], 0), axis=1)
    small = jnp.concatenate([first_gain, first_shift, query_bias, value_bias, outproj_bias, second_gain, second_shift, down_bias, up_bias])
    n = first_gain.shape[0]
    small = gather_small(plan, small[None])
    vec = lambda i: small[:, i * n:(i + 1) * n].reshape(1, D)
    gain1, shift1, qbias, vbias, obias, gain2, shift2, dbias = [vec(i) for i in range(8)]
    ubias = small[:, 8 * n:].reshape(total, blocks, rows).transpose(1, 0, 2).reshape(1, F)
    pieces = gather_pieces(plan, inproj_weight, small)
    up_local = up_weight.reshape(rows, total, blocks, rows).transpose(0, 2, 1, 3).reshape(rows, F)
    down_local = [down_weight[b * rows:(b + 1) * rows] for b in range(blocks)]
    wide = lax.all_gather(jnp.concatenate([outproj_weight, up_local] + down_local, axis=1), AXES, axis=0, tiled=True)
    bias = jnp.concatenate([qbias, jnp.zeros_like(qbias), vbias], axis=1)
    n1, qkv, w_in = project(order, tokens, gain1, shift1, bias, pieces)
    ctx, lse = attend(prefix_len, padding_len, qkv)
    resid, n2 = branch(ctx, wide, tokens, obias, gain2, shift2)
    half = blocks // 2
    cut = D // 2
    n_pairs = D // 128
    def back(first, x, earlier=()):
        return attend_back(prefix_len, padding_len, qkv, x, lse, first, n_pairs // 4, cut, earlier)
    acc, dn2, keep, send, ub1 = ffn(pos, n2, grad_out, wide, ubias, 0, half)
    g1 = Reduction(plan, keep, send)
    acc, dn2, keep, send, ub2 = ffn(pos, n2, grad_out, wide, ubias, half, half, 0, (acc, dn2))
    g2 = Reduction(plan, keep, send)
    acc = step(acc, dn2, g1)
    out, dres, low, dctx, mid = middle(resid, acc, dn2, grad_out, gain2, dbias, wide)
    dctx = step(dctx, dres, g2)
    d1 = back(0, dctx)
    dctx = step(dctx, d1[0], g1)
    d1 = back(n_pairs // 4, dctx, d1)
    n1a, _ = tie(n1, d1[0])
    g3 = Reduction(plan, *weight_grad(pos, (n1a, ctx), ((d1[0], 0), (d1[1], 0), (d1[2], 0), (low, 0), (low, cut // 256)), (0, 0, 0, 1, 1), width=cut))
    dctx, _ = tie(dctx, g3.terms[0])
    dctx = step(dctx, dctx, g1, g2)
    d2 = back(n_pairs // 2, dctx)
    dctx = step(dctx, d2[0], g3)
    d2 = back(n_pairs * 3 // 4, dctx, d2)
    n1b = step(n1, d2[0], g2, g1)
    per = lambda v: v.reshape(total, -1)
    att = jnp.concatenate([d1[3], d2[3]], axis=1)
    ubg = jnp.concatenate([ub1, ub2], axis=1).reshape(blocks, total, rows).transpose(1, 0, 2).reshape(total, -1)
    early = jnp.concatenate([per(att[0]), per(att[1]), per(mid[2]), per(mid[0]), per(mid[1]), per(mid[3]), ubg], axis=1)
    early = jnp.pad(early, ((0, 0), (0, cut - early.shape[1])))
    g4 = Reduction(plan, *weight_grad(pos, (n1b,), ((d2[0], 0), (d2[1], 0), (d2[2], 0)), (0, 0, 0), early, width=cut))
    dres, _ = tie(dres, g4.terms[0])
    dres = step(dres, dres, g3)
    parts = [d1[0], d2[0], d1[1], d2[1], d1[2], d2[2]]
    tokens_grad, end1 = last(parts, w_in, tokens, dres, gain1, 0, R // 512)
    dres = step(dres, end1, g4)
    tokens_grad, end2 = last(parts, w_in, tokens, dres, gain1, R // 512, R // 512, (tokens_grad,))
    end = step(end1 + end2, end2, g3, g4, g2)
    end = step(end, end, g4)
    in2, in1, ffn2, ffn1 = g4.finish(), g3.finish(), g2.finish(), g1.finish()
    late = scatter_small(plan, jnp.concatenate([per(end[0]), per(end[1])], axis=1))
    up_grad = jnp.concatenate([ffn1[:, :F // 2], ffn2[:, :F // 2]], axis=1).reshape(rows, blocks, total, rows).transpose(0, 2, 1, 3).reshape(rows, F)
    down_grad = jnp.concatenate([g[:, F // 2 + b * D:F // 2 + (b + 1) * D] for g in (ffn1, ffn2) for b in range(half)], axis=0)
    out_grad = jnp.concatenate([in1[3 * rows:4 * rows], in1[4 * rows:]], axis=1)
    in_grad = jnp.concatenate([g[k * rows:(k + 1) * rows] for k in range(3) for g in (in1, in2)], axis=1)
    early = in2[3 * rows]
    e = [early[i * n:(i + 1) * n] for i in range(6)]
    return (out, tokens_grad, late[:n], late[n:], in_grad, e[0], e[1], out_grad, e[2], e[3], e[4], up_grad, early[6 * n:6 * n + F // total], down_grad, e[5])

def solution(mesh):
    plan = Plan(mesh.shape["dp"], mesh.shape["fsdp"])
    rows, flat = P(AXES, None), P(AXES)
    ins = (rows, flat, flat, flat, flat, rows, flat, flat, rows, flat, flat, flat, rows, flat, rows, flat, rows)
    outs = (rows, rows, flat, flat, rows, flat, flat, rows, flat, flat, flat, rows, flat, rows, flat)
    return jax.shard_map(functools.partial(body, plan), mesh=mesh, in_specs=ins, out_specs=outs, check_vma=False)
```

```python
import functools, math
import jax, jax.numpy as jnp
from jax import lax
from jax.sharding import PartitionSpec as P
from jax.experimental import pallas as pl
from jax.experimental.pallas import tpu as pltpu
HEADS=16
EPSILON = 1e-05
NEGATIVE = -1000000000.0
bf16=jnp.bfloat16; f32=jnp.float32
VMEM_LIMIT=60*1024*1024
HINT=pl.CostEstimate(flops=1000, bytes_accessed=1000, transcendentals=0)
def cp(n=1): return pltpu.CompilerParams(dimension_semantics=("arbitrary",)*n, vmem_limit_bytes=VMEM_LIMIT)
def dot(a,b): return lax.dot_general(a,b,(((1,),(0,)),((),())),preferred_element_type=f32)
def dot_nt(a,b): return lax.dot_general(a,b,(((1,),(1,)),((),())),preferred_element_type=f32)
def dot_tn(a,b): return lax.dot_general(a,b,(((0,),(0,)),((),())),preferred_element_type=f32)

GAIN1, SHIFT1, QBIAS, VBIAS, OBIAS, GAIN2, SHIFT2, DBIAS, UBIAS = range(9)

def row_of(ref, k):
    return ref[k:k + 1, :]

def norm_kernel(tokens_ref, out_ref):
    x = tokens_ref[...].astype(f32)
    center = x - jnp.mean(x, axis=-1, keepdims=True)
    spread = jnp.mean(center * center, axis=-1, keepdims=True)
    out_ref[...] = center * lax.rsqrt(spread + EPSILON)

def norm(tokens, tm=256):
    R, D = tokens.shape
    rows = pl.BlockSpec((tm, D), lambda i: (i, 0))
    return pl.pallas_call(
        norm_kernel, grid=(R // tm,), in_specs=[rows], out_specs=rows, out_shape=jax.ShapeDtypeStruct((R, D), f32),
        compiler_params=cp(), name="norm", cost_estimate=HINT,
    )(tokens)

def in_order(order_ref, pieces, whole_ref):
    n, rows, _ = pieces[0].shape
    for p, piece in enumerate(pieces):
        for i in range(n):
            whole_ref[pl.ds(pl.multiple_of(order_ref[p * n + i] * rows, rows), rows), :] = piece[i]

def project_kernel(order_ref, xhat_ref, *refs, count):
    pieces, sides = refs[:count], refs[count:2 * count]
    normed_ref, out_ref, weight_ref, vec_ref, side_ref, all_ref = refs[2 * count:]
    step = pl.program_id(0)
    @pl.when(step == 0)
    def _():
        in_order(order_ref, sides, side_ref)
        all_ref[...] = jnp.transpose(side_ref[...].astype(f32))
        vec_ref[...] = all_ref[:16, :]
        normed_ref[...] = (xhat_ref[...] * all_ref[GAIN1:GAIN1 + 1, :] + all_ref[SHIFT1:SHIFT1 + 1, :]).astype(bf16)
    in_order(order_ref, pieces, weight_ref)
    D = normed_ref.shape[1]
    tn = out_ref.shape[1]
    third = pl.num_programs(0) // 3
    at = pl.ds(pl.multiple_of(lax.rem(step, D // tn) * tn, tn), tn)
    bias = jnp.where(step < third, all_ref[QBIAS:QBIAS + 1, at], jnp.where(step < 2 * third, 0.0, all_ref[VBIAS:VBIAS + 1, at]))
    factor = jnp.where(step < third, 0.125, 1.0)
    out = dot(normed_ref[...], weight_ref[...]) + bias
    out_ref[...] = (out * factor).astype(bf16)

def project(order, xhat, pieces, tn=512):
    R, D = xhat.shape
    n, rows, width = pieces[0].shape
    N = 3 * D
    cols = pl.BlockSpec((R, tn), lambda j: (0, j))
    full = pl.BlockSpec((R, D), lambda j: (0, 0))
    return pl.pallas_call(
        functools.partial(project_kernel, count=len(pieces)), grid=(N // tn,),
        in_specs=[pl.BlockSpec(memory_space=pltpu.SMEM), full]
        + [pl.BlockSpec((n, rows, tn), lambda j: (0, 0, j))] * len(pieces)
        + [pl.BlockSpec((n, rows, 128), lambda j: (0, 0, width // 128 - 1))] * len(pieces),
        out_specs=[full, cols, pl.BlockSpec((D, tn), lambda j: (0, j)), pl.BlockSpec((16, D), lambda j: (0, 0))],
        out_shape=[jax.ShapeDtypeStruct((R, D), bf16), jax.ShapeDtypeStruct((R, N), bf16), jax.ShapeDtypeStruct((D, N), bf16),
                   jax.ShapeDtypeStruct((16, D), f32)],
        scratch_shapes=[pltpu.VMEM((D, 128), bf16), pltpu.VMEM((128, D), f32)],
        compiler_params=cp(), name="project", cost_estimate=HINT,
    )(order, xhat, *pieces, *pieces)

def key_bias(prefix, limit, lo, q0, bq, transposed, diagonal):
    shape = (bq, bq)
    kd = 0 if transposed else 1
    k = lo + lax.broadcasted_iota(jnp.int32, shape, kd)
    ok = k < limit
    if diagonal:
        q = q0 + lax.broadcasted_iota(jnp.int32, shape, 1 - kd)
        ok = ok & ((k < prefix) | (k <= q))
    return jnp.where(ok, 0.0, NEGATIVE)

def attend_kernel(prefix_ref, padding_ref, q_ref, k_ref, v_ref, out_ref, lse_ref, bias_ref, *, bq):
    L = q_ref.shape[0]
    step = pl.program_id(0)
    prefix = prefix_ref[0]
    limit = L - padding_ref[0]
    n = L // bq
    lane = lax.broadcasted_iota(jnp.int32, (1, 128), 1)
    @pl.when(step == 0)
    def _():
        for b in range(n):
            bias_ref[b] = key_bias(prefix, limit, b * bq, b * bq, bq, True, True)
    vT = jnp.transpose(v_ref[...])
    ones = jnp.ones((16, L), bf16)
    values = [jnp.concatenate([vT[64 * h:64 * h + 64], ones], axis=0) for h in range(2)]
    for b in range(n):
        start, stop = b * bq, (b + 1) * bq
        q = q_ref[start:stop, :]
        both = jnp.concatenate([jnp.where(lane < 64, q, 0), jnp.where(lane >= 64, q, 0)], axis=0).astype(bf16)
        s = []
        for kb in range(b + 1):
            t = dot_nt(k_ref[kb * bq:(kb + 1) * bq, :], both)
            if kb == b:
                t = t + jnp.concatenate([bias_ref[b], bias_ref[b]], axis=1)
            elif (kb + 1) * bq > L - 384:
                kk = kb * bq + lax.broadcasted_iota(jnp.int32, (bq, 1), 0)
                t = t + jnp.where(kk < limit, 0.0, NEGATIVE)
            s.append(t)
        m = functools.reduce(jnp.maximum, [jnp.max(t, axis=0, keepdims=True) for t in s])
        acc = [None, None]
        for kb in range(b + 1):
            e = jnp.exp(s[kb] - m).astype(bf16)
            for h in range(2):
                t = dot(values[h][:, kb * bq:(kb + 1) * bq], e[:, h * bq:(h + 1) * bq])
                acc[h] = t if acc[h] is None else acc[h] + t
        ctx = [a[:64] * (1.0 / a[64:65]) for a in acc]
        out_ref[start:stop, :] = jnp.transpose(jnp.concatenate(ctx, axis=0)).astype(bf16)
        for h in range(2):
            lse_ref[pl.ds(2 * step + h, 1), start:stop] = m[:, h * bq:(h + 1) * bq] + jnp.log(acc[h][64:65])

def attend(prefix, padding, qkv, bq=256):
    L = qkv.shape[0]
    D = qkv.shape[1] // 3
    n = D // 128
    smem = pl.BlockSpec(memory_space=pltpu.SMEM)
    col = lambda off: pl.BlockSpec((L, 128), lambda j: (0, j + off))
    return pl.pallas_call(
        functools.partial(attend_kernel, bq=bq), grid=(n,),
        in_specs=[smem, smem, col(0), col(n), col(2 * n)],
        out_specs=[col(0), pl.BlockSpec((2 * n, L), lambda j: (0, 0))],
        out_shape=[jax.ShapeDtypeStruct((L, D), bf16), jax.ShapeDtypeStruct((2 * n, L), f32)],
        scratch_shapes=[pltpu.VMEM((L // bq, bq, bq), f32)],
        compiler_params=cp(), name="attend",
        cost_estimate=HINT,
    )(prefix, padding, qkv, qkv, qkv)

def branch_kernel(order_ref, ctx_ref, tokens_ref, vec_ref, *refs):
    *pieces, resid_ref, normed_ref, weight_ref = refs
    @pl.when(pl.program_id(0) == 0)
    def _():
        in_order(order_ref, pieces, weight_ref)
    resid = tokens_ref[...].astype(f32) + (dot(ctx_ref[...], weight_ref[...]) + row_of(vec_ref, OBIAS))
    center = resid - jnp.mean(resid, axis=-1, keepdims=True)
    spread = jnp.mean(center * center, axis=-1, keepdims=True)
    normed = center * lax.rsqrt(spread + EPSILON) * row_of(vec_ref, GAIN2) + row_of(vec_ref, SHIFT2)
    resid_ref[...] = resid
    normed_ref[...] = normed.astype(bf16)

def branch(order, ctx, tokens, vecs, pieces, tm=256):
    R, D = ctx.shape
    n, high, _ = pieces[0].shape
    rows = pl.BlockSpec((tm, D), lambda i: (i, 0))
    return pl.pallas_call(
        branch_kernel, grid=(R // tm,),
        in_specs=[pl.BlockSpec(memory_space=pltpu.SMEM), rows, rows, pl.BlockSpec(vecs.shape, lambda i: (0, 0))]
        + [pl.BlockSpec((n, high, D), lambda i: (0, 0, 3))] * len(pieces),
        out_specs=[rows, rows, pl.BlockSpec((D, D), lambda i: (0, 0))],
        out_shape=[jax.ShapeDtypeStruct((R, D), f32), jax.ShapeDtypeStruct((R, D), bf16), jax.ShapeDtypeStruct((D, D), bf16)],
        compiler_params=cp(), name="branch", cost_estimate=HINT,
    )(order, ctx, tokens, vecs, *pieces)

def ffn_kernel(pos_ref, normed_ref, grad_ref, vec_ref, up_ref, down_ref, out_ref, dn_ref, keep1_ref, send1_ref, keep2_ref, send2_ref, biasg_ref,
               ups_ref, dns_ref, up_sem, dn_sem, *, shards, per, blocks):
    step = pl.program_id(0)
    last = pl.num_programs(0) - 1
    D = normed_ref.shape[1]
    tf = ups_ref.shape[3]
    half = shards // 2
    rows = D // shards
    each = blocks // 2
    slot = lax.rem(step, 2)
    block = lax.div(step, per)
    bslot = lax.rem(block, 2)
    groups = ((keep1_ref, send1_ref), (keep2_ref, send2_ref))

    def up_copies(slot, step, group):
        cols = pl.ds(pl.multiple_of(step * tf - group * each * D, tf), tf)
        return [pltpu.make_async_copy(ups_ref.at[slot, pl.ds(k * half, half)], groups[group][k].at[:, :, cols], up_sem.at[slot, k]) for k in range(2)]

    def down_copies(bslot, block, group):
        cols = pl.ds(pl.multiple_of((each + block - group * each) * D, D), D)
        return [pltpu.make_async_copy(dns_ref.at[bslot, pl.ds(k * half, half)], groups[group][k].at[:, :, cols], dn_sem.at[bslot, k]) for k in range(2)]

    def each_group(block, do):
        for group in range(2):
            pl.when((block >= group * each) & (block < (group + 1) * each))(functools.partial(do, group))

    def start_up(group):
        for c in up_copies(slot, step, group):
            c.start()

    def wait_up(slot, step):
        def do(group):
            for c in up_copies(slot, step, group):
                c.wait()
        each_group(lax.div(step, per), do)

    def start_down(group):
        for c in down_copies(bslot, block, group):
            c.start()

    def wait_down(bslot, block):
        def do(group):
            for c in down_copies(bslot, block, group):
                c.wait()
        each_group(block, do)

    @pl.when(step == 0)
    def _():
        out_ref[...] = jnp.zeros_like(out_ref)
        dn_ref[...] = jnp.zeros_like(dn_ref)

    @pl.when(step >= 2)
    def _():
        wait_up(slot, step - 2)

    @pl.when((step >= 2 * per) & (lax.rem(step, per) == 0))
    def _():
        wait_down(bslot, block - 2)

    n2 = normed_ref[...]
    go = grad_ref[...]
    up = up_ref[...]
    down = down_ref[...]
    bias = row_of(vec_ref, UBIAS)
    for k in range(1, blocks):
        bias = jnp.where(block == k, row_of(vec_ref, UBIAS + k), bias)
    u = dot(n2, up) + bias
    cdf = 0.5 * (1.0 + lax.erf(u * math.sqrt(0.5)))
    a = (u * cdf).astype(bf16)
    slope = cdf + u * (jnp.exp(-0.5 * u * u) * (1.0 / math.sqrt(2 * math.pi)))
    du = (dot_nt(go, down) * slope).astype(bf16)
    out_ref[...] += dot(a, down)
    dn_ref[...] += dot_nt(du, up)
    biasg_ref[...] = jnp.sum(du.astype(f32), axis=0, keepdims=True)
    upg = dot_tn(n2, du).astype(bf16)
    for i in range(shards):
        ups_ref[slot, pos_ref[i]] = upg[i * rows:(i + 1) * rows]
    downg = dot_tn(a, go).astype(bf16)
    here = tf // rows
    at = lax.rem(step, per) * here
    for i in range(here):
        dns_ref[bslot, pos_ref[at + i]] = downg[i * rows:(i + 1) * rows]
    each_group(block, start_up)

    @pl.when(lax.rem(step, per) == per - 1)
    def _():
        each_group(block, start_down)

    @pl.when(step == last)
    def _():
        for c in up_copies(1 - slot, step - 1, 1) + up_copies(slot, step, 1) + down_copies(1 - bslot, block - 1, 1) + down_copies(bslot, block, 1):
            c.wait()

def ffn(pos, normed, grad, vecs, wide, tf=512):
    R, D = normed.shape
    blocks = wide.shape[1] // D // 2
    F = blocks * D
    shards = pos.shape[0]
    rows = D // shards
    per = D // tf
    full = pl.BlockSpec((R, D), lambda j: (0, 0))
    hbm = pl.BlockSpec(memory_space=pl.ANY)
    part = jax.ShapeDtypeStruct((shards // 2, rows, F), bf16)
    return pl.pallas_call(
        functools.partial(ffn_kernel, shards=shards, per=per, blocks=blocks), grid=(F // tf,),
        in_specs=[pl.BlockSpec(memory_space=pltpu.SMEM), full, full, pl.BlockSpec((16, tf), lambda j: (0, lax.rem(j, per))),
                  pl.BlockSpec((D, tf), lambda j: (0, j)), pl.BlockSpec((tf, D), lambda j: (lax.rem(j, per), blocks + lax.div(j, per)))],
        out_specs=[full, full, hbm, hbm, hbm, hbm, pl.BlockSpec((1, tf), lambda j: (0, j))],
        out_shape=[jax.ShapeDtypeStruct((R, D), f32), jax.ShapeDtypeStruct((R, D), f32), part, part, part, part, jax.ShapeDtypeStruct((1, F), f32)],
        scratch_shapes=[pltpu.VMEM((2, shards, rows, tf), bf16), pltpu.VMEM((2, shards, rows, D), bf16),
                        pltpu.SemaphoreType.DMA((2, 2)), pltpu.SemaphoreType.DMA((2, 2))],
        compiler_params=cp(), name="ffn", cost_estimate=HINT,
    )(pos, normed, grad, vecs, wide, wide)

def middle_kernel(resid_ref, outacc_ref, dn_ref, go_ref, vec_ref, weight_ref,
                  out_ref, dres_ref, low_ref, dctx_ref, small_ref):
    i = pl.program_id(0)
    resid = resid_ref[...]
    out_ref[...] = (resid + outacc_ref[...] + row_of(vec_ref, DBIAS)).astype(bf16)
    center = resid - jnp.mean(resid, axis=-1, keepdims=True)
    spread = jnp.mean(center * center, axis=-1, keepdims=True)
    r = lax.rsqrt(spread + EPSILON)
    nhat = center * r
    dn = dn_ref[...]
    go = go_ref[...].astype(f32)
    e = dn * row_of(vec_ref, GAIN2)
    d_res = go + r * (e - jnp.mean(e, axis=-1, keepdims=True) - nhat * jnp.mean(e * nhat, axis=-1, keepdims=True))
    dres_ref[...] = d_res
    low = d_res.astype(bf16)
    low_ref[...] = low
    dctx_ref[...] = dot_nt(low, weight_ref[...]).astype(bf16)
    @pl.when(i == 0)
    def _():
        small_ref[...] = jnp.zeros_like(small_ref)
    small_ref[0:1, :] += jnp.sum(dn * nhat, axis=0, keepdims=True)
    small_ref[1:2, :] += jnp.sum(dn, axis=0, keepdims=True)
    small_ref[2:3, :] += jnp.sum(low.astype(f32), axis=0, keepdims=True)
    small_ref[3:4, :] += jnp.sum(go, axis=0, keepdims=True)

def middle(resid, outacc, dn, go, vecs, weight, tm=256):
    R, D = resid.shape
    rows = pl.BlockSpec((tm, D), lambda i: (i, 0))
    low = jax.ShapeDtypeStruct((R, D), bf16)
    return pl.pallas_call(
        middle_kernel, grid=(R // tm,),
        in_specs=[rows, rows, rows, rows, pl.BlockSpec(vecs.shape, lambda i: (0, 0)), pl.BlockSpec((D, D), lambda i: (0, 0))],
        out_specs=[rows, rows, rows, rows, pl.BlockSpec((8, D), lambda i: (0, 0))],
        out_shape=[low, jax.ShapeDtypeStruct((R, D), f32), low, low, jax.ShapeDtypeStruct((8, D), f32)],
        compiler_params=cp(), name="middle",
        cost_estimate=HINT,
    )(resid, outacc, dn, go, vecs, weight)

def attend_back_kernel(prefix_ref, padding_ref, q_ref, k_ref, v_ref, do_ref, o_ref, lse_ref, *refs, bq, first):
    dq_ref, dk_ref, dv_ref, small_ref, dka_ref, dva_ref, bias_ref = refs[-7:]
    L = q_ref.shape[0]
    step = pl.program_id(0) + first
    prefix = prefix_ref[0]
    limit = L - padding_ref[0]
    n = L // bq
    lane = lax.broadcasted_iota(jnp.int32, (1, 128), 1)
    @pl.when(pl.program_id(0) == 0)
    def _():
        for b in range(n):
            bias_ref[b] = key_bias(prefix, limit, b * bq, b * bq, bq, True, True)
    kT = jnp.transpose(k_ref[...])
    prod = do_ref[...].astype(f32) * o_ref[...].astype(f32)
    row = lax.broadcasted_iota(jnp.int32, (8, 128), 0)
    col = lax.broadcasted_iota(jnp.int32, (8, 128), 1)
    pick = jnp.where((col // 64) == row, 1.0, 0.0)
    delta = lax.dot_general(pick, prod, (((1,), (1,)), ((), ())), precision=lax.Precision.HIGHEST, preferred_element_type=f32)
    for b in range(n):
        start, stop = b * bq, (b + 1) * bq
        q = q_ref[start:stop, :]
        do = do_ref[start:stop, :]
        both = jnp.concatenate([jnp.where(lane < 64, q, 0), jnp.where(lane >= 64, q, 0)], axis=0).astype(bf16)
        dboth = jnp.concatenate([jnp.where(lane < 64, do, 0), jnp.where(lane >= 64, do, 0)], axis=0).astype(bf16)
        lse = jnp.concatenate([lse_ref[pl.ds(2 * step, 1), start:stop], lse_ref[pl.ds(2 * step + 1, 1), start:stop]], axis=1)
        inner = jnp.concatenate([delta[0:1, start:stop], delta[1:2, start:stop]], axis=1)
        dq = [None, None]
        for kb in range(b + 1):
            ks = slice(kb * bq, (kb + 1) * bq)
            s = dot_nt(k_ref[ks, :], both)
            if kb == b:
                s = s + jnp.concatenate([bias_ref[b], bias_ref[b]], axis=1)
            elif (kb + 1) * bq > L - 384:
                kk = kb * bq + lax.broadcasted_iota(jnp.int32, (bq, 1), 0)
                s = s + jnp.where(kk < limit, 0.0, NEGATIVE)
            p = jnp.exp(s - lse)
            ds = (p * (dot_nt(v_ref[ks, :], dboth) - inner)).astype(bf16)
            tv = dot(p.astype(bf16), dboth)
            tk = dot(ds, both)
            if kb == b:
                dva_ref[ks, :] = tv
                dka_ref[ks, :] = tk
            else:
                dva_ref[ks, :] += tv
                dka_ref[ks, :] += tk
            for h in range(2):
                t = dot(kT[64 * h:64 * h + 64, ks], ds[:, h * bq:(h + 1) * bq])
                dq[h] = t if dq[h] is None else dq[h] + t
        dq_ref[start:stop, :] = (jnp.transpose(jnp.concatenate(dq, axis=0)) * 0.125).astype(bf16)
    dk_ref[...] = dka_ref[...].astype(bf16)
    dv_ref[...] = dva_ref[...].astype(bf16)
    small_ref[0:1, :] = jnp.sum(dq_ref[...].astype(f32), axis=0, keepdims=True)
    small_ref[1:2, :] = jnp.sum(dv_ref[...].astype(f32), axis=0, keepdims=True)

def attend_back(prefix, padding, qkv, dctx, ctx, lse, first, count, width, earlier=(), bq=256):
    L = qkv.shape[0]
    D = dctx.shape[1]
    n = D // 128
    at = first % (width // 128)
    smem = pl.BlockSpec(memory_space=pltpu.SMEM)
    col = lambda off: pl.BlockSpec((L, 128), lambda j: (0, j + off))
    o = jax.ShapeDtypeStruct((L, width), bf16)
    return pl.pallas_call(
        functools.partial(attend_back_kernel, bq=bq, first=first), grid=(count,),
        in_specs=[smem, smem, col(first), col(n + first), col(2 * n + first), col(first), col(first), pl.BlockSpec((2 * n, L), lambda j: (0, 0))]
        + [pl.BlockSpec(memory_space=pl.ANY)] * len(earlier),
        out_specs=[col(at), col(at), col(at), pl.BlockSpec((8, 128), lambda j: (0, j + at))],
        out_shape=[o, o, o, jax.ShapeDtypeStruct((8, width), f32)],
        scratch_shapes=[pltpu.VMEM((L, 128), f32), pltpu.VMEM((L, 128), f32), pltpu.VMEM((L // bq, bq, bq), f32)],
        input_output_aliases={8 + i: i for i in range(len(earlier))},
        compiler_params=cp(), name="attend_back",
        cost_estimate=HINT,
    )(prefix, padding, qkv, qkv, qkv, dctx, ctx, lse, *earlier)

def weight_grad_kernel(pos_ref, *refs, sources, extra):
    left = refs[:max(sources) + 1]
    refs = refs[len(left):]
    right = refs[:len(sources)]
    refs = refs[len(right):]
    small_ref = refs[0] if extra else None
    keep_ref, send_ref, wide_ref = refs[1 if extra else 0:]
    shards = wide_ref.shape[0]
    half = shards // 2
    rows = left[0].shape[1] // shards
    for g, (source, d_ref) in enumerate(zip(sources, right)):
        value = dot_tn(left[source][...], d_ref[...]).astype(bf16)
        for i in range(shards):
            wide_ref[pos_ref[i], g * rows:(g + 1) * rows, :] = value[i * rows:(i + 1) * rows]
    if extra:
        for i in range(shards):
            wide_ref[pos_ref[i], len(sources) * rows:, :] = jnp.broadcast_to(small_ref[i:i + 1, :], (extra, small_ref.shape[1])).astype(bf16)
    keep_ref[...] = wide_ref[:half]
    send_ref[...] = wide_ref[half:]

def weight_grad(pos, left, right, sources, small=None, width=512, tn=256):
    R, D = left[0].shape
    shards = pos.shape[0]
    rows = D // shards
    extra = min(rows, 16) if small is not None else 0
    high = len(right) * rows + extra
    part = pl.BlockSpec((shards // 2, high, tn), lambda j: (0, 0, j))
    half = jax.ShapeDtypeStruct((shards // 2, high, width), bf16)
    more = [small] if extra else []
    cols = lambda first: pl.BlockSpec((R, tn), lambda j: (0, j + first))
    return pl.pallas_call(
        functools.partial(weight_grad_kernel, sources=sources, extra=extra), grid=(width // tn,),
        in_specs=[pl.BlockSpec(memory_space=pltpu.SMEM)] + [pl.BlockSpec((R, D), lambda j: (0, 0))] * len(left)
        + [cols(first) for _, first in right] + [pl.BlockSpec((shards, tn), lambda j: (0, j))] * len(more),
        out_specs=[part, part], out_shape=[half, half],
        scratch_shapes=[pltpu.VMEM((shards, high, tn), bf16)],
        compiler_params=cp(), name="weight_grad",
        cost_estimate=HINT,
    )(pos, *left, *[r for r, _ in right], *more)

def cotangent_kernel(*refs, count, chained):
    parts, w_ref, refs = refs[:count], refs[count], refs[count + 1:]
    step = pl.program_id(0)
    if chained:
        earlier_in, acc_ref, earlier_ref, sem = refs
        copy = pltpu.make_async_copy(earlier_in, earlier_ref, sem.at[0])
        @pl.when(step == 0)
        def _():
            copy.start()
    else:
        acc_ref, = refs
    for k, part in enumerate(parts):
        @pl.when(step == k)
        def _():
            term = dot_nt(part[...], w_ref[...])
            if k:
                term = term + acc_ref[...]
            if chained and k == count - 1:
                copy.wait()
                term = term + earlier_ref[...]
            acc_ref[...] = term

def cotangent(parts, w, number, earlier=None):
    R, width = parts[0].shape
    D = w.shape[0]
    per = D // width
    chained = earlier is not None
    return pl.pallas_call(
        functools.partial(cotangent_kernel, count=len(parts), chained=chained), grid=(len(parts),),
        in_specs=[pl.BlockSpec((R, width), lambda j: (0, 0))] * len(parts) + [pl.BlockSpec((D, width), lambda j: (0, j * per + number))]
        + [pl.BlockSpec(memory_space=pl.ANY)] * chained,
        out_specs=pl.BlockSpec((R, D), lambda j: (0, 0)), out_shape=jax.ShapeDtypeStruct((R, D), f32),
        scratch_shapes=[pltpu.VMEM((R, D), f32), pltpu.SemaphoreType.DMA((1,))] if chained else [],
        compiler_params=cp(), name="cotangent", cost_estimate=HINT,
    )(*parts, w, *([earlier] if chained else []))

def norm_back_kernel(dn_ref, xhat_ref, tokens_ref, dres_ref, vec_ref, out_ref, small_ref):
    dn = dn_ref[...]
    nhat = xhat_ref[...]
    x = tokens_ref[...].astype(f32)
    center = x - jnp.mean(x, axis=-1, keepdims=True)
    r = lax.rsqrt(jnp.mean(center * center, axis=-1, keepdims=True) + EPSILON)
    e = dn * row_of(vec_ref, GAIN1)
    d = dres_ref[...] + r * (e - jnp.mean(e, axis=-1, keepdims=True) - nhat * jnp.mean(e * nhat, axis=-1, keepdims=True))
    out_ref[...] = d.astype(bf16)
    @pl.when(pl.program_id(0) == 0)
    def _():
        small_ref[...] = jnp.zeros_like(small_ref)
    small_ref[0:1, :] += jnp.sum(dn * nhat, axis=0, keepdims=True)
    small_ref[1:2, :] += jnp.sum(dn, axis=0, keepdims=True)

def norm_back(dn, xhat, tokens, dres, vecs, tm=256):
    R, D = tokens.shape
    rows = pl.BlockSpec((tm, D), lambda i: (i, 0))
    return pl.pallas_call(
        norm_back_kernel, grid=(R // tm,),
        in_specs=[rows, rows, rows, rows, pl.BlockSpec(vecs.shape, lambda i: (0, 0))],
        out_specs=[rows, pl.BlockSpec((8, D), lambda i: (0, 0))],
        out_shape=[jax.ShapeDtypeStruct((R, D), bf16), jax.ShapeDtypeStruct((8, D), f32)],
        compiler_params=cp(), name="norm_back", cost_estimate=HINT,
    )(dn, xhat, tokens, dres, vecs)

def owned_kernel(*refs, counts, rows, blocks, wide):
    parts, at = [], 0
    for c in counts:
        parts.append(sum(r[0].astype(f32) for r in refs[at:at + c]))
        at += c
    up_ref, down_ref = refs[at:]
    half = blocks // len(counts)
    D = down_ref.shape[1]
    for h, part in enumerate(parts):
        for b in range(half):
            down_ref[(h * half + b) * rows:(h * half + b + 1) * rows, :] = part[:, (half + b) * D:(half + b + 1) * D]
    per = D // rows
    group = blocks * rows
    lane = lax.broadcasted_iota(jnp.int32, (rows, 128), 1)
    for tile in range(blocks * D // 128):
        value = None
        for k in range(128 // rows):
            unit = (tile * 128 + k * rows) // rows
            shard, b = unit // blocks, unit % blocks
            source = (b % half) * D + shard * rows
            piece = parts[b // half][:, source // 128 * 128:source // 128 * 128 + 128]
            shift = (k * rows - source % 128) % 128
            if shift:
                piece = pltpu.roll(piece, shift, 1)
            value = piece if value is None else jnp.where(lane >= k * rows, piece, value)
        up_ref[:, tile * 128:(tile + 1) * 128] = value

def owned(groups, D, blocks):
    _, rows, width = groups[0][0].shape
    terms = [t for g in groups for t in g]
    return pl.pallas_call(
        functools.partial(owned_kernel, counts=[len(g) for g in groups], rows=rows, blocks=blocks, wide=width), grid=(1,),
        in_specs=[pl.BlockSpec((1, rows, width), lambda i: (0, 0, 0))] * len(terms),
        out_specs=[pl.BlockSpec((rows, blocks * D), lambda i: (0, 0)), pl.BlockSpec((blocks * rows, D), lambda i: (0, 0))],
        out_shape=[jax.ShapeDtypeStruct((rows, blocks * D), f32), jax.ShapeDtypeStruct((blocks * rows, D), f32)],
        compiler_params=cp(), name="owned", cost_estimate=HINT,
    )(*terms)


class Plan:
    def __init__(self, dp, fsdp):
        self.total = dp * fsdp
        bits = self.total.bit_length() - 1
        low = fsdp.bit_length() - 1
        if fsdp == 4:
            self.core, z, rest = low, list(range(low)), list(range(low + 1, bits))
        else:
            self.core, z, rest = 0, list(range(1, low)), list(range(low, bits))
        a, b = rest[:len(rest) // 2], rest[len(rest) // 2:]
        self.stages = [(a, b), (b, a), (z, z)]
        self.third = len(z) == low

    def masks(self, stage, core):
        bits = self.stages[stage][core]
        return [sum(1 << b for k, b in enumerate(bits) if j >> k & 1) for j in range(1 << len(bits))]

    def pairs(self, stage, j):
        return [(i, i ^ self.masks(stage, i >> self.core & 1)[j]) for i in range(self.total)]

    def size(self, stage):
        return 1 << len(self.stages[stage][0])

    def places(self, me, fixed=False):
        shard = lax.iota(jnp.int32, self.total)
        rel = shard ^ me
        core = (shard >> self.core) & 1
        pos = (rel >> self.core) & 1
        for k, (a, b) in enumerate(self.stages):
            pick = lambda bits, v: sum((((v >> bit) & 1) << k) for k, bit in enumerate(bits))
            own = pick(a, shard) if fixed and k == 2 else jnp.where(core == 0, pick(a, rel), pick(b, rel))
            pos = (pos << len(a)) + own
        return pos

AXES = ("dp", "fsdp")

def swap_core(plan, x):
    return lax.ppermute(x, AXES, [(i, i ^ (1 << plan.core)) for i in range(plan.total)])

def exchange(plan, x, stage, j):
    return lax.ppermute(x, AXES, plan.pairs(stage, j))

class Gathering:
    def __init__(self, plan, shard):
        self.plan, self.shard = plan, shard
        self.arrays = [exchange(plan, shard, 2, j) for j in range(1, plan.size(2))]

    def spread(self):
        column = jnp.stack([self.shard] + self.arrays)
        self.near = [exchange(self.plan, column, 1, j) for j in range(1, self.plan.size(1))]
        self.far = [exchange(self.plan, column, 0, j) for j in range(1, self.plan.size(0))]
        self.arrays = [column] + self.near + self.far

    def spread_again(self):
        n = self.plan.size(1)
        near, far = self.arrays[:n], self.arrays[n:]
        rest = [[exchange(self.plan, p, 0, j + 1) for p in near[1:]] for j in range(len(far))]
        other = [swap_core(self.plan, p) for p in self.arrays]
        self.first, self.other, self.arrays = self.arrays, other, [p for row in rest for p in row]

    def finish(self):
        n = self.plan.size(1)
        sides = (self.first, self.arrays), (self.other, [swap_core(self.plan, p) for p in self.arrays])
        pieces = []
        for first, rest in sides:
            pieces += first[:n]
            for j in range(self.plan.size(0) - 1):
                pieces += [first[n + j]] + rest[j * (n - 1):(j + 1) * (n - 1)]
        return pieces

def step(x, after, *reductions):
    x, _ = tie(x, after, *reductions)
    reductions = [r for r in reductions if r.stage < 3]
    if reductions:
        for r in reductions:
            r.add()
        x, = tie(x, *reductions)
        for r in reductions:
            r.go()
    return x

class Reduction:
    def __init__(self, plan, keep, send, one=False):
        self.plan, self.stage, self.size, self.one = plan, 0, keep.shape[0], one and plan.third
        self.terms = [keep, swap_core(plan, send)]
        self.sent = []

    def add(self):
        n = self.plan.size(self.stage)
        part = self.size // n
        if self.one and self.stage == 2:
            self.sent = [sum(t[:n].astype(f32) for t in self.terms).astype(self.terms[0].dtype)]
            return
        self.sent = [sum(t[j * part:(j + 1) * part].astype(f32) for t in self.terms).astype(self.terms[0].dtype) for j in range(1, n)]

    def go(self):
        if self.one and self.stage == 2:
            self.terms = [lax.psum_scatter(self.sent[0], AXES[1], scatter_dimension=0, tiled=False)[None]]
        else:
            self.terms = self.terms + [exchange(self.plan, s, self.stage, j + 1) for j, s in enumerate(self.sent)]
        self.sent = []
        self.size //= self.plan.size(self.stage)
        self.stage += 1

    def finish(self):
        while self.stage < 3:
            self.add()
            self.go()
        return sum(t[0].astype(f32) for t in self.terms)

def tie(*trees):
    flat = []
    for t in trees:
        flat += t.terms + t.sent if isinstance(t, Reduction) else t.arrays if isinstance(t, Gathering) else [t]
    flat = list(lax.optimization_barrier(tuple(flat)))
    out = []
    for t in trees:
        if isinstance(t, Reduction):
            t.terms = [flat.pop(0) for _ in t.terms]
            t.sent = [flat.pop(0) for _ in t.sent]
        elif isinstance(t, Gathering):
            t.arrays = [flat.pop(0) for _ in t.arrays]
        else:
            out.append(flat.pop(0))
    return out

def body(plan, tokens, prefix_len, padding_len, first_gain, first_shift, inproj_weight, query_bias, value_bias,
         outproj_weight, outproj_bias, second_gain, second_shift, up_weight, up_bias, down_weight, down_bias, grad_out):
    total = plan.total
    R, D = tokens.shape
    F = up_weight.shape[1]
    rows = D // total
    blocks = F // D
    me = lax.axis_index(AXES)
    pos = plan.places(me)
    pos_one = plan.places(me, plan.third)
    shard = lax.iota(jnp.int32, total)
    order = jnp.sum(jnp.where(pos[None, :] == shard[:, None], shard[None, :], 0), axis=1)
    n = first_gain.shape[0]
    half = blocks // 2
    up_local = up_weight.reshape(rows, total, blocks, rows).transpose(0, 2, 1, 3).reshape(rows, F)
    down_local = [down_weight[b * rows:(b + 1) * rows] for b in range(blocks)]
    small = jnp.concatenate([first_gain, first_shift, query_bias, value_bias, outproj_bias, second_gain, second_shift, down_bias, up_bias])
    small = jnp.pad(small.reshape(8 + blocks, rows).T, ((0, 0), (0, 128 - 8 - blocks)))
    inward = Gathering(plan, jnp.concatenate([inproj_weight, outproj_weight, small], axis=1))
    wide = lax.all_gather(jnp.concatenate([up_local] + down_local, axis=1), AXES, axis=0, tiled=True)
    xhat = norm(tokens)
    xhat, = tie(xhat, inward)
    inward.spread()
    xhat, = tie(xhat, inward)
    inward.spread_again()
    xhat, *inward.other = tie(xhat, *inward.other, inward)
    inward = inward.finish()
    n1, qkv, w_in, vecs = project(order, xhat, inward)
    ctx, lse = attend(prefix_len, padding_len, qkv)
    resid, n2, w_out = branch(order, ctx, tokens, vecs, inward)
    cut = D // 2
    n_pairs = D // 128
    def back(first, x, earlier=()):
        return attend_back(prefix_len, padding_len, qkv, x, ctx, lse, first, n_pairs // 4, cut, earlier)
    acc, dn2, keep1, send1, keep2, send2, ubias_grad = ffn(pos_one, n2, grad_out, vecs, wide)
    g1 = Reduction(plan, keep1, send1, True)
    g2 = Reduction(plan, keep2, send2, True)
    out, dres, low, dctx, mid = middle(resid, acc, dn2, grad_out, vecs, w_out)
    dctx = step(dctx, dres, g1)
    d1 = back(0, dctx)
    dctx = step(dctx, d1[0], g2)
    d1 = back(n_pairs // 4, dctx, d1)
    n1a = step(n1, d1[0], g1)
    g3 = Reduction(plan, *weight_grad(pos, (n1a, ctx), ((d1[0], 0), (d1[1], 0), (d1[2], 0), (low, 0), (low, cut // 256)), (0, 0, 0, 1, 1), width=cut))
    dctx, _ = tie(dctx, g3.terms[0])
    d2 = back(n_pairs // 2, dctx)
    w_in = step(w_in, d2[0], g2, g1)
    part = cotangent(d1[:3], w_in, 0)
    dctx = step(dctx, part, g3)
    d2 = back(n_pairs * 3 // 4, dctx, d2)
    n1b = step(n1, d2[0], g2)
    per = lambda v: v.reshape(total, -1)
    att = jnp.concatenate([d1[3], d2[3]], axis=1)
    ubg = ubias_grad.reshape(blocks, total, rows).transpose(1, 0, 2).reshape(total, -1)
    early = jnp.concatenate([per(att[0]), per(att[1]), per(mid[2]), per(mid[0]), per(mid[1]), per(mid[3]), ubg], axis=1)
    early = jnp.pad(early, ((0, 0), (0, cut - early.shape[1])))
    g4 = Reduction(plan, *weight_grad(pos, (n1b,), ((d2[0], 0), (d2[1], 0), (d2[2], 0)), (0, 0, 0), early, width=cut))
    part = step(part, g4.terms[0], g3)
    part = cotangent(d2[:3], w_in, 1, part)
    part = step(part, part, g4, g3)
    tokens_grad, end = norm_back(part, xhat, tokens, dres, vecs)
    end = step(end, end, g4)
    end = jnp.concatenate([per(end[0]), per(end[1])], axis=1)
    end = jnp.sum(jnp.where((pos[:, None] == shard[None, :])[:, :, None], end[:, None, :], 0.0), axis=0)[:, None, :]
    late = Reduction(plan, end[:total // 2], end[total // 2:])
    out = step(out, out, late, g4)
    out = step(out, out, late, g1, g2)
    out = step(out, out, late, g4)
    late, in1, in2 = late.finish()[0], g3.finish(), g4.finish()
    up_grad, down_grad = owned([g1.terms, g2.terms], D, blocks)
    out_grad = jnp.concatenate([in1[3 * rows:4 * rows], in1[4 * rows:]], axis=1)
    in_grad = jnp.concatenate([g[k * rows:(k + 1) * rows] for k in range(3) for g in (in1, in2)], axis=1)
    early = in2[3 * rows]
    e = [early[i * n:(i + 1) * n] for i in range(6)]
    return (out, tokens_grad, late[:n], late[n:], in_grad, e[0], e[1], out_grad, e[2], e[3], e[4], up_grad, early[6 * n:6 * n + F // total], down_grad, e[5])

def solution(mesh):
    plan = Plan(mesh.shape["dp"], mesh.shape["fsdp"])
    rows, flat = P(AXES, None), P(AXES)
    ins = (rows, flat, flat, flat, flat, rows, flat, flat, rows, flat, flat, flat, rows, flat, rows, flat, rows)
    outs = (rows, rows, flat, flat, rows, flat, flat, rows, flat, flat, flat, rows, flat, rows, flat)
    return jax.shard_map(functools.partial(body, plan), mesh=mesh, in_specs=ins, out_specs=outs, check_vma=False)
```

```python
import functools, math
import jax, jax.numpy as jnp
from jax import lax
from jax.sharding import PartitionSpec as P
from jax.experimental import pallas as pl
from jax.experimental.pallas import tpu as pltpu
HEADS=16
EPSILON = 1e-05
NEGATIVE = -1000000000.0
bf16=jnp.bfloat16; f32=jnp.float32
VMEM_LIMIT=60*1024*1024
HINT=pl.CostEstimate(flops=1000, bytes_accessed=1000, transcendentals=0)
def cp(n=1): return pltpu.CompilerParams(dimension_semantics=("arbitrary",)*n, vmem_limit_bytes=VMEM_LIMIT)
def dot(a,b): return lax.dot_general(a,b,(((1,),(0,)),((),())),preferred_element_type=f32)
def dot_nt(a,b): return lax.dot_general(a,b,(((1,),(1,)),((),())),preferred_element_type=f32)
def dot_tn(a,b): return lax.dot_general(a,b,(((0,),(0,)),((),())),preferred_element_type=f32)

GAIN1, SHIFT1, QBIAS, VBIAS, OBIAS, GAIN2, SHIFT2, DBIAS, UBIAS = range(9)

def row_of(ref, k):
    return ref[k:k + 1, :]

def norm_kernel(tokens_ref, out_ref):
    x = tokens_ref[...].astype(f32)
    mean = jnp.mean(x, axis=-1, keepdims=True)
    center = x - mean
    r = lax.rsqrt(jnp.mean(center * center, axis=-1, keepdims=True) + EPSILON)
    lane = lax.broadcasted_iota(jnp.int32, out_ref.shape, 1)
    out_ref[...] = jnp.where(lane == 0, mean, r)

def norm(tokens, tm=256):
    R, D = tokens.shape
    return pl.pallas_call(
        norm_kernel, grid=(R // tm,), in_specs=[pl.BlockSpec((tm, D), lambda i: (i, 0))], out_specs=pl.BlockSpec((tm, 128), lambda i: (i, 0)),
        out_shape=jax.ShapeDtypeStruct((R, 128), f32), compiler_params=cp(), name="norm", cost_estimate=HINT,
    )(tokens)

def in_order(order_ref, pieces, whole_ref):
    n, rows, _ = pieces[0].shape
    for p, piece in enumerate(pieces):
        for i in range(n):
            whole_ref[pl.ds(pl.multiple_of(order_ref[p * n + i] * rows, rows), rows), :] = piece[i]

def project_kernel(order_ref, tokens_ref, stat_ref, *refs, count):
    pieces, sides = refs[:count], refs[count:2 * count]
    normed_ref, out_ref, vec_ref, weight_ref, side_ref, all_ref = refs[2 * count:]
    step = pl.program_id(0)
    @pl.when(step == 0)
    def _():
        in_order(order_ref, sides, side_ref)
        all_ref[...] = jnp.transpose(side_ref[...].astype(f32))
        vec_ref[...] = all_ref[:16, :]
        xhat = (tokens_ref[...].astype(f32) - stat_ref[:, 0:1]) * stat_ref[:, 1:2]
        normed_ref[...] = (xhat * all_ref[GAIN1:GAIN1 + 1, :] + all_ref[SHIFT1:SHIFT1 + 1, :]).astype(bf16)
    in_order(order_ref, pieces, weight_ref)
    D = normed_ref.shape[1]
    tn = out_ref.shape[1]
    third = pl.num_programs(0) // 3
    at = pl.ds(pl.multiple_of(lax.rem(step, D // tn) * tn, tn), tn)
    bias = jnp.where(step < third, all_ref[QBIAS:QBIAS + 1, at], jnp.where(step < 2 * third, 0.0, all_ref[VBIAS:VBIAS + 1, at]))
    factor = jnp.where(step < third, 0.125, 1.0)
    out = dot(normed_ref[...], weight_ref[...]) + bias
    out_ref[...] = (out * factor).astype(bf16)

def project(order, tokens, stats, pieces, tn=512):
    R, D = tokens.shape
    n, rows, width = pieces[0].shape
    N = 3 * D
    full = pl.BlockSpec((R, D), lambda j: (0, 0))
    return pl.pallas_call(
        functools.partial(project_kernel, count=len(pieces)), grid=(N // tn,),
        in_specs=[pl.BlockSpec(memory_space=pltpu.SMEM), full, pl.BlockSpec((R, 128), lambda j: (0, 0))]
        + [pl.BlockSpec((n, rows, tn), lambda j: (0, 0, j))] * len(pieces)
        + [pl.BlockSpec((n, rows, 128), lambda j: (0, 0, width // 128 - 1))] * len(pieces),
        out_specs=[full, pl.BlockSpec((R, tn), lambda j: (0, j)), pl.BlockSpec((16, D), lambda j: (0, 0))],
        out_shape=[jax.ShapeDtypeStruct((R, D), bf16), jax.ShapeDtypeStruct((R, N), bf16), jax.ShapeDtypeStruct((16, D), f32)],
        scratch_shapes=[pltpu.VMEM((D, tn), bf16), pltpu.VMEM((D, 128), bf16), pltpu.VMEM((128, D), f32)],
        compiler_params=cp(), name="project", cost_estimate=HINT,
    )(order, tokens, stats, *pieces, *pieces)

def key_bias(prefix, limit, lo, q0, bq, transposed, diagonal):
    shape = (bq, bq)
    kd = 0 if transposed else 1
    k = lo + lax.broadcasted_iota(jnp.int32, shape, kd)
    ok = k < limit
    if diagonal:
        q = q0 + lax.broadcasted_iota(jnp.int32, shape, 1 - kd)
        ok = ok & ((k < prefix) | (k <= q))
    return jnp.where(ok, 0.0, NEGATIVE)

def attend_kernel(prefix_ref, padding_ref, q_ref, k_ref, v_ref, out_ref, lse_ref, bias_ref, *, bq):
    L = q_ref.shape[0]
    step = pl.program_id(0)
    prefix = prefix_ref[0]
    limit = L - padding_ref[0]
    n = L // bq
    lane = lax.broadcasted_iota(jnp.int32, (1, 128), 1)
    @pl.when(step == 0)
    def _():
        for b in range(n):
            bias_ref[b] = key_bias(prefix, limit, b * bq, b * bq, bq, True, True)
    vT = jnp.transpose(v_ref[...])
    ones = jnp.ones((16, L), bf16)
    values = [jnp.concatenate([vT[64 * h:64 * h + 64], ones], axis=0) for h in range(2)]
    for b in range(n):
        start, stop = b * bq, (b + 1) * bq
        q = q_ref[start:stop, :]
        both = jnp.concatenate([jnp.where(lane < 64, q, 0), jnp.where(lane >= 64, q, 0)], axis=0).astype(bf16)
        s = []
        for kb in range(b + 1):
            t = dot_nt(k_ref[kb * bq:(kb + 1) * bq, :], both)
            if kb == b:
                t = t + jnp.concatenate([bias_ref[b], bias_ref[b]], axis=1)
            elif (kb + 1) * bq > L - 384:
                kk = kb * bq + lax.broadcasted_iota(jnp.int32, (bq, 1), 0)
                t = t + jnp.where(kk < limit, 0.0, NEGATIVE)
            s.append(t)
        m = functools.reduce(jnp.maximum, [jnp.max(t, axis=0, keepdims=True) for t in s])
        acc = [None, None]
        for kb in range(b + 1):
            e = jnp.exp(s[kb] - m).astype(bf16)
            for h in range(2):
                t = dot(values[h][:, kb * bq:(kb + 1) * bq], e[:, h * bq:(h + 1) * bq])
                acc[h] = t if acc[h] is None else acc[h] + t
        ctx = [a[:64] * (1.0 / a[64:65]) for a in acc]
        out_ref[start:stop, :] = jnp.transpose(jnp.concatenate(ctx, axis=0)).astype(bf16)
        for h in range(2):
            lse_ref[pl.ds(2 * step + h, 1), start:stop] = m[:, h * bq:(h + 1) * bq] + jnp.log(acc[h][64:65])

def attend(prefix, padding, qkv, bq=256):
    L = qkv.shape[0]
    D = qkv.shape[1] // 3
    n = D // 128
    smem = pl.BlockSpec(memory_space=pltpu.SMEM)
    col = lambda off: pl.BlockSpec((L, 128), lambda j: (0, j + off))
    return pl.pallas_call(
        functools.partial(attend_kernel, bq=bq), grid=(n,),
        in_specs=[smem, smem, col(0), col(n), col(2 * n)],
        out_specs=[col(0), pl.BlockSpec((2 * n, L), lambda j: (0, 0))],
        out_shape=[jax.ShapeDtypeStruct((L, D), bf16), jax.ShapeDtypeStruct((2 * n, L), f32)],
        scratch_shapes=[pltpu.VMEM((L // bq, bq, bq), f32)],
        compiler_params=cp(), name="attend",
        cost_estimate=HINT,
    )(prefix, padding, qkv, qkv, qkv)

def branch_kernel(order_ref, ctx_ref, tokens_ref, vec_ref, *refs):
    *pieces, resid_ref, normed_ref, weight_ref = refs
    @pl.when(pl.program_id(0) == 0)
    def _():
        in_order(order_ref, pieces, weight_ref)
    resid = tokens_ref[...].astype(f32) + (dot(ctx_ref[...], weight_ref[...]) + row_of(vec_ref, OBIAS))
    center = resid - jnp.mean(resid, axis=-1, keepdims=True)
    spread = jnp.mean(center * center, axis=-1, keepdims=True)
    normed = center * lax.rsqrt(spread + EPSILON) * row_of(vec_ref, GAIN2) + row_of(vec_ref, SHIFT2)
    resid_ref[...] = resid
    normed_ref[...] = normed.astype(bf16)

def branch(order, ctx, tokens, vecs, pieces, tm=256):
    R, D = ctx.shape
    n, high, _ = pieces[0].shape
    rows = pl.BlockSpec((tm, D), lambda i: (i, 0))
    return pl.pallas_call(
        branch_kernel, grid=(R // tm,),
        in_specs=[pl.BlockSpec(memory_space=pltpu.SMEM), rows, rows, pl.BlockSpec(vecs.shape, lambda i: (0, 0))]
        + [pl.BlockSpec((n, high, D), lambda i: (0, 0, 3))] * len(pieces),
        out_specs=[rows, rows, pl.BlockSpec((D, D), lambda i: (0, 0))],
        out_shape=[jax.ShapeDtypeStruct((R, D), f32), jax.ShapeDtypeStruct((R, D), bf16), jax.ShapeDtypeStruct((D, D), bf16)],
        compiler_params=cp(), name="branch", cost_estimate=HINT,
    )(order, ctx, tokens, vecs, *pieces)

def ffn_kernel(pos_ref, normed_ref, grad_ref, vec_ref, rows_ref, up_ref, down_ref, resid_in, weight_in,
               result_out, low_out, dctx_out, keep1_ref, send1_ref, keep2_ref, send2_ref, biasg_ref, small_ref,
               out_ref, dn_ref, ups_ref, dns_ref, resid_ref, weight_ref, result_ref, low_ref, dctx_ref, up_sem, dn_sem, in_sem, out_sem, *, shards, per, blocks, tm):
    step = pl.program_id(0)
    last = pl.num_programs(0) - 1
    D = normed_ref.shape[1]
    tf = ups_ref.shape[3]
    half = shards // 2
    rows = D // shards
    each = blocks // 2
    slot = lax.rem(step, 2)
    block = lax.div(step, per)
    bslot = lax.rem(block, 2)
    groups = ((keep1_ref, send1_ref), (keep2_ref, send2_ref))

    def up_copies(slot, step, group):
        cols = pl.ds(pl.multiple_of(step * tf - group * each * D, tf), tf)
        return [pltpu.make_async_copy(ups_ref.at[slot, pl.ds(k * half, half)], groups[group][k].at[:, :, cols], up_sem.at[slot, k]) for k in range(2)]

    def down_copies(bslot, block, group):
        cols = pl.ds(pl.multiple_of((each + block - group * each) * D, D), D)
        return [pltpu.make_async_copy(dns_ref.at[bslot, pl.ds(k * half, half)], groups[group][k].at[:, :, cols], dn_sem.at[bslot, k]) for k in range(2)]

    def each_group(block, do):
        for group in range(2):
            pl.when((block >= group * each) & (block < (group + 1) * each))(functools.partial(do, group))

    def start_up(group):
        for c in up_copies(slot, step, group):
            c.start()

    def wait_up(slot, step):
        def do(group):
            for c in up_copies(slot, step, group):
                c.wait()
        each_group(lax.div(step, per), do)

    def start_down(group):
        for c in down_copies(bslot, block, group):
            c.start()

    def wait_down(bslot, block):
        def do(group):
            for c in down_copies(bslot, block, group):
                c.wait()
        each_group(block, do)

    loads = [pltpu.make_async_copy(resid_in, resid_ref, in_sem.at[0]), pltpu.make_async_copy(weight_in, weight_ref, in_sem.at[1])]

    @pl.when(step == 0)
    def _():
        for c in loads:
            c.start()
        out_ref[...] = jnp.zeros_like(out_ref)
        dn_ref[...] = jnp.zeros_like(dn_ref)

    @pl.when(step >= 2)
    def _():
        wait_up(slot, step - 2)

    @pl.when((step >= 2 * per) & (lax.rem(step, per) == 0))
    def _():
        wait_down(bslot, block - 2)

    n2 = normed_ref[...]
    go = grad_ref[...]
    up = up_ref[...]
    down = down_ref[...]
    bias = row_of(vec_ref, UBIAS)
    for k in range(1, blocks):
        bias = jnp.where(block == k, row_of(vec_ref, UBIAS + k), bias)
    u = dot(n2, up) + bias
    cdf = 0.5 * (1.0 + lax.erf(u * math.sqrt(0.5)))
    a = (u * cdf).astype(bf16)
    slope = cdf + u * (jnp.exp(-0.5 * u * u) * (1.0 / math.sqrt(2 * math.pi)))
    du = (dot_nt(go, down) * slope).astype(bf16)
    out_ref[...] += dot(a, down)
    dn_ref[...] += dot_nt(du, up)
    biasg_ref[...] = jnp.sum(du.astype(f32), axis=0, keepdims=True)
    upg = dot_tn(n2, du).astype(bf16)
    for i in range(shards):
        ups_ref[slot, pos_ref[i]] = upg[i * rows:(i + 1) * rows]
    downg = dot_tn(a, go).astype(bf16)
    here = tf // rows
    at = lax.rem(step, per) * here
    for i in range(here):
        dns_ref[bslot, pos_ref[at + i]] = downg[i * rows:(i + 1) * rows]
    each_group(block, start_up)

    @pl.when(lax.rem(step, per) == per - 1)
    def _():
        each_group(block, start_down)

    @pl.when(step == last)
    def _():
        for c in loads:
            c.wait()
        small_ref[...] = jnp.zeros_like(small_ref)
        stores = []
        for i in range(resid_ref.shape[0] // tm):
            at = slice(i * tm, (i + 1) * tm)
            resid = resid_ref[at]
            result_ref[at] = (resid + out_ref[at] + row_of(rows_ref, DBIAS)).astype(bf16)
            center = resid - jnp.mean(resid, axis=-1, keepdims=True)
            r = lax.rsqrt(jnp.mean(center * center, axis=-1, keepdims=True) + EPSILON)
            nhat = center * r
            dn = dn_ref[at]
            go = grad_ref[at].astype(f32)
            e = dn * row_of(rows_ref, GAIN2)
            low = (go + r * (e - jnp.mean(e, axis=-1, keepdims=True) - nhat * jnp.mean(e * nhat, axis=-1, keepdims=True))).astype(bf16)
            low_ref[at] = low
            dctx_ref[at] = dot_nt(low, weight_ref[...]).astype(bf16)
            small_ref[0:1, :] += jnp.sum(dn * nhat, axis=0, keepdims=True)
            small_ref[1:2, :] += jnp.sum(dn, axis=0, keepdims=True)
            small_ref[2:3, :] += jnp.sum(low.astype(f32), axis=0, keepdims=True)
            small_ref[3:4, :] += jnp.sum(go, axis=0, keepdims=True)
            for k, (here, there) in enumerate(((result_ref, result_out), (low_ref, low_out), (dctx_ref, dctx_out))):
                c = pltpu.make_async_copy(here.at[pl.ds(i * tm, tm)], there.at[pl.ds(i * tm, tm)], out_sem.at[i, k])
                c.start()
                stores.append(c)
        for c in stores + up_copies(1 - slot, step - 1, 1) + up_copies(slot, step, 1) + down_copies(1 - bslot, block - 1, 1) + down_copies(bslot, block, 1):
            c.wait()

def ffn(pos, normed, grad, vecs, wide, resid, weight, tf=512, tm=256):
    R, D = normed.shape
    blocks = wide.shape[1] // D // 2
    F = blocks * D
    shards = pos.shape[0]
    rows = D // shards
    per = D // tf
    full = pl.BlockSpec((R, D), lambda j: (0, 0))
    hbm = pl.BlockSpec(memory_space=pl.ANY)
    part = jax.ShapeDtypeStruct((shards // 2, rows, F), bf16)
    low = jax.ShapeDtypeStruct((R, D), bf16)
    return pl.pallas_call(
        functools.partial(ffn_kernel, shards=shards, per=per, blocks=blocks, tm=tm), grid=(F // tf,),
        in_specs=[pl.BlockSpec(memory_space=pltpu.SMEM), full, full, pl.BlockSpec((16, tf), lambda j: (0, lax.rem(j, per))), pl.BlockSpec((16, D), lambda j: (0, 0)),
                  pl.BlockSpec((D, tf), lambda j: (0, j)), pl.BlockSpec((tf, D), lambda j: (lax.rem(j, per), blocks + lax.div(j, per))), hbm, hbm],
        out_specs=[hbm] * 7 + [pl.BlockSpec((1, tf), lambda j: (0, j)), pl.BlockSpec((8, D), lambda j: (0, 0))],
        out_shape=[low, low, low, part, part, part, part, jax.ShapeDtypeStruct((1, F), f32), jax.ShapeDtypeStruct((8, D), f32)],
        scratch_shapes=[pltpu.VMEM((R, D), f32), pltpu.VMEM((R, D), f32), pltpu.VMEM((2, shards, rows, tf), bf16), pltpu.VMEM((2, shards, rows, D), bf16),
                        pltpu.VMEM((R, D), f32), pltpu.VMEM((D, D), bf16), pltpu.VMEM((R, D), bf16), pltpu.VMEM((R, D), bf16), pltpu.VMEM((R, D), bf16),
                        pltpu.SemaphoreType.DMA((2, 2)), pltpu.SemaphoreType.DMA((2, 2)), pltpu.SemaphoreType.DMA((2,)), pltpu.SemaphoreType.DMA((R // tm, 3))],
        compiler_params=cp(), name="ffn", cost_estimate=HINT,
    )(pos, normed, grad, vecs, vecs, wide, wide, resid, weight)

def attend_back_kernel(prefix_ref, padding_ref, q_ref, k_ref, v_ref, do_ref, o_ref, lse_ref, *refs, bq, first):
    d_ref, small_ref, dka_ref, dva_ref, bias_ref = refs[-5:]
    L = q_ref.shape[0]
    step = pl.program_id(0) + first
    prefix = prefix_ref[0]
    limit = L - padding_ref[0]
    n = L // bq
    lane = lax.broadcasted_iota(jnp.int32, (1, 128), 1)
    @pl.when(pl.program_id(0) == 0)
    def _():
        for b in range(n):
            bias_ref[b] = key_bias(prefix, limit, b * bq, b * bq, bq, True, True)
    kT = jnp.transpose(k_ref[...])
    prod = do_ref[...].astype(f32) * o_ref[...].astype(f32)
    row = lax.broadcasted_iota(jnp.int32, (8, 128), 0)
    col = lax.broadcasted_iota(jnp.int32, (8, 128), 1)
    pick = jnp.where((col // 64) == row, 1.0, 0.0)
    delta = lax.dot_general(pick, prod, (((1,), (1,)), ((), ())), precision=lax.Precision.HIGHEST, preferred_element_type=f32)
    for b in range(n):
        start, stop = b * bq, (b + 1) * bq
        q = q_ref[start:stop, :]
        do = do_ref[start:stop, :]
        both = jnp.concatenate([jnp.where(lane < 64, q, 0), jnp.where(lane >= 64, q, 0)], axis=0).astype(bf16)
        dboth = jnp.concatenate([jnp.where(lane < 64, do, 0), jnp.where(lane >= 64, do, 0)], axis=0).astype(bf16)
        lse = jnp.concatenate([lse_ref[pl.ds(2 * step, 1), start:stop], lse_ref[pl.ds(2 * step + 1, 1), start:stop]], axis=1)
        inner = jnp.concatenate([delta[0:1, start:stop], delta[1:2, start:stop]], axis=1)
        dq = [None, None]
        for kb in range(b + 1):
            ks = slice(kb * bq, (kb + 1) * bq)
            s = dot_nt(k_ref[ks, :], both)
            if kb == b:
                s = s + jnp.concatenate([bias_ref[b], bias_ref[b]], axis=1)
            elif (kb + 1) * bq > L - 384:
                kk = kb * bq + lax.broadcasted_iota(jnp.int32, (bq, 1), 0)
                s = s + jnp.where(kk < limit, 0.0, NEGATIVE)
            p = jnp.exp(s - lse)
            ds = (p * (dot_nt(v_ref[ks, :], dboth) - inner)).astype(bf16)
            tv = dot(p.astype(bf16), dboth)
            tk = dot(ds, both)
            if kb == b:
                dva_ref[ks, :] = tv
                dka_ref[ks, :] = tk
            else:
                dva_ref[ks, :] += tv
                dka_ref[ks, :] += tk
            for h in range(2):
                t = dot(kT[64 * h:64 * h + 64, ks], ds[:, h * bq:(h + 1) * bq])
                dq[h] = t if dq[h] is None else dq[h] + t
        d_ref[0, start:stop, :] = (jnp.transpose(jnp.concatenate(dq, axis=0)) * 0.125).astype(bf16)
    d_ref[1] = dka_ref[...].astype(bf16)
    d_ref[2] = dva_ref[...].astype(bf16)
    small_ref[0:1, :] = jnp.sum(d_ref[0].astype(f32), axis=0, keepdims=True)
    small_ref[1:2, :] = jnp.sum(d_ref[2].astype(f32), axis=0, keepdims=True)

def attend_back(prefix, padding, qkv, dctx, ctx, lse, first, count, width, earlier=(), bq=256):
    L = qkv.shape[0]
    D = dctx.shape[1]
    n = D // 128
    at = first % (width // 128)
    smem = pl.BlockSpec(memory_space=pltpu.SMEM)
    col = lambda off: pl.BlockSpec((L, 128), lambda j: (0, j + off))
    return pl.pallas_call(
        functools.partial(attend_back_kernel, bq=bq, first=first), grid=(count,),
        in_specs=[smem, smem, col(first), col(n + first), col(2 * n + first), col(first), col(first), pl.BlockSpec((2 * n, L), lambda j: (0, 0))]
        + [pl.BlockSpec(memory_space=pl.ANY)] * len(earlier),
        out_specs=[pl.BlockSpec((3, L, 128), lambda j: (0, 0, j + at)), pl.BlockSpec((8, 128), lambda j: (0, j + at))],
        out_shape=[jax.ShapeDtypeStruct((3, L, width), bf16), jax.ShapeDtypeStruct((8, width), f32)],
        scratch_shapes=[pltpu.VMEM((L, 128), f32), pltpu.VMEM((L, 128), f32), pltpu.VMEM((L // bq, bq, bq), f32)],
        input_output_aliases={8 + i: i for i in range(len(earlier))},
        compiler_params=cp(), name="attend_back",
        cost_estimate=HINT,
    )(prefix, padding, qkv, qkv, qkv, dctx, ctx, lse, *earlier)

def weight_grad_kernel(pos_ref, left_ref, d_ref, *refs, each, other, extra):
    refs = list(refs)
    if other:
        low_ref, second_in = refs[:2]
        refs = refs[2:]
    if extra:
        small_ref = refs.pop(0)
    keep_ref, send_ref, stage_ref, stage_sem = refs[:4]
    refs = refs[4:]
    if other:
        second_ref, second_sem = refs[:2]
        refs = refs[2:]
    if extra:
        extra_ref, extra_sem = refs
    step = pl.program_id(0)
    steps = 3 * each + other
    _, shards, rows, tn = stage_ref.shape
    half = shards // 2
    slot = lax.rem(step, 2)

    def copies(slot, step):
        high = pl.ds(pl.multiple_of(lax.div(step, each) * rows, rows), rows)
        cols = pl.ds(pl.multiple_of(lax.rem(step, each) * tn, tn), tn)
        return [pltpu.make_async_copy(stage_ref.at[slot, pl.ds(k * half, half)], out.at[:, high, cols], stage_sem.at[slot, k]) for k, out in enumerate((keep_ref, send_ref))]

    if extra:
        behind = [pltpu.make_async_copy(extra_ref.at[pl.ds(k * half, half)], out.at[:, pl.ds(3 * rows, extra), :], extra_sem.at[k]) for k, out in enumerate((keep_ref, send_ref))]
    if other:
        second = pltpu.make_async_copy(second_in, second_ref, second_sem.at[0])

    @pl.when(step == 0)
    def _():
        if other:
            second.start()
        if extra:
            for i in range(shards):
                extra_ref[pos_ref[i]] = jnp.broadcast_to(small_ref[i:i + 1, :], extra_ref.shape[1:]).astype(bf16)
            for c in behind:
                c.start()

    @pl.when(step >= 2)
    def _():
        for c in copies(slot, step - 2):
            c.wait()

    def put(value):
        for i in range(shards):
            stage_ref[slot, pos_ref[i]] = value[i * rows:(i + 1) * rows].astype(bf16)

    if other:
        @pl.when(step == 3 * each)
        def _():
            second.wait()

        @pl.when(step >= 3 * each)
        def _():
            put(dot_tn(second_ref[...], low_ref[...]))

        @pl.when(step < 3 * each)
        def _():
            put(dot_tn(left_ref[...], d_ref[0]))
    else:
        put(dot_tn(left_ref[...], d_ref[0]))
    for c in copies(slot, step):
        c.start()

    @pl.when(step == steps - 1)
    def _():
        for c in copies(1 - slot, step - 1) + copies(slot, step) + (behind if extra else []):
            c.wait()

def weight_grad(pos, left, d, second=None, low=None, small=None, tn=512):
    R, D = left.shape
    _, _, width = d.shape
    shards = pos.shape[0]
    rows = D // shards
    each = width // tn
    other = D // tn if second is not None else 0
    extra = min(rows, 16) if small is not None else 0
    high = (3 * each + other) // each * rows + extra
    half = jax.ShapeDtypeStruct((shards // 2, high, width), bf16)
    hbm = pl.BlockSpec(memory_space=pl.ANY)
    specs = [pl.BlockSpec(memory_space=pltpu.SMEM), pl.BlockSpec((R, D), lambda j: (0, 0)),
             pl.BlockSpec((1, R, tn), lambda j: (jnp.minimum(lax.div(j, each), 2), 0, jnp.where(j < 3 * each, lax.rem(j, each), each - 1)))]
    args = [pos, left, d]
    scratch = [pltpu.VMEM((2, shards, rows, tn), bf16), pltpu.SemaphoreType.DMA((2, 2))]
    if other:
        specs = specs + [pl.BlockSpec((R, tn), lambda j: (0, jnp.maximum(j - 3 * each, 0))), hbm]
        args = args + [low, second]
        scratch = scratch + [pltpu.VMEM((R, D), bf16), pltpu.SemaphoreType.DMA((1,))]
    if extra:
        specs = specs + [pl.BlockSpec((shards, width), lambda j: (0, 0))]
        args = args + [small]
        scratch = scratch + [pltpu.VMEM((shards, extra, width), bf16), pltpu.SemaphoreType.DMA((2,))]
    return pl.pallas_call(
        functools.partial(weight_grad_kernel, each=each, other=other, extra=extra), grid=(3 * each + other,),
        in_specs=specs, out_specs=[hbm, hbm], out_shape=[half, half], scratch_shapes=scratch,
        compiler_params=cp(), name="weight_grad", cost_estimate=HINT,
    )(*args)

def cotangent_kernel(order_ref, d_ref, *refs, count, final, tm):
    pieces, refs = refs[:count], refs[count:]
    step = pl.program_id(0)
    if final:
        stat_ref, vec_ref, earlier_in, tokens_in, low_in, out_ref, small_ref, weight_ref, acc_ref, earlier_ref, tokens_ref, low_ref, result_ref, in_sem, out_sem = refs
        loads = [pltpu.make_async_copy(a, b, in_sem.at[k]) for k, (a, b) in enumerate(((earlier_in, earlier_ref), (tokens_in, tokens_ref), (low_in, low_ref)))]
        @pl.when(step == 0)
        def _():
            for c in loads:
                c.start()
    else:
        out_ref, weight_ref, acc_ref = refs
    in_order(order_ref, pieces, weight_ref)
    term = dot_nt(d_ref[0], weight_ref[...])
    @pl.when(step == 0)
    def _():
        acc_ref[...] = term
    @pl.when(step > 0)
    def _():
        acc_ref[...] += term

    @pl.when(step == 2)
    def _():
        if not final:
            out_ref[...] = acc_ref[...].astype(bf16)
        else:
            for c in loads:
                c.wait()
            small_ref[...] = jnp.zeros_like(small_ref)
            gain = row_of(vec_ref, GAIN1)
            stores = []
            for i in range(acc_ref.shape[0] // tm):
                at = slice(i * tm, (i + 1) * tm)
                dn = acc_ref[at] + earlier_ref[at].astype(f32)
                r = stat_ref[at, 1:2]
                nhat = (tokens_ref[at].astype(f32) - stat_ref[at, 0:1]) * r
                e = dn * gain
                d = low_ref[at].astype(f32) + r * (e - jnp.mean(e, axis=-1, keepdims=True) - nhat * jnp.mean(e * nhat, axis=-1, keepdims=True))
                result_ref[at] = d.astype(bf16)
                small_ref[0:1, :] += jnp.sum(dn * nhat, axis=0, keepdims=True)
                small_ref[1:2, :] += jnp.sum(dn, axis=0, keepdims=True)
                c = pltpu.make_async_copy(result_ref.at[pl.ds(i * tm, tm)], out_ref.at[pl.ds(i * tm, tm)], out_sem.at[i])
                c.start()
                stores.append(c)
            for c in stores:
                c.wait()

def cotangent(order, d, pieces, number, earlier=None, stats=None, vecs=None, tokens=None, low=None, tm=256):
    _, R, width = d.shape
    n, rows, _ = pieces[0].shape
    D = rows * n * len(pieces)
    per = D // width
    final = earlier is not None
    hbm = pl.BlockSpec(memory_space=pl.ANY)
    specs = [pl.BlockSpec(memory_space=pltpu.SMEM), pl.BlockSpec((1, R, width), lambda j: (j, 0, 0))]
    specs = specs + [pl.BlockSpec((n, rows, width), lambda j: (0, 0, j * per + number))] * len(pieces)
    scratch = [pltpu.VMEM((D, width), bf16), pltpu.VMEM((R, D), f32)]
    result = jax.ShapeDtypeStruct((R, D), bf16)
    more = ()
    if final:
        specs = specs + [pl.BlockSpec((R, 128), lambda j: (0, 0)), pl.BlockSpec(vecs.shape, lambda j: (0, 0)), hbm, hbm, hbm]
        more = (stats, vecs, earlier, tokens, low)
        outs, shapes = [hbm, pl.BlockSpec((8, D), lambda j: (0, 0))], [result, jax.ShapeDtypeStruct((8, D), f32)]
        scratch = scratch + [pltpu.VMEM((R, D), bf16)] * 4 + [pltpu.SemaphoreType.DMA((3,)), pltpu.SemaphoreType.DMA((R // tm,))]
    else:
        outs, shapes = pl.BlockSpec((R, D), lambda j: (0, 0)), result
    return pl.pallas_call(
        functools.partial(cotangent_kernel, count=len(pieces), final=final, tm=tm), grid=(3,),
        in_specs=specs, out_specs=outs, out_shape=shapes, scratch_shapes=scratch,
        compiler_params=cp(), name="cotangent", cost_estimate=HINT,
    )(order, d, *pieces, *more)

def owned_kernel(*refs, counts, rows, blocks, wide):
    parts, at = [], 0
    for c in counts:
        parts.append(sum(r[0].astype(f32) for r in refs[at:at + c]))
        at += c
    up_ref, down_ref = refs[at:]
    half = blocks // len(counts)
    D = down_ref.shape[1]
    for h, part in enumerate(parts):
        for b in range(half):
            down_ref[(h * half + b) * rows:(h * half + b + 1) * rows, :] = part[:, (half + b) * D:(half + b + 1) * D]
    per = D // rows
    group = blocks * rows
    lane = lax.broadcasted_iota(jnp.int32, (rows, 128), 1)
    for tile in range(blocks * D // 128):
        value = None
        for k in range(128 // rows):
            unit = (tile * 128 + k * rows) // rows
            shard, b = unit // blocks, unit % blocks
            source = (b % half) * D + shard * rows
            piece = parts[b // half][:, source // 128 * 128:source // 128 * 128 + 128]
            shift = (k * rows - source % 128) % 128
            if shift:
                piece = pltpu.roll(piece, shift, 1)
            value = piece if value is None else jnp.where(lane >= k * rows, piece, value)
        up_ref[:, tile * 128:(tile + 1) * 128] = value

def owned(groups, D, blocks):
    _, rows, width = groups[0][0].shape
    terms = [t for g in groups for t in g]
    return pl.pallas_call(
        functools.partial(owned_kernel, counts=[len(g) for g in groups], rows=rows, blocks=blocks, wide=width), grid=(1,),
        in_specs=[pl.BlockSpec((1, rows, width), lambda i: (0, 0, 0))] * len(terms),
        out_specs=[pl.BlockSpec((rows, blocks * D), lambda i: (0, 0)), pl.BlockSpec((blocks * rows, D), lambda i: (0, 0))],
        out_shape=[jax.ShapeDtypeStruct((rows, blocks * D), f32), jax.ShapeDtypeStruct((blocks * rows, D), f32)],
        compiler_params=cp(), name="owned", cost_estimate=HINT,
    )(*terms)


class Plan:
    def __init__(self, dp, fsdp):
        self.total = dp * fsdp
        bits = self.total.bit_length() - 1
        low = fsdp.bit_length() - 1
        if fsdp == 4:
            self.core, z, rest = low, list(range(low)), list(range(low + 1, bits))
        else:
            self.core, z, rest = 0, list(range(1, low)), list(range(low, bits))
        a, b = rest[:len(rest) // 2], rest[len(rest) // 2:]
        self.stages = [(a, b), (b, a), (z, z)]
        self.third = len(z) == low

    def masks(self, stage, core):
        bits = self.stages[stage][core]
        return [sum(1 << b for k, b in enumerate(bits) if j >> k & 1) for j in range(1 << len(bits))]

    def pairs(self, stage, j):
        return [(i, i ^ self.masks(stage, i >> self.core & 1)[j]) for i in range(self.total)]

    def size(self, stage):
        return 1 << len(self.stages[stage][0])

    def places(self, me, fixed=False):
        shard = lax.iota(jnp.int32, self.total)
        rel = shard ^ me
        core = (shard >> self.core) & 1
        pos = (rel >> self.core) & 1
        for k, (a, b) in enumerate(self.stages):
            pick = lambda bits, v: sum((((v >> bit) & 1) << k) for k, bit in enumerate(bits))
            own = pick(a, shard) if fixed and k == 2 else jnp.where(core == 0, pick(a, rel), pick(b, rel))
            pos = (pos << len(a)) + own
        return pos

AXES = ("dp", "fsdp")

def swap_core(plan, x):
    return lax.ppermute(x, AXES, [(i, i ^ (1 << plan.core)) for i in range(plan.total)])

def exchange(plan, x, stage, j):
    return lax.ppermute(x, AXES, plan.pairs(stage, j))

class Gathering:
    def __init__(self, plan, shard):
        self.plan, self.shard = plan, shard
        self.arrays = [exchange(plan, shard, 2, j) for j in range(1, plan.size(2))]

    def spread(self):
        column = jnp.stack([self.shard] + self.arrays)
        self.near = [exchange(self.plan, column, 1, j) for j in range(1, self.plan.size(1))]
        self.far = [exchange(self.plan, column, 0, j) for j in range(1, self.plan.size(0))]
        self.arrays = [column] + self.near + self.far

    def spread_again(self):
        n = self.plan.size(1)
        near, far = self.arrays[:n], self.arrays[n:]
        rest = [[exchange(self.plan, p, 0, j + 1) for p in near[1:]] for j in range(len(far))]
        other = [swap_core(self.plan, p) for p in self.arrays]
        self.first, self.other, self.arrays = self.arrays, other, [p for row in rest for p in row]

    def finish(self):
        n = self.plan.size(1)
        sides = (self.first, self.arrays), (self.other, [swap_core(self.plan, p) for p in self.arrays])
        pieces = []
        for first, rest in sides:
            pieces += first[:n]
            for j in range(self.plan.size(0) - 1):
                pieces += [first[n + j]] + rest[j * (n - 1):(j + 1) * (n - 1)]
        return pieces

def step(x, after, *reductions):
    x, _ = tie(x, after, *reductions)
    reductions = [r for r in reductions if r.stage < 3]
    if reductions:
        for r in reductions:
            r.add()
        x, = tie(x, *reductions)
        for r in reductions:
            r.go()
    return x

class Reduction:
    def __init__(self, plan, keep, send, one=False):
        self.plan, self.stage, self.size, self.one = plan, 0, keep.shape[0], one and plan.third
        self.terms = [keep, swap_core(plan, send)]
        self.sent = []

    def add(self):
        n = self.plan.size(self.stage)
        part = self.size // n
        if self.one and self.stage == 2:
            self.sent = [sum(t[:n].astype(f32) for t in self.terms).astype(self.terms[0].dtype)]
            return
        self.sent = [sum(t[j * part:(j + 1) * part].astype(f32) for t in self.terms).astype(self.terms[0].dtype) for j in range(1, n)]

    def go(self):
        if self.one and self.stage == 2:
            self.terms = [lax.psum_scatter(self.sent[0], AXES[1], scatter_dimension=0, tiled=False)[None]]
        else:
            self.terms = self.terms + [exchange(self.plan, s, self.stage, j + 1) for j, s in enumerate(self.sent)]
        self.sent = []
        self.size //= self.plan.size(self.stage)
        self.stage += 1

    def finish(self):
        while self.stage < 3:
            self.add()
            self.go()
        return sum(t[0].astype(f32) for t in self.terms)

def tie(*trees):
    flat = []
    for t in trees:
        flat += t.terms + t.sent if isinstance(t, Reduction) else t.arrays if isinstance(t, Gathering) else [t]
    flat = list(lax.optimization_barrier(tuple(flat)))
    out = []
    for t in trees:
        if isinstance(t, Reduction):
            t.terms = [flat.pop(0) for _ in t.terms]
            t.sent = [flat.pop(0) for _ in t.sent]
        elif isinstance(t, Gathering):
            t.arrays = [flat.pop(0) for _ in t.arrays]
        else:
            out.append(flat.pop(0))
    return out

def body(plan, tokens, prefix_len, padding_len, first_gain, first_shift, inproj_weight, query_bias, value_bias,
         outproj_weight, outproj_bias, second_gain, second_shift, up_weight, up_bias, down_weight, down_bias, grad_out):
    total = plan.total
    R, D = tokens.shape
    F = up_weight.shape[1]
    rows = D // total
    blocks = F // D
    me = lax.axis_index(AXES)
    pos = plan.places(me)
    pos_one = plan.places(me, plan.third)
    shard = lax.iota(jnp.int32, total)
    order = jnp.sum(jnp.where(pos[None, :] == shard[:, None], shard[None, :], 0), axis=1)
    n = first_gain.shape[0]
    half = blocks // 2
    up_local = up_weight.reshape(rows, total, blocks, rows).transpose(0, 2, 1, 3).reshape(rows, F)
    down_local = [down_weight[b * rows:(b + 1) * rows] for b in range(blocks)]
    small = jnp.concatenate([first_gain, first_shift, query_bias, value_bias, outproj_bias, second_gain, second_shift, down_bias, up_bias])
    small = jnp.pad(small.reshape(8 + blocks, rows).T, ((0, 0), (0, 128 - 8 - blocks)))
    inward = Gathering(plan, jnp.concatenate([inproj_weight, outproj_weight, small], axis=1))
    wide = lax.all_gather(jnp.concatenate([up_local] + down_local, axis=1), AXES, axis=0, tiled=True)
    stats = norm(tokens)
    stats, = tie(stats, inward)
    inward.spread()
    stats, = tie(stats, inward)
    inward.spread_again()
    stats, *inward.other = tie(stats, *inward.other, inward)
    inward = inward.finish()
    n1, qkv, vecs = project(order, tokens, stats, inward)
    ctx, lse = attend(prefix_len, padding_len, qkv)
    resid, n2, w_out = branch(order, ctx, tokens, vecs, inward)
    cut = D // 2
    n_pairs = D // 128
    def back(first, x, earlier=()):
        return attend_back(prefix_len, padding_len, qkv, x, ctx, lse, first, n_pairs // 4, cut, earlier)
    out, low, dctx, keep1, send1, keep2, send2, ubias_grad, mid = ffn(pos_one, n2, grad_out, vecs, wide, resid, w_out)
    g1 = Reduction(plan, keep1, send1, True)
    g2 = Reduction(plan, keep2, send2, True)
    d1 = back(0, dctx)
    dctx = step(dctx, d1[0], g1)
    d1 = back(n_pairs // 4, dctx, d1)
    n1a = step(n1, d1[0], g2)
    g3 = Reduction(plan, *weight_grad(pos, n1a, d1[0], ctx, low))
    dctx, _ = tie(dctx, g3.terms[0])
    d2 = back(n_pairs // 2, dctx)
    dctx = step(dctx, d2[0], g1)
    d2 = back(n_pairs * 3 // 4, dctx, d2)
    n1b = step(n1, d2[0], g2, g1)
    per = lambda v: v.reshape(total, -1)
    att = jnp.concatenate([d1[1], d2[1]], axis=1)
    ubg = ubias_grad.reshape(blocks, total, rows).transpose(1, 0, 2).reshape(total, -1)
    early = jnp.concatenate([per(att[0]), per(att[1]), per(mid[2]), per(mid[0]), per(mid[1]), per(mid[3]), ubg], axis=1)
    early = jnp.pad(early, ((0, 0), (0, cut - early.shape[1])))
    g4 = Reduction(plan, *weight_grad(pos, n1b, d2[0], small=early))
    da = step(d1[0], g4.terms[0], g3, g2)
    part = cotangent(order, da, inward, 0)
    part = step(part, part, g4, g3)
    tokens_grad, end = cotangent(order, d2[0], inward, 1, part, stats, vecs, tokens, low)
    bits = [plan.core] + [bit for bit in range(total.bit_length() - 1) if bit != plan.core]
    swap = lambda v, bit: lax.ppermute(v, AXES, [(i, i ^ (1 << bit)) for i in range(total)])
    end = step(end[:2], end, g4)
    other = swap(end, bits[0])
    end = step(end, end, g3, g1)
    end, other = tie(end, other, g4)
    g4.add()
    g4.go()
    arriving = plan.size(2) - 1
    for k, bit in enumerate(bits[1:]):
        end = end + other
        other = swap(end, bit)
        if k < arriving:
            at = k - arriving
            other, g4.terms[at] = tie(other, g4.terms[at])
        if k == 1:
            other, = tie(other, g3)
    late = lax.dynamic_slice_in_dim(end + other, me * n, n, axis=1)
    in1, in2 = g3.finish(), g4.finish()
    up_grad, down_grad = owned([g1.terms, g2.terms], D, blocks)
    out_grad = jnp.concatenate([in1[3 * rows:4 * rows], in1[4 * rows:]], axis=1)
    in_grad = jnp.concatenate([g[k * rows:(k + 1) * rows] for k in range(3) for g in (in1, in2)], axis=1)
    early = in2[3 * rows]
    e = [early[i * n:(i + 1) * n] for i in range(6)]
    return (out, tokens_grad, late[0], late[1], in_grad, e[0], e[1], out_grad, e[2], e[3], e[4], up_grad, early[6 * n:6 * n + F // total], down_grad, e[5])

def solution(mesh):
    plan = Plan(mesh.shape["dp"], mesh.shape["fsdp"])
    rows, flat = P(AXES, None), P(AXES)
    ins = (rows, flat, flat, flat, flat, rows, flat, flat, rows, flat, flat, flat, rows, flat, rows, flat, rows)
    outs = (rows, rows, flat, flat, rows, flat, flat, rows, flat, flat, flat, rows, flat, rows, flat)
    return jax.shard_map(functools.partial(body, plan), mesh=mesh, in_specs=ins, out_specs=outs, check_vma=False)
```

```python
import functools, math
import jax, jax.numpy as jnp
from jax import lax
from jax.sharding import PartitionSpec as P
from jax.experimental import pallas as pl
from jax.experimental.pallas import tpu as pltpu
HEADS=16
EPSILON = 1e-05
NEGATIVE = -1000000000.0
bf16=jnp.bfloat16; f32=jnp.float32
VMEM_LIMIT=60*1024*1024
HINT=pl.CostEstimate(flops=1000, bytes_accessed=1000, transcendentals=0)
def cp(n=1): return pltpu.CompilerParams(dimension_semantics=("arbitrary",)*n, vmem_limit_bytes=VMEM_LIMIT)
def dot(a,b): return lax.dot_general(a,b,(((1,),(0,)),((),())),preferred_element_type=f32)
def dot_nt(a,b): return lax.dot_general(a,b,(((1,),(1,)),((),())),preferred_element_type=f32)
def dot_tn(a,b): return lax.dot_general(a,b,(((0,),(0,)),((),())),preferred_element_type=f32)

GAIN1, SHIFT1, QBIAS, VBIAS, OBIAS, GAIN2, SHIFT2, DBIAS, UBIAS = range(9)

def row_of(ref, k):
    return ref[k:k + 1, :]

def norm_kernel(tokens_ref, out_ref):
    x = tokens_ref[...].astype(f32)
    mean = jnp.mean(x, axis=-1, keepdims=True)
    center = x - mean
    r = lax.rsqrt(jnp.mean(center * center, axis=-1, keepdims=True) + EPSILON)
    lane = lax.broadcasted_iota(jnp.int32, out_ref.shape, 1)
    out_ref[...] = jnp.where(lane == 0, mean, r)

def norm(tokens, tm=256):
    R, D = tokens.shape
    return pl.pallas_call(
        norm_kernel, grid=(R // tm,), in_specs=[pl.BlockSpec((tm, D), lambda i: (i, 0))], out_specs=pl.BlockSpec((tm, 128), lambda i: (i, 0)),
        out_shape=jax.ShapeDtypeStruct((R, 128), f32), compiler_params=cp(), name="norm", cost_estimate=HINT,
    )(tokens)

def in_order(order_ref, pieces, whole_ref):
    n, rows, _ = pieces[0].shape
    for p, piece in enumerate(pieces):
        for i in range(n):
            whole_ref[pl.ds(pl.multiple_of(order_ref[p * n + i] * rows, rows), rows), :] = piece[i]

def project_kernel(order_ref, tokens_ref, stat_ref, *refs, count):
    pieces, sides = refs[:count], refs[count:2 * count]
    normed_ref, out_ref, vec_ref, weight_ref, side_ref, all_ref = refs[2 * count:]
    step = pl.program_id(0)
    @pl.when(step == 0)
    def _():
        in_order(order_ref, sides, side_ref)
        all_ref[...] = jnp.transpose(side_ref[...].astype(f32))
        vec_ref[...] = all_ref[:16, :]
        xhat = (tokens_ref[...].astype(f32) - stat_ref[:, 0:1]) * stat_ref[:, 1:2]
        normed_ref[...] = (xhat * all_ref[GAIN1:GAIN1 + 1, :] + all_ref[SHIFT1:SHIFT1 + 1, :]).astype(bf16)
    in_order(order_ref, pieces, weight_ref)
    D = normed_ref.shape[1]
    tn = out_ref.shape[1]
    third = pl.num_programs(0) // 3
    at = pl.ds(pl.multiple_of(lax.rem(step, D // tn) * tn, tn), tn)
    bias = jnp.where(step < third, all_ref[QBIAS:QBIAS + 1, at], jnp.where(step < 2 * third, 0.0, all_ref[VBIAS:VBIAS + 1, at]))
    factor = jnp.where(step < third, 0.125, 1.0)
    out = dot(normed_ref[...], weight_ref[...]) + bias
    out_ref[...] = (out * factor).astype(bf16)

def project(order, tokens, stats, pieces, tn=512):
    R, D = tokens.shape
    n, rows, width = pieces[0].shape
    N = 3 * D
    full = pl.BlockSpec((R, D), lambda j: (0, 0))
    return pl.pallas_call(
        functools.partial(project_kernel, count=len(pieces)), grid=(N // tn,),
        in_specs=[pl.BlockSpec(memory_space=pltpu.SMEM), full, pl.BlockSpec((R, 128), lambda j: (0, 0))]
        + [pl.BlockSpec((n, rows, tn), lambda j: (0, 0, j))] * len(pieces)
        + [pl.BlockSpec((n, rows, 128), lambda j: (0, 0, width // 128 - 1))] * len(pieces),
        out_specs=[full, pl.BlockSpec((R, tn), lambda j: (0, j)), pl.BlockSpec((16, D), lambda j: (0, 0))],
        out_shape=[jax.ShapeDtypeStruct((R, D), bf16), jax.ShapeDtypeStruct((R, N), bf16), jax.ShapeDtypeStruct((16, D), f32)],
        scratch_shapes=[pltpu.VMEM((D, tn), bf16), pltpu.VMEM((D, 128), bf16), pltpu.VMEM((128, D), f32)],
        compiler_params=cp(), name="project", cost_estimate=HINT,
    )(order, tokens, stats, *pieces, *pieces)

def key_bias(prefix, limit, lo, q0, bq, transposed, diagonal):
    shape = (bq, bq)
    kd = 0 if transposed else 1
    k = lo + lax.broadcasted_iota(jnp.int32, shape, kd)
    ok = k < limit
    if diagonal:
        q = q0 + lax.broadcasted_iota(jnp.int32, shape, 1 - kd)
        ok = ok & ((k < prefix) | (k <= q))
    return jnp.where(ok, 0.0, NEGATIVE)

def attend_kernel(prefix_ref, padding_ref, q_ref, k_ref, v_ref, out_ref, lse_ref, bias_ref, *, bq):
    L = q_ref.shape[0]
    step = pl.program_id(0)
    prefix = prefix_ref[0]
    limit = L - padding_ref[0]
    n = L // bq
    lane = lax.broadcasted_iota(jnp.int32, (1, 128), 1)
    @pl.when(step == 0)
    def _():
        for b in range(n):
            bias_ref[b] = key_bias(prefix, limit, b * bq, b * bq, bq, True, True)
    vT = jnp.transpose(v_ref[...])
    ones = jnp.ones((16, L), bf16)
    values = [jnp.concatenate([vT[64 * h:64 * h + 64], ones], axis=0) for h in range(2)]
    for b in range(n):
        start, stop = b * bq, (b + 1) * bq
        q = q_ref[start:stop, :]
        both = jnp.concatenate([jnp.where(lane < 64, q, 0), jnp.where(lane >= 64, q, 0)], axis=0).astype(bf16)
        s = []
        for kb in range(b + 1):
            t = dot_nt(k_ref[kb * bq:(kb + 1) * bq, :], both)
            if kb == b:
                t = t + jnp.concatenate([bias_ref[b], bias_ref[b]], axis=1)
            elif (kb + 1) * bq > L - 384:
                kk = kb * bq + lax.broadcasted_iota(jnp.int32, (bq, 1), 0)
                t = t + jnp.where(kk < limit, 0.0, NEGATIVE)
            s.append(t)
        m = functools.reduce(jnp.maximum, [jnp.max(t, axis=0, keepdims=True) for t in s])
        acc = [None, None]
        for kb in range(b + 1):
            e = jnp.exp(s[kb] - m).astype(bf16)
            for h in range(2):
                t = dot(values[h][:, kb * bq:(kb + 1) * bq], e[:, h * bq:(h + 1) * bq])
                acc[h] = t if acc[h] is None else acc[h] + t
        ctx = [a[:64] * (1.0 / a[64:65]) for a in acc]
        out_ref[start:stop, :] = jnp.transpose(jnp.concatenate(ctx, axis=0)).astype(bf16)
        for h in range(2):
            lse_ref[pl.ds(2 * step + h, 1), start:stop] = m[:, h * bq:(h + 1) * bq] + jnp.log(acc[h][64:65])

def attend(prefix, padding, qkv, bq=256):
    L = qkv.shape[0]
    D = qkv.shape[1] // 3
    n = D // 128
    smem = pl.BlockSpec(memory_space=pltpu.SMEM)
    col = lambda off: pl.BlockSpec((L, 128), lambda j: (0, j + off))
    return pl.pallas_call(
        functools.partial(attend_kernel, bq=bq), grid=(n,),
        in_specs=[smem, smem, col(0), col(n), col(2 * n)],
        out_specs=[col(0), pl.BlockSpec((2 * n, L), lambda j: (0, 0))],
        out_shape=[jax.ShapeDtypeStruct((L, D), bf16), jax.ShapeDtypeStruct((2 * n, L), f32)],
        scratch_shapes=[pltpu.VMEM((L // bq, bq, bq), f32)],
        compiler_params=cp(), name="attend",
        cost_estimate=HINT,
    )(prefix, padding, qkv, qkv, qkv)

def branch_kernel(order_ref, ctx_ref, tokens_ref, vec_ref, *refs):
    *pieces, resid_ref, normed_ref, weight_ref = refs
    @pl.when(pl.program_id(0) == 0)
    def _():
        in_order(order_ref, pieces, weight_ref)
    resid = tokens_ref[...].astype(f32) + (dot(ctx_ref[...], weight_ref[...]) + row_of(vec_ref, OBIAS))
    center = resid - jnp.mean(resid, axis=-1, keepdims=True)
    spread = jnp.mean(center * center, axis=-1, keepdims=True)
    normed = center * lax.rsqrt(spread + EPSILON) * row_of(vec_ref, GAIN2) + row_of(vec_ref, SHIFT2)
    resid_ref[...] = resid
    normed_ref[...] = normed.astype(bf16)

def branch(order, ctx, tokens, vecs, pieces, tm=256):
    R, D = ctx.shape
    n, high, _ = pieces[0].shape
    rows = pl.BlockSpec((tm, D), lambda i: (i, 0))
    return pl.pallas_call(
        branch_kernel, grid=(R // tm,),
        in_specs=[pl.BlockSpec(memory_space=pltpu.SMEM), rows, rows, pl.BlockSpec(vecs.shape, lambda i: (0, 0))]
        + [pl.BlockSpec((n, high, D), lambda i: (0, 0, 3))] * len(pieces),
        out_specs=[rows, rows, pl.BlockSpec((D, D), lambda i: (0, 0))],
        out_shape=[jax.ShapeDtypeStruct((R, D), f32), jax.ShapeDtypeStruct((R, D), bf16), jax.ShapeDtypeStruct((D, D), bf16)],
        compiler_params=cp(), name="branch", cost_estimate=HINT,
    )(order, ctx, tokens, vecs, *pieces)

def ffn_kernel(pos_ref, normed_ref, grad_ref, vec_ref, rows_ref, up_ref, down_ref, resid_in, weight_in,
               result_out, low_out, dctx_out, keep1_ref, send1_ref, keep2_ref, send2_ref, biasg_ref, small_ref,
               out_ref, dn_ref, ups_ref, dns_ref, resid_ref, weight_ref, result_ref, low_ref, dctx_ref, up_sem, dn_sem, in_sem, out_sem, *, shards, per, blocks, tm):
    step = pl.program_id(0)
    last = pl.num_programs(0) - 1
    D = normed_ref.shape[1]
    tf = ups_ref.shape[3]
    half = shards // 2
    rows = D // shards
    each = blocks // 2
    slot = lax.rem(step, 2)
    block = lax.div(step, per)
    bslot = lax.rem(block, 2)
    groups = ((keep1_ref, send1_ref), (keep2_ref, send2_ref))

    def up_copies(slot, step, group):
        cols = pl.ds(pl.multiple_of(step * tf - group * each * D, tf), tf)
        return [pltpu.make_async_copy(ups_ref.at[slot, pl.ds(k * half, half)], groups[group][k].at[:, :, cols], up_sem.at[slot, k]) for k in range(2)]

    def down_copies(bslot, block, group):
        cols = pl.ds(pl.multiple_of((each + block - group * each) * D, D), D)
        return [pltpu.make_async_copy(dns_ref.at[bslot, pl.ds(k * half, half)], groups[group][k].at[:, :, cols], dn_sem.at[bslot, k]) for k in range(2)]

    def each_group(block, do):
        for group in range(2):
            pl.when((block >= group * each) & (block < (group + 1) * each))(functools.partial(do, group))

    def start_up(group):
        for c in up_copies(slot, step, group):
            c.start()

    def wait_up(slot, step):
        def do(group):
            for c in up_copies(slot, step, group):
                c.wait()
        each_group(lax.div(step, per), do)

    def start_down(group):
        for c in down_copies(bslot, block, group):
            c.start()

    def wait_down(bslot, block):
        def do(group):
            for c in down_copies(bslot, block, group):
                c.wait()
        each_group(block, do)

    loads = [pltpu.make_async_copy(resid_in, resid_ref, in_sem.at[0]), pltpu.make_async_copy(weight_in, weight_ref, in_sem.at[1])]

    @pl.when(step == 0)
    def _():
        for c in loads:
            c.start()
        out_ref[...] = jnp.zeros_like(out_ref)
        dn_ref[...] = jnp.zeros_like(dn_ref)

    @pl.when(step >= 2)
    def _():
        wait_up(slot, step - 2)

    @pl.when((step >= 2 * per) & (lax.rem(step, per) == 0))
    def _():
        wait_down(bslot, block - 2)

    n2 = normed_ref[...]
    go = grad_ref[...]
    up = up_ref[...]
    down = down_ref[...]
    bias = row_of(vec_ref, UBIAS)
    for k in range(1, blocks):
        bias = jnp.where(block == k, row_of(vec_ref, UBIAS + k), bias)
    u = dot(n2, up) + bias
    cdf = 0.5 * (1.0 + lax.erf(u * math.sqrt(0.5)))
    a = (u * cdf).astype(bf16)
    slope = cdf + u * (jnp.exp(-0.5 * u * u) * (1.0 / math.sqrt(2 * math.pi)))
    du = (dot_nt(go, down) * slope).astype(bf16)
    out_ref[...] += dot(a, down)
    dn_ref[...] += dot_nt(du, up)
    biasg_ref[...] = jnp.sum(du.astype(f32), axis=0, keepdims=True)
    upg = dot_tn(n2, du).astype(bf16)
    for i in range(shards):
        ups_ref[slot, pos_ref[i]] = upg[i * rows:(i + 1) * rows]
    downg = dot_tn(a, go).astype(bf16)
    here = tf // rows
    at = lax.rem(step, per) * here
    for i in range(here):
        dns_ref[bslot, pos_ref[at + i]] = downg[i * rows:(i + 1) * rows]
    each_group(block, start_up)

    @pl.when(lax.rem(step, per) == per - 1)
    def _():
        each_group(block, start_down)

    @pl.when(step == last)
    def _():
        for c in loads:
            c.wait()
        small_ref[...] = jnp.zeros_like(small_ref)
        stores = []
        for i in range(resid_ref.shape[0] // tm):
            at = slice(i * tm, (i + 1) * tm)
            resid = resid_ref[at]
            result_ref[at] = (resid + out_ref[at] + row_of(rows_ref, DBIAS)).astype(bf16)
            center = resid - jnp.mean(resid, axis=-1, keepdims=True)
            r = lax.rsqrt(jnp.mean(center * center, axis=-1, keepdims=True) + EPSILON)
            nhat = center * r
            dn = dn_ref[at]
            go = grad_ref[at].astype(f32)
            e = dn * row_of(rows_ref, GAIN2)
            low = (go + r * (e - jnp.mean(e, axis=-1, keepdims=True) - nhat * jnp.mean(e * nhat, axis=-1, keepdims=True))).astype(bf16)
            low_ref[at] = low
            dctx_ref[at] = dot_nt(low, weight_ref[...]).astype(bf16)
            small_ref[0:1, :] += jnp.sum(dn * nhat, axis=0, keepdims=True)
            small_ref[1:2, :] += jnp.sum(dn, axis=0, keepdims=True)
            small_ref[2:3, :] += jnp.sum(low.astype(f32), axis=0, keepdims=True)
            small_ref[3:4, :] += jnp.sum(go, axis=0, keepdims=True)
            for k, (here, there) in enumerate(((result_ref, result_out), (low_ref, low_out), (dctx_ref, dctx_out))):
                c = pltpu.make_async_copy(here.at[pl.ds(i * tm, tm)], there.at[pl.ds(i * tm, tm)], out_sem.at[i, k])
                c.start()
                stores.append(c)
        for c in stores + up_copies(1 - slot, step - 1, 1) + up_copies(slot, step, 1) + down_copies(1 - bslot, block - 1, 1) + down_copies(bslot, block, 1):
            c.wait()

def ffn(pos, normed, grad, vecs, wide, resid, weight, tf=512, tm=256):
    R, D = normed.shape
    blocks = wide.shape[1] // D // 2
    F = blocks * D
    shards = pos.shape[0]
    rows = D // shards
    per = D // tf
    full = pl.BlockSpec((R, D), lambda j: (0, 0))
    hbm = pl.BlockSpec(memory_space=pl.ANY)
    part = jax.ShapeDtypeStruct((shards // 2, rows, F), bf16)
    low = jax.ShapeDtypeStruct((R, D), bf16)
    return pl.pallas_call(
        functools.partial(ffn_kernel, shards=shards, per=per, blocks=blocks, tm=tm), grid=(F // tf,),
        in_specs=[pl.BlockSpec(memory_space=pltpu.SMEM), full, full, pl.BlockSpec((16, tf), lambda j: (0, lax.rem(j, per))), pl.BlockSpec((16, D), lambda j: (0, 0)),
                  pl.BlockSpec((D, tf), lambda j: (0, j)), pl.BlockSpec((tf, D), lambda j: (lax.rem(j, per), blocks + lax.div(j, per))), hbm, hbm],
        out_specs=[hbm] * 7 + [pl.BlockSpec((1, tf), lambda j: (0, j)), pl.BlockSpec((8, D), lambda j: (0, 0))],
        out_shape=[low, low, low, part, part, part, part, jax.ShapeDtypeStruct((1, F), f32), jax.ShapeDtypeStruct((8, D), f32)],
        scratch_shapes=[pltpu.VMEM((R, D), f32), pltpu.VMEM((R, D), f32), pltpu.VMEM((2, shards, rows, tf), bf16), pltpu.VMEM((2, shards, rows, D), bf16),
                        pltpu.VMEM((R, D), f32), pltpu.VMEM((D, D), bf16), pltpu.VMEM((R, D), bf16), pltpu.VMEM((R, D), bf16), pltpu.VMEM((R, D), bf16),
                        pltpu.SemaphoreType.DMA((2, 2)), pltpu.SemaphoreType.DMA((2, 2)), pltpu.SemaphoreType.DMA((2,)), pltpu.SemaphoreType.DMA((R // tm, 3))],
        compiler_params=cp(), name="ffn", cost_estimate=HINT,
    )(pos, normed, grad, vecs, vecs, wide, wide, resid, weight)

def attend_back_kernel(prefix_ref, padding_ref, q_ref, k_ref, v_ref, do_ref, o_ref, lse_ref, *refs, bq, first):
    d_ref, small_ref, dka_ref, dva_ref, bias_ref = refs[-5:]
    L = q_ref.shape[0]
    step = pl.program_id(0) + first
    prefix = prefix_ref[0]
    limit = L - padding_ref[0]
    n = L // bq
    lane = lax.broadcasted_iota(jnp.int32, (1, 128), 1)
    @pl.when(pl.program_id(0) == 0)
    def _():
        for b in range(n):
            bias_ref[b] = key_bias(prefix, limit, b * bq, b * bq, bq, True, True)
    kT = jnp.transpose(k_ref[...])
    prod = do_ref[...].astype(f32) * o_ref[...].astype(f32)
    row = lax.broadcasted_iota(jnp.int32, (8, 128), 0)
    col = lax.broadcasted_iota(jnp.int32, (8, 128), 1)
    pick = jnp.where((col // 64) == row, 1.0, 0.0)
    delta = lax.dot_general(pick, prod, (((1,), (1,)), ((), ())), precision=lax.Precision.HIGHEST, preferred_element_type=f32)
    for b in range(n):
        start, stop = b * bq, (b + 1) * bq
        q = q_ref[start:stop, :]
        do = do_ref[start:stop, :]
        both = jnp.concatenate([jnp.where(lane < 64, q, 0), jnp.where(lane >= 64, q, 0)], axis=0).astype(bf16)
        dboth = jnp.concatenate([jnp.where(lane < 64, do, 0), jnp.where(lane >= 64, do, 0)], axis=0).astype(bf16)
        lse = jnp.concatenate([lse_ref[pl.ds(2 * step, 1), start:stop], lse_ref[pl.ds(2 * step + 1, 1), start:stop]], axis=1)
        inner = jnp.concatenate([delta[0:1, start:stop], delta[1:2, start:stop]], axis=1)
        dq = [None, None]
        for kb in range(b + 1):
            ks = slice(kb * bq, (kb + 1) * bq)
            s = dot_nt(k_ref[ks, :], both)
            if kb == b:
                s = s + jnp.concatenate([bias_ref[b], bias_ref[b]], axis=1)
            elif (kb + 1) * bq > L - 384:
                kk = kb * bq + lax.broadcasted_iota(jnp.int32, (bq, 1), 0)
                s = s + jnp.where(kk < limit, 0.0, NEGATIVE)
            p = jnp.exp(s - lse)
            ds = (p * (dot_nt(v_ref[ks, :], dboth) - inner)).astype(bf16)
            tv = dot(p.astype(bf16), dboth)
            tk = dot(ds, both)
            if kb == b:
                dva_ref[ks, :] = tv
                dka_ref[ks, :] = tk
            else:
                dva_ref[ks, :] += tv
                dka_ref[ks, :] += tk
            for h in range(2):
                t = dot(kT[64 * h:64 * h + 64, ks], ds[:, h * bq:(h + 1) * bq])
                dq[h] = t if dq[h] is None else dq[h] + t
        d_ref[0, start:stop, :] = (jnp.transpose(jnp.concatenate(dq, axis=0)) * 0.125).astype(bf16)
    d_ref[1] = dka_ref[...].astype(bf16)
    d_ref[2] = dva_ref[...].astype(bf16)
    small_ref[0:1, :] = jnp.sum(d_ref[0].astype(f32), axis=0, keepdims=True)
    small_ref[1:2, :] = jnp.sum(d_ref[2].astype(f32), axis=0, keepdims=True)

def attend_back(prefix, padding, qkv, dctx, ctx, lse, first, count, width, earlier=(), bq=256):
    L = qkv.shape[0]
    D = dctx.shape[1]
    n = D // 128
    at = first % (width // 128)
    smem = pl.BlockSpec(memory_space=pltpu.SMEM)
    col = lambda off: pl.BlockSpec((L, 128), lambda j: (0, j + off))
    return pl.pallas_call(
        functools.partial(attend_back_kernel, bq=bq, first=first), grid=(count,),
        in_specs=[smem, smem, col(first), col(n + first), col(2 * n + first), col(first), col(first), pl.BlockSpec((2 * n, L), lambda j: (0, 0))]
        + [pl.BlockSpec(memory_space=pl.ANY)] * len(earlier),
        out_specs=[pl.BlockSpec((3, L, 128), lambda j: (0, 0, j + at)), pl.BlockSpec((8, 128), lambda j: (0, j + at))],
        out_shape=[jax.ShapeDtypeStruct((3, L, width), bf16), jax.ShapeDtypeStruct((8, width), f32)],
        scratch_shapes=[pltpu.VMEM((L, 128), f32), pltpu.VMEM((L, 128), f32), pltpu.VMEM((L // bq, bq, bq), f32)],
        input_output_aliases={8 + i: i for i in range(len(earlier))},
        compiler_params=cp(), name="attend_back",
        cost_estimate=HINT,
    )(prefix, padding, qkv, qkv, qkv, dctx, ctx, lse, *earlier)

def weight_grad_kernel(pos_ref, left_ref, d_ref, *refs, each, other, extra):
    refs = list(refs)
    if other:
        low_ref, second_in = refs[:2]
        refs = refs[2:]
    if extra:
        small_ref = refs.pop(0)
    keep_ref, send_ref, stage_ref, stage_sem = refs[:4]
    refs = refs[4:]
    if other:
        second_ref, second_sem = refs[:2]
        refs = refs[2:]
    if extra:
        extra_ref, extra_sem = refs
    step = pl.program_id(0)
    steps = 3 * each + other
    _, shards, rows, tn = stage_ref.shape
    half = shards // 2
    slot = lax.rem(step, 2)

    def copies(slot, step):
        high = pl.ds(pl.multiple_of(lax.div(step, each) * rows, rows), rows)
        cols = pl.ds(pl.multiple_of(lax.rem(step, each) * tn, tn), tn)
        return [pltpu.make_async_copy(stage_ref.at[slot, pl.ds(k * half, half)], out.at[:, high, cols], stage_sem.at[slot, k]) for k, out in enumerate((keep_ref, send_ref))]

    if extra:
        behind = [pltpu.make_async_copy(extra_ref.at[pl.ds(k * half, half)], out.at[:, pl.ds(3 * rows, extra), :], extra_sem.at[k]) for k, out in enumerate((keep_ref, send_ref))]
    if other:
        second = pltpu.make_async_copy(second_in, second_ref, second_sem.at[0])

    @pl.when(step == 0)
    def _():
        if other:
            second.start()
        if extra:
            for i in range(shards):
                extra_ref[pos_ref[i]] = jnp.broadcast_to(small_ref[i:i + 1, :], extra_ref.shape[1:]).astype(bf16)
            for c in behind:
                c.start()

    @pl.when(step >= 2)
    def _():
        for c in copies(slot, step - 2):
            c.wait()

    def put(value):
        for i in range(shards):
            stage_ref[slot, pos_ref[i]] = value[i * rows:(i + 1) * rows].astype(bf16)

    if other:
        @pl.when(step == 3 * each)
        def _():
            second.wait()

        @pl.when(step >= 3 * each)
        def _():
            put(dot_tn(second_ref[...], low_ref[...]))

        @pl.when(step < 3 * each)
        def _():
            put(dot_tn(left_ref[...], d_ref[0]))
    else:
        put(dot_tn(left_ref[...], d_ref[0]))
    for c in copies(slot, step):
        c.start()

    @pl.when(step == steps - 1)
    def _():
        for c in copies(1 - slot, step - 1) + copies(slot, step) + (behind if extra else []):
            c.wait()

def weight_grad(pos, left, d, second=None, low=None, small=None, tn=512):
    R, D = left.shape
    _, _, width = d.shape
    shards = pos.shape[0]
    rows = D // shards
    each = width // tn
    other = D // tn if second is not None else 0
    extra = min(rows, 16) if small is not None else 0
    high = (3 * each + other) // each * rows + extra
    half = jax.ShapeDtypeStruct((shards // 2, high, width), bf16)
    hbm = pl.BlockSpec(memory_space=pl.ANY)
    specs = [pl.BlockSpec(memory_space=pltpu.SMEM), pl.BlockSpec((R, D), lambda j: (0, 0)),
             pl.BlockSpec((1, R, tn), lambda j: (jnp.minimum(lax.div(j, each), 2), 0, jnp.where(j < 3 * each, lax.rem(j, each), each - 1)))]
    args = [pos, left, d]
    scratch = [pltpu.VMEM((2, shards, rows, tn), bf16), pltpu.SemaphoreType.DMA((2, 2))]
    if other:
        specs = specs + [pl.BlockSpec((R, tn), lambda j: (0, jnp.maximum(j - 3 * each, 0))), hbm]
        args = args + [low, second]
        scratch = scratch + [pltpu.VMEM((R, D), bf16), pltpu.SemaphoreType.DMA((1,))]
    if extra:
        specs = specs + [pl.BlockSpec((shards, width), lambda j: (0, 0))]
        args = args + [small]
        scratch = scratch + [pltpu.VMEM((shards, extra, width), bf16), pltpu.SemaphoreType.DMA((2,))]
    return pl.pallas_call(
        functools.partial(weight_grad_kernel, each=each, other=other, extra=extra), grid=(3 * each + other,),
        in_specs=specs, out_specs=[hbm, hbm], out_shape=[half, half], scratch_shapes=scratch,
        compiler_params=cp(), name="weight_grad", cost_estimate=HINT,
    )(*args)

def cotangent_kernel(order_ref, d_ref, *refs, count, final, tm):
    pieces, refs = refs[:count], refs[count:]
    step = pl.program_id(0)
    if final:
        stat_ref, vec_ref, earlier_in, tokens_in, low_in, out_ref, small_ref, weight_ref, acc_ref, earlier_ref, tokens_ref, low_ref, result_ref, in_sem, out_sem = refs
        loads = [pltpu.make_async_copy(a, b, in_sem.at[k]) for k, (a, b) in enumerate(((earlier_in, earlier_ref), (tokens_in, tokens_ref), (low_in, low_ref)))]
        @pl.when(step == 0)
        def _():
            for c in loads:
                c.start()
    else:
        out_ref, weight_ref, acc_ref = refs
    in_order(order_ref, pieces, weight_ref)
    term = dot_nt(d_ref[0], weight_ref[...])
    @pl.when(step == 0)
    def _():
        acc_ref[...] = term
    @pl.when(step > 0)
    def _():
        acc_ref[...] += term

    @pl.when(step == 2)
    def _():
        if not final:
            out_ref[...] = acc_ref[...].astype(bf16)
        else:
            for c in loads:
                c.wait()
            small_ref[...] = jnp.zeros_like(small_ref)
            gain = row_of(vec_ref, GAIN1)
            stores = []
            for i in range(acc_ref.shape[0] // tm):
                at = slice(i * tm, (i + 1) * tm)
                dn = acc_ref[at] + earlier_ref[at].astype(f32)
                r = stat_ref[at, 1:2]
                nhat = (tokens_ref[at].astype(f32) - stat_ref[at, 0:1]) * r
                e = dn * gain
                d = low_ref[at].astype(f32) + r * (e - jnp.mean(e, axis=-1, keepdims=True) - nhat * jnp.mean(e * nhat, axis=-1, keepdims=True))
                result_ref[at] = d.astype(bf16)
                small_ref[0:1, :] += jnp.sum(dn * nhat, axis=0, keepdims=True)
                small_ref[1:2, :] += jnp.sum(dn, axis=0, keepdims=True)
                c = pltpu.make_async_copy(result_ref.at[pl.ds(i * tm, tm)], out_ref.at[pl.ds(i * tm, tm)], out_sem.at[i])
                c.start()
                stores.append(c)
            for c in stores:
                c.wait()

def cotangent(order, d, pieces, number, earlier=None, stats=None, vecs=None, tokens=None, low=None, tm=256):
    _, R, width = d.shape
    n, rows, _ = pieces[0].shape
    D = rows * n * len(pieces)
    per = D // width
    final = earlier is not None
    hbm = pl.BlockSpec(memory_space=pl.ANY)
    specs = [pl.BlockSpec(memory_space=pltpu.SMEM), pl.BlockSpec((1, R, width), lambda j: (j, 0, 0))]
    specs = specs + [pl.BlockSpec((n, rows, width), lambda j: (0, 0, j * per + number))] * len(pieces)
    scratch = [pltpu.VMEM((D, width), bf16), pltpu.VMEM((R, D), f32)]
    result = jax.ShapeDtypeStruct((R, D), bf16)
    more = ()
    if final:
        specs = specs + [pl.BlockSpec((R, 128), lambda j: (0, 0)), pl.BlockSpec(vecs.shape, lambda j: (0, 0)), hbm, hbm, hbm]
        more = (stats, vecs, earlier, tokens, low)
        outs, shapes = [hbm, pl.BlockSpec((8, D), lambda j: (0, 0))], [result, jax.ShapeDtypeStruct((8, D), f32)]
        scratch = scratch + [pltpu.VMEM((R, D), bf16)] * 4 + [pltpu.SemaphoreType.DMA((3,)), pltpu.SemaphoreType.DMA((R // tm,))]
    else:
        outs, shapes = pl.BlockSpec((R, D), lambda j: (0, 0)), result
    return pl.pallas_call(
        functools.partial(cotangent_kernel, count=len(pieces), final=final, tm=tm), grid=(3,),
        in_specs=specs, out_specs=outs, out_shape=shapes, scratch_shapes=scratch,
        compiler_params=cp(), name="cotangent", cost_estimate=HINT,
    )(order, d, *pieces, *more)

def owned_kernel(*refs, counts, rows, blocks, wide):
    parts, at = [], 0
    for c in counts:
        parts.append(sum(r[0].astype(f32) for r in refs[at:at + c]))
        at += c
    up_ref, down_ref = refs[at:]
    half = blocks // len(counts)
    D = down_ref.shape[1]
    for h, part in enumerate(parts):
        for b in range(half):
            down_ref[(h * half + b) * rows:(h * half + b + 1) * rows, :] = part[:, (half + b) * D:(half + b + 1) * D]
    per = D // rows
    group = blocks * rows
    lane = lax.broadcasted_iota(jnp.int32, (rows, 128), 1)
    for tile in range(blocks * D // 128):
        value = None
        for k in range(128 // rows):
            unit = (tile * 128 + k * rows) // rows
            shard, b = unit // blocks, unit % blocks
            source = (b % half) * D + shard * rows
            piece = parts[b // half][:, source // 128 * 128:source // 128 * 128 + 128]
            shift = (k * rows - source % 128) % 128
            if shift:
                piece = pltpu.roll(piece, shift, 1)
            value = piece if value is None else jnp.where(lane >= k * rows, piece, value)
        up_ref[:, tile * 128:(tile + 1) * 128] = value

def owned(groups, D, blocks):
    _, rows, width = groups[0][0].shape
    terms = [t for g in groups for t in g]
    return pl.pallas_call(
        functools.partial(owned_kernel, counts=[len(g) for g in groups], rows=rows, blocks=blocks, wide=width), grid=(1,),
        in_specs=[pl.BlockSpec((1, rows, width), lambda i: (0, 0, 0))] * len(terms),
        out_specs=[pl.BlockSpec((rows, blocks * D), lambda i: (0, 0)), pl.BlockSpec((blocks * rows, D), lambda i: (0, 0))],
        out_shape=[jax.ShapeDtypeStruct((rows, blocks * D), f32), jax.ShapeDtypeStruct((blocks * rows, D), f32)],
        compiler_params=cp(), name="owned", cost_estimate=HINT,
    )(*terms)


class Plan:
    def __init__(self, dp, fsdp):
        self.total = dp * fsdp
        bits = self.total.bit_length() - 1
        low = fsdp.bit_length() - 1
        if fsdp == 4:
            self.core, z, rest = low, list(range(low)), list(range(low + 1, bits))
        else:
            self.core, z, rest = 0, list(range(1, low)), list(range(low, bits))
        a, b = rest[:len(rest) // 2], rest[len(rest) // 2:]
        self.stages = [(a, b), (b, a), (z, z)]
        self.third = len(z) == low

    def masks(self, stage, core):
        bits = self.stages[stage][core]
        return [sum(1 << b for k, b in enumerate(bits) if j >> k & 1) for j in range(1 << len(bits))]

    def pairs(self, stage, j):
        return [(i, i ^ self.masks(stage, i >> self.core & 1)[j]) for i in range(self.total)]

    def size(self, stage):
        return 1 << len(self.stages[stage][0])

    def places(self, me, fixed=False):
        shard = lax.iota(jnp.int32, self.total)
        rel = shard ^ me
        core = (shard >> self.core) & 1
        pos = (rel >> self.core) & 1
        for k, (a, b) in enumerate(self.stages):
            pick = lambda bits, v: sum((((v >> bit) & 1) << k) for k, bit in enumerate(bits))
            own = pick(a, shard) if fixed and k == 2 else jnp.where(core == 0, pick(a, rel), pick(b, rel))
            pos = (pos << len(a)) + own
        return pos

AXES = ("dp", "fsdp")

def swap_core(plan, x):
    return lax.ppermute(x, AXES, [(i, i ^ (1 << plan.core)) for i in range(plan.total)])

def exchange(plan, x, stage, j):
    return lax.ppermute(x, AXES, plan.pairs(stage, j))

class Gathering:
    def __init__(self, plan, shard):
        self.plan, self.shard = plan, shard
        self.arrays = [exchange(plan, shard, 2, j) for j in range(1, plan.size(2))]

    def spread(self):
        column = jnp.stack([self.shard] + self.arrays)
        self.near = [exchange(self.plan, column, 1, j) for j in range(1, self.plan.size(1))]
        self.far = [exchange(self.plan, column, 0, j) for j in range(1, self.plan.size(0))]
        self.arrays = [column] + self.near + self.far

    def spread_again(self):
        n = self.plan.size(1)
        near, far = self.arrays[:n], self.arrays[n:]
        rest = [[exchange(self.plan, p, 0, j + 1) for p in near[1:]] for j in range(len(far))]
        other = [swap_core(self.plan, p) for p in self.arrays]
        self.first, self.other, self.arrays = self.arrays, other, [p for row in rest for p in row]

    def finish(self):
        n = self.plan.size(1)
        sides = (self.first, self.arrays), (self.other, [swap_core(self.plan, p) for p in self.arrays])
        pieces = []
        for first, rest in sides:
            pieces += first[:n]
            for j in range(self.plan.size(0) - 1):
                pieces += [first[n + j]] + rest[j * (n - 1):(j + 1) * (n - 1)]
        return pieces

def step(x, after, *reductions):
    x, _ = tie(x, after, *reductions)
    reductions = [r for r in reductions if r.stage < 3]
    if reductions:
        for r in reductions:
            r.add()
        x, = tie(x, *reductions)
        for r in reductions:
            r.go()
    return x

class Reduction:
    def __init__(self, plan, keep, send, one=False):
        self.plan, self.stage, self.size, self.one = plan, 0, keep.shape[0], one and plan.third
        self.terms = [keep, swap_core(plan, send)]
        self.sent = []

    def add(self):
        n = self.plan.size(self.stage)
        part = self.size // n
        if self.one and self.stage == 2:
            self.sent = [sum(t[:n].astype(f32) for t in self.terms).astype(self.terms[0].dtype)]
            return
        self.sent = [sum(t[j * part:(j + 1) * part].astype(f32) for t in self.terms).astype(self.terms[0].dtype) for j in range(1, n)]

    def go(self):
        if self.one and self.stage == 2:
            self.terms = [lax.psum_scatter(self.sent[0], AXES[1], scatter_dimension=0, tiled=False)[None]]
        else:
            self.terms = self.terms + [exchange(self.plan, s, self.stage, j + 1) for j, s in enumerate(self.sent)]
        self.sent = []
        self.size //= self.plan.size(self.stage)
        self.stage += 1

    def finish(self):
        while self.stage < 3:
            self.add()
            self.go()
        return sum(t[0].astype(f32) for t in self.terms)

def tie(*trees):
    flat = []
    for t in trees:
        flat += t.terms + t.sent if isinstance(t, Reduction) else t.arrays if isinstance(t, Gathering) else [t]
    flat = list(lax.optimization_barrier(tuple(flat)))
    out = []
    for t in trees:
        if isinstance(t, Reduction):
            t.terms = [flat.pop(0) for _ in t.terms]
            t.sent = [flat.pop(0) for _ in t.sent]
        elif isinstance(t, Gathering):
            t.arrays = [flat.pop(0) for _ in t.arrays]
        else:
            out.append(flat.pop(0))
    return out

def body(plan, tokens, prefix_len, padding_len, first_gain, first_shift, inproj_weight, query_bias, value_bias,
         outproj_weight, outproj_bias, second_gain, second_shift, up_weight, up_bias, down_weight, down_bias, grad_out):
    total = plan.total
    R, D = tokens.shape
    F = up_weight.shape[1]
    rows = D // total
    blocks = F // D
    me = lax.axis_index(AXES)
    pos = plan.places(me)
    pos_one = plan.places(me, plan.third)
    shard = lax.iota(jnp.int32, total)
    order = jnp.sum(jnp.where(pos[None, :] == shard[:, None], shard[None, :], 0), axis=1)
    n = first_gain.shape[0]
    half = blocks // 2
    up_local = up_weight.reshape(rows, total, blocks, rows).transpose(0, 2, 1, 3).reshape(rows, F)
    down_local = [down_weight[b * rows:(b + 1) * rows] for b in range(blocks)]
    small = jnp.concatenate([first_gain, first_shift, query_bias, value_bias, outproj_bias, second_gain, second_shift, down_bias, up_bias])
    small = jnp.pad(small.reshape(8 + blocks, rows).T, ((0, 0), (0, 128 - 8 - blocks)))
    inward = Gathering(plan, jnp.concatenate([inproj_weight, outproj_weight, small], axis=1))
    wide = lax.all_gather(jnp.concatenate([up_local] + down_local, axis=1), AXES, axis=0, tiled=True)
    stats = norm(tokens)
    stats, = tie(stats, inward)
    inward.spread()
    stats, = tie(stats, inward)
    inward.spread_again()
    stats, *inward.other = tie(stats, *inward.other, inward)
    inward = inward.finish()
    n1, qkv, vecs = project(order, tokens, stats, inward)
    ctx, lse = attend(prefix_len, padding_len, qkv)
    resid, n2, w_out = branch(order, ctx, tokens, vecs, inward)
    cut = D // 2
    n_pairs = D // 128
    def back(first, x, earlier=()):
        return attend_back(prefix_len, padding_len, qkv, x, ctx, lse, first, n_pairs // 4, cut, earlier)
    out, low, dctx, keep1, send1, keep2, send2, ubias_grad, mid = ffn(pos_one, n2, grad_out, vecs, wide, resid, w_out)
    g1 = Reduction(plan, keep1, send1, True)
    g2 = Reduction(plan, keep2, send2, True)
    d1 = back(0, dctx)
    dctx = step(dctx, d1[0], g1)
    d1 = back(n_pairs // 4, dctx, d1)
    n1a = step(n1, d1[0], g2)
    g3 = Reduction(plan, *weight_grad(pos, n1a, d1[0], ctx, low))
    dctx, _ = tie(dctx, g3.terms[0])
    d2 = back(n_pairs // 2, dctx)
    dctx = step(dctx, d2[0], g1)
    d2 = back(n_pairs * 3 // 4, dctx, d2)
    n1b = step(n1, d2[0], g2, g1)
    per = lambda v: v.reshape(total, -1)
    att = jnp.concatenate([d1[1], d2[1]], axis=1)
    ubg = ubias_grad.reshape(blocks, total, rows).transpose(1, 0, 2).reshape(total, -1)
    early = jnp.concatenate([per(att[0]), per(att[1]), per(mid[2]), per(mid[0]), per(mid[1]), per(mid[3]), ubg], axis=1)
    early = jnp.pad(early, ((0, 0), (0, cut - early.shape[1])))
    g4 = Reduction(plan, *weight_grad(pos, n1b, d2[0], small=early))
    da = step(d1[0], g4.terms[0], g3, g2)
    part = cotangent(order, da, inward, 0)
    part = step(part, part, g4)
    tokens_grad, end = cotangent(order, d2[0], inward, 1, part, stats, vecs, tokens, low)
    bits = [plan.core] + [bit for bit in range(total.bit_length() - 1) if bit != plan.core]
    swap = lambda v, bit: lax.ppermute(v, AXES, [(i, i ^ (1 << bit)) for i in range(total)])
    end = step(end[:2], end, g4)
    other = swap(end, bits[0])
    end = step(end, end, g3, g1)
    end, other = tie(end, other, g4)
    g4.add()
    g4.go()
    arriving = plan.size(2) - 1
    for k, bit in enumerate(bits[1:]):
        end = end + other
        other = swap(end, bit)
        if k < arriving:
            at = k - arriving
            other, g4.terms[at] = tie(other, g4.terms[at])
        if k == 0:
            other = step(other, other, g3)
    late = lax.dynamic_slice_in_dim(end + other, me * n, n, axis=1)
    in1, in2 = g3.finish(), g4.finish()
    up_grad, down_grad = owned([g1.terms, g2.terms], D, blocks)
    out_grad = jnp.concatenate([in1[3 * rows:4 * rows], in1[4 * rows:]], axis=1)
    in_grad = jnp.concatenate([g[k * rows:(k + 1) * rows] for k in range(3) for g in (in1, in2)], axis=1)
    early = in2[3 * rows]
    e = [early[i * n:(i + 1) * n] for i in range(6)]
    return (out, tokens_grad, late[0], late[1], in_grad, e[0], e[1], out_grad, e[2], e[3], e[4], up_grad, early[6 * n:6 * n + F // total], down_grad, e[5])

def solution(mesh):
    plan = Plan(mesh.shape["dp"], mesh.shape["fsdp"])
    rows, flat = P(AXES, None), P(AXES)
    ins = (rows, flat, flat, flat, flat, rows, flat, flat, rows, flat, flat, flat, rows, flat, rows, flat, rows)
    outs = (rows, rows, flat, flat, rows, flat, flat, rows, flat, flat, flat, rows, flat, rows, flat)
    return jax.shard_map(functools.partial(body, plan), mesh=mesh, in_specs=ins, out_specs=outs, check_vma=False)
```

```python
import functools, math
import jax, jax.numpy as jnp
from jax import lax
from jax.sharding import PartitionSpec as P
from jax.experimental import pallas as pl
from jax.experimental.pallas import tpu as pltpu
HEADS=16
EPSILON = 1e-05
NEGATIVE = -1000000000.0
bf16=jnp.bfloat16; f32=jnp.float32
VMEM_LIMIT=60*1024*1024
HINT=pl.CostEstimate(flops=1000, bytes_accessed=1000, transcendentals=0)
def cp(n=1): return pltpu.CompilerParams(dimension_semantics=("arbitrary",)*n, vmem_limit_bytes=VMEM_LIMIT)
def dot(a,b): return lax.dot_general(a,b,(((1,),(0,)),((),())),preferred_element_type=f32)
def dot_nt(a,b): return lax.dot_general(a,b,(((1,),(1,)),((),())),preferred_element_type=f32)
def dot_tn(a,b): return lax.dot_general(a,b,(((0,),(0,)),((),())),preferred_element_type=f32)

GAIN1, SHIFT1, QBIAS, VBIAS, OBIAS, GAIN2, SHIFT2, DBIAS, UBIAS = range(9)

def row_of(ref, k):
    return ref[k:k + 1, :]

def norm_kernel(tokens_ref, out_ref):
    x = tokens_ref[...].astype(f32)
    mean = jnp.mean(x, axis=-1, keepdims=True)
    center = x - mean
    r = lax.rsqrt(jnp.mean(center * center, axis=-1, keepdims=True) + EPSILON)
    lane = lax.broadcasted_iota(jnp.int32, out_ref.shape, 1)
    out_ref[...] = jnp.where(lane == 0, mean, r)

def norm(tokens, tm=256):
    R, D = tokens.shape
    return pl.pallas_call(
        norm_kernel, grid=(R // tm,), in_specs=[pl.BlockSpec((tm, D), lambda i: (i, 0))], out_specs=pl.BlockSpec((tm, 128), lambda i: (i, 0)),
        out_shape=jax.ShapeDtypeStruct((R, 128), f32), compiler_params=cp(), name="norm", cost_estimate=HINT,
    )(tokens)

def in_order(order_ref, pieces, whole_ref):
    n, rows, _ = pieces[0].shape
    for p, piece in enumerate(pieces):
        for i in range(n):
            whole_ref[pl.ds(pl.multiple_of(order_ref[p * n + i] * rows, rows), rows), :] = piece[i]

def project_kernel(order_ref, tokens_ref, stat_ref, *refs, count):
    pieces, sides = refs[:count], refs[count:2 * count]
    normed_ref, out_ref, vec_ref, weight_ref, side_ref, all_ref = refs[2 * count:]
    step = pl.program_id(0)
    @pl.when(step == 0)
    def _():
        in_order(order_ref, sides, side_ref)
        all_ref[...] = jnp.transpose(side_ref[...].astype(f32))
        vec_ref[...] = all_ref[:16, :]
        xhat = (tokens_ref[...].astype(f32) - stat_ref[:, 0:1]) * stat_ref[:, 1:2]
        normed_ref[...] = (xhat * all_ref[GAIN1:GAIN1 + 1, :] + all_ref[SHIFT1:SHIFT1 + 1, :]).astype(bf16)
    in_order(order_ref, pieces, weight_ref)
    D = normed_ref.shape[1]
    tn = out_ref.shape[1]
    third = pl.num_programs(0) // 3
    at = pl.ds(pl.multiple_of(lax.rem(step, D // tn) * tn, tn), tn)
    bias = jnp.where(step < third, all_ref[QBIAS:QBIAS + 1, at], jnp.where(step < 2 * third, 0.0, all_ref[VBIAS:VBIAS + 1, at]))
    factor = jnp.where(step < third, 0.125, 1.0)
    out = dot(normed_ref[...], weight_ref[...]) + bias
    out_ref[...] = (out * factor).astype(bf16)

def project(order, tokens, stats, pieces, tn=512):
    R, D = tokens.shape
    n, rows, width = pieces[0].shape
    N = 3 * D
    full = pl.BlockSpec((R, D), lambda j: (0, 0))
    return pl.pallas_call(
        functools.partial(project_kernel, count=len(pieces)), grid=(N // tn,),
        in_specs=[pl.BlockSpec(memory_space=pltpu.SMEM), full, pl.BlockSpec((R, 128), lambda j: (0, 0))]
        + [pl.BlockSpec((n, rows, tn), lambda j: (0, 0, j))] * len(pieces)
        + [pl.BlockSpec((n, rows, 128), lambda j: (0, 0, width // 128 - 1))] * len(pieces),
        out_specs=[full, pl.BlockSpec((R, tn), lambda j: (0, j)), pl.BlockSpec((16, D), lambda j: (0, 0))],
        out_shape=[jax.ShapeDtypeStruct((R, D), bf16), jax.ShapeDtypeStruct((R, N), bf16), jax.ShapeDtypeStruct((16, D), f32)],
        scratch_shapes=[pltpu.VMEM((D, tn), bf16), pltpu.VMEM((D, 128), bf16), pltpu.VMEM((128, D), f32)],
        compiler_params=cp(), name="project", cost_estimate=HINT,
    )(order, tokens, stats, *pieces, *pieces)

def key_bias(prefix, limit, lo, q0, bq, transposed, diagonal):
    shape = (bq, bq)
    kd = 0 if transposed else 1
    k = lo + lax.broadcasted_iota(jnp.int32, shape, kd)
    ok = k < limit
    if diagonal:
        q = q0 + lax.broadcasted_iota(jnp.int32, shape, 1 - kd)
        ok = ok & ((k < prefix) | (k <= q))
    return jnp.where(ok, 0.0, NEGATIVE)

def attend_kernel(prefix_ref, padding_ref, q_ref, k_ref, v_ref, out_ref, lse_ref, bias_ref, *, bq):
    L = q_ref.shape[0]
    step = pl.program_id(0)
    prefix = prefix_ref[0]
    limit = L - padding_ref[0]
    n = L // bq
    lane = lax.broadcasted_iota(jnp.int32, (1, 128), 1)
    @pl.when(step == 0)
    def _():
        for b in range(n):
            bias_ref[b] = key_bias(prefix, limit, b * bq, b * bq, bq, True, True)
    vT = jnp.transpose(v_ref[...])
    ones = jnp.ones((16, L), bf16)
    values = [jnp.concatenate([vT[64 * h:64 * h + 64], ones], axis=0) for h in range(2)]
    for b in range(n):
        start, stop = b * bq, (b + 1) * bq
        q = q_ref[start:stop, :]
        both = jnp.concatenate([jnp.where(lane < 64, q, 0), jnp.where(lane >= 64, q, 0)], axis=0).astype(bf16)
        s = []
        for kb in range(b + 1):
            t = dot_nt(k_ref[kb * bq:(kb + 1) * bq, :], both)
            if kb == b:
                t = t + jnp.concatenate([bias_ref[b], bias_ref[b]], axis=1)
            elif (kb + 1) * bq > L - 384:
                kk = kb * bq + lax.broadcasted_iota(jnp.int32, (bq, 1), 0)
                t = t + jnp.where(kk < limit, 0.0, NEGATIVE)
            s.append(t)
        m = functools.reduce(jnp.maximum, [jnp.max(t, axis=0, keepdims=True) for t in s])
        acc = [None, None]
        for kb in range(b + 1):
            e = jnp.exp(s[kb] - m).astype(bf16)
            for h in range(2):
                t = dot(values[h][:, kb * bq:(kb + 1) * bq], e[:, h * bq:(h + 1) * bq])
                acc[h] = t if acc[h] is None else acc[h] + t
        ctx = [a[:64] * (1.0 / a[64:65]) for a in acc]
        out_ref[start:stop, :] = jnp.transpose(jnp.concatenate(ctx, axis=0)).astype(bf16)
        for h in range(2):
            lse_ref[pl.ds(2 * step + h, 1), start:stop] = m[:, h * bq:(h + 1) * bq] + jnp.log(acc[h][64:65])

def attend(prefix, padding, qkv, bq=256):
    L = qkv.shape[0]
    D = qkv.shape[1] // 3
    n = D // 128
    smem = pl.BlockSpec(memory_space=pltpu.SMEM)
    col = lambda off: pl.BlockSpec((L, 128), lambda j: (0, j + off))
    return pl.pallas_call(
        functools.partial(attend_kernel, bq=bq), grid=(n,),
        in_specs=[smem, smem, col(0), col(n), col(2 * n)],
        out_specs=[col(0), pl.BlockSpec((2 * n, L), lambda j: (0, 0))],
        out_shape=[jax.ShapeDtypeStruct((L, D), bf16), jax.ShapeDtypeStruct((2 * n, L), f32)],
        scratch_shapes=[pltpu.VMEM((L // bq, bq, bq), f32)],
        compiler_params=cp(), name="attend",
        cost_estimate=HINT,
    )(prefix, padding, qkv, qkv, qkv)

def branch_kernel(order_ref, ctx_ref, tokens_ref, vec_ref, *refs):
    *pieces, resid_ref, normed_ref, weight_ref = refs
    @pl.when(pl.program_id(0) == 0)
    def _():
        in_order(order_ref, pieces, weight_ref)
    resid = tokens_ref[...].astype(f32) + (dot(ctx_ref[...], weight_ref[...]) + row_of(vec_ref, OBIAS))
    center = resid - jnp.mean(resid, axis=-1, keepdims=True)
    spread = jnp.mean(center * center, axis=-1, keepdims=True)
    normed = center * lax.rsqrt(spread + EPSILON) * row_of(vec_ref, GAIN2) + row_of(vec_ref, SHIFT2)
    resid_ref[...] = resid
    normed_ref[...] = normed.astype(bf16)

def branch(order, ctx, tokens, vecs, pieces, tm=256):
    R, D = ctx.shape
    n, high, _ = pieces[0].shape
    rows = pl.BlockSpec((tm, D), lambda i: (i, 0))
    return pl.pallas_call(
        branch_kernel, grid=(R // tm,),
        in_specs=[pl.BlockSpec(memory_space=pltpu.SMEM), rows, rows, pl.BlockSpec(vecs.shape, lambda i: (0, 0))]
        + [pl.BlockSpec((n, high, D), lambda i: (0, 0, 3))] * len(pieces),
        out_specs=[rows, rows, pl.BlockSpec((D, D), lambda i: (0, 0))],
        out_shape=[jax.ShapeDtypeStruct((R, D), f32), jax.ShapeDtypeStruct((R, D), bf16), jax.ShapeDtypeStruct((D, D), bf16)],
        compiler_params=cp(), name="branch", cost_estimate=HINT,
    )(order, ctx, tokens, vecs, *pieces)

def ffn_kernel(pos_ref, normed_ref, grad_ref, vec_ref, rows_ref, up_ref, down_ref, resid_in, weight_in,
               result_out, low_out, dctx_out, keep1_ref, send1_ref, keep2_ref, send2_ref, biasg_ref, small_ref,
               out_ref, dn_ref, ups_ref, dns_ref, resid_ref, weight_ref, result_ref, low_ref, dctx_ref, up_sem, dn_sem, in_sem, out_sem, *, shards, per, blocks, tm):
    step = pl.program_id(0)
    last = pl.num_programs(0) - 1
    D = normed_ref.shape[1]
    tf = ups_ref.shape[3]
    half = shards // 2
    rows = D // shards
    each = blocks // 2
    slot = lax.rem(step, 2)
    block = lax.div(step, per)
    bslot = lax.rem(block, 2)
    groups = ((keep1_ref, send1_ref), (keep2_ref, send2_ref))

    def up_copies(slot, step, group):
        cols = pl.ds(pl.multiple_of(step * tf - group * each * D, tf), tf)
        return [pltpu.make_async_copy(ups_ref.at[slot, pl.ds(k * half, half)], groups[group][k].at[:, :, cols], up_sem.at[slot, k]) for k in range(2)]

    def down_copies(bslot, block, group):
        cols = pl.ds(pl.multiple_of((each + block - group * each) * D, D), D)
        return [pltpu.make_async_copy(dns_ref.at[bslot, pl.ds(k * half, half)], groups[group][k].at[:, :, cols], dn_sem.at[bslot, k]) for k in range(2)]

    def each_group(block, do):
        for group in range(2):
            pl.when((block >= group * each) & (block < (group + 1) * each))(functools.partial(do, group))

    def start_up(group):
        for c in up_copies(slot, step, group):
            c.start()

    def wait_up(slot, step):
        def do(group):
            for c in up_copies(slot, step, group):
                c.wait()
        each_group(lax.div(step, per), do)

    def start_down(group):
        for c in down_copies(bslot, block, group):
            c.start()

    def wait_down(bslot, block):
        def do(group):
            for c in down_copies(bslot, block, group):
                c.wait()
        each_group(block, do)

    loads = [pltpu.make_async_copy(resid_in, resid_ref, in_sem.at[0]), pltpu.make_async_copy(weight_in, weight_ref, in_sem.at[1])]

    @pl.when(step == 0)
    def _():
        for c in loads:
            c.start()
        out_ref[...] = jnp.zeros_like(out_ref)
        dn_ref[...] = jnp.zeros_like(dn_ref)

    @pl.when(step >= 2)
    def _():
        wait_up(slot, step - 2)

    @pl.when((step >= 2 * per) & (lax.rem(step, per) == 0))
    def _():
        wait_down(bslot, block - 2)

    n2 = normed_ref[...]
    go = grad_ref[...]
    up = up_ref[...]
    down = down_ref[...]
    bias = row_of(vec_ref, UBIAS)
    for k in range(1, blocks):
        bias = jnp.where(block == k, row_of(vec_ref, UBIAS + k), bias)
    u = dot(n2, up) + bias
    cdf = 0.5 * (1.0 + lax.erf(u * math.sqrt(0.5)))
    a = (u * cdf).astype(bf16)
    slope = cdf + u * (jnp.exp(-0.5 * u * u) * (1.0 / math.sqrt(2 * math.pi)))
    du = (dot_nt(go, down) * slope).astype(bf16)
    out_ref[...] += dot(a, down)
    dn_ref[...] += dot_nt(du, up)
    biasg_ref[...] = jnp.sum(du.astype(f32), axis=0, keepdims=True)
    upg = dot_tn(n2, du).astype(bf16)
    for i in range(shards):
        ups_ref[slot, pos_ref[i]] = upg[i * rows:(i + 1) * rows]
    downg = dot_tn(a, go).astype(bf16)
    here = tf // rows
    at = lax.rem(step, per) * here
    for i in range(here):
        dns_ref[bslot, pos_ref[at + i]] = downg[i * rows:(i + 1) * rows]
    each_group(block, start_up)

    @pl.when(lax.rem(step, per) == per - 1)
    def _():
        each_group(block, start_down)

    @pl.when(step == last)
    def _():
        for c in loads:
            c.wait()
        small_ref[...] = jnp.zeros_like(small_ref)
        pairs = ((result_ref, result_out), (low_ref, low_out), (dctx_ref, dctx_out))

        def stores(i):
            at = pl.ds(pl.multiple_of(i * tm, tm), tm)
            return [pltpu.make_async_copy(here.at[at], there.at[at], out_sem.at[i, k]) for k, (here, there) in enumerate(pairs)]

        def tile(i, carry):
            at = pl.ds(pl.multiple_of(i * tm, tm), tm)
            resid = resid_ref[at, :]
            result_ref[at, :] = (resid + out_ref[at, :] + row_of(rows_ref, DBIAS)).astype(bf16)
            center = resid - jnp.mean(resid, axis=-1, keepdims=True)
            r = lax.rsqrt(jnp.mean(center * center, axis=-1, keepdims=True) + EPSILON)
            nhat = center * r
            dn = dn_ref[at, :]
            go = grad_ref[at, :].astype(f32)
            e = dn * row_of(rows_ref, GAIN2)
            low = (go + r * (e - jnp.mean(e, axis=-1, keepdims=True) - nhat * jnp.mean(e * nhat, axis=-1, keepdims=True))).astype(bf16)
            low_ref[at, :] = low
            dctx_ref[at, :] = dot_nt(low, weight_ref[...]).astype(bf16)
            small_ref[0:1, :] += jnp.sum(dn * nhat, axis=0, keepdims=True)
            small_ref[1:2, :] += jnp.sum(dn, axis=0, keepdims=True)
            small_ref[2:3, :] += jnp.sum(low.astype(f32), axis=0, keepdims=True)
            small_ref[3:4, :] += jnp.sum(go, axis=0, keepdims=True)
            for c in stores(i):
                c.start()
            return carry

        tiles = resid_ref.shape[0] // tm
        lax.fori_loop(0, tiles, tile, 0)
        for i in range(tiles):
            for c in stores(i):
                c.wait()
        for c in up_copies(1 - slot, step - 1, 1) + up_copies(slot, step, 1) + down_copies(1 - bslot, block - 1, 1) + down_copies(bslot, block, 1):
            c.wait()

def ffn(pos, normed, grad, vecs, wide, resid, weight, tf=512, tm=256):
    R, D = normed.shape
    blocks = wide.shape[1] // D // 2
    F = blocks * D
    shards = pos.shape[0]
    rows = D // shards
    per = D // tf
    full = pl.BlockSpec((R, D), lambda j: (0, 0))
    hbm = pl.BlockSpec(memory_space=pl.ANY)
    part = jax.ShapeDtypeStruct((shards // 2, rows, F), bf16)
    low = jax.ShapeDtypeStruct((R, D), bf16)
    return pl.pallas_call(
        functools.partial(ffn_kernel, shards=shards, per=per, blocks=blocks, tm=tm), grid=(F // tf,),
        in_specs=[pl.BlockSpec(memory_space=pltpu.SMEM), full, full, pl.BlockSpec((16, tf), lambda j: (0, lax.rem(j, per))), pl.BlockSpec((16, D), lambda j: (0, 0)),
                  pl.BlockSpec((D, tf), lambda j: (0, j)), pl.BlockSpec((tf, D), lambda j: (lax.rem(j, per), blocks + lax.div(j, per))), hbm, hbm],
        out_specs=[hbm] * 7 + [pl.BlockSpec((1, tf), lambda j: (0, j)), pl.BlockSpec((8, D), lambda j: (0, 0))],
        out_shape=[low, low, low, part, part, part, part, jax.ShapeDtypeStruct((1, F), f32), jax.ShapeDtypeStruct((8, D), f32)],
        scratch_shapes=[pltpu.VMEM((R, D), f32), pltpu.VMEM((R, D), f32), pltpu.VMEM((2, shards, rows, tf), bf16), pltpu.VMEM((2, shards, rows, D), bf16),
                        pltpu.VMEM((R, D), f32), pltpu.VMEM((D, D), bf16), pltpu.VMEM((R, D), bf16), pltpu.VMEM((R, D), bf16), pltpu.VMEM((R, D), bf16),
                        pltpu.SemaphoreType.DMA((2, 2)), pltpu.SemaphoreType.DMA((2, 2)), pltpu.SemaphoreType.DMA((2,)), pltpu.SemaphoreType.DMA((R // tm, 3))],
        compiler_params=cp(), name="ffn", cost_estimate=HINT,
    )(pos, normed, grad, vecs, vecs, wide, wide, resid, weight)

def attend_back_kernel(prefix_ref, padding_ref, q_ref, k_ref, v_ref, do_ref, o_ref, lse_ref, *refs, bq, first):
    d_ref, small_ref, dka_ref, dva_ref, bias_ref = refs[-5:]
    L = q_ref.shape[0]
    step = pl.program_id(0) + first
    prefix = prefix_ref[0]
    limit = L - padding_ref[0]
    n = L // bq
    lane = lax.broadcasted_iota(jnp.int32, (1, 128), 1)
    @pl.when(pl.program_id(0) == 0)
    def _():
        for b in range(n):
            bias_ref[b] = key_bias(prefix, limit, b * bq, b * bq, bq, True, True)
    kT = jnp.transpose(k_ref[...])
    prod = do_ref[...].astype(f32) * o_ref[...].astype(f32)
    row = lax.broadcasted_iota(jnp.int32, (8, 128), 0)
    col = lax.broadcasted_iota(jnp.int32, (8, 128), 1)
    pick = jnp.where((col // 64) == row, 1.0, 0.0)
    delta = lax.dot_general(pick, prod, (((1,), (1,)), ((), ())), precision=lax.Precision.HIGHEST, preferred_element_type=f32)
    for b in range(n):
        start, stop = b * bq, (b + 1) * bq
        q = q_ref[start:stop, :]
        do = do_ref[start:stop, :]
        both = jnp.concatenate([jnp.where(lane < 64, q, 0), jnp.where(lane >= 64, q, 0)], axis=0).astype(bf16)
        dboth = jnp.concatenate([jnp.where(lane < 64, do, 0), jnp.where(lane >= 64, do, 0)], axis=0).astype(bf16)
        lse = jnp.concatenate([lse_ref[pl.ds(2 * step, 1), start:stop], lse_ref[pl.ds(2 * step + 1, 1), start:stop]], axis=1)
        inner = jnp.concatenate([delta[0:1, start:stop], delta[1:2, start:stop]], axis=1)
        dq = [None, None]
        for kb in range(b + 1):
            ks = slice(kb * bq, (kb + 1) * bq)
            s = dot_nt(k_ref[ks, :], both)
            if kb == b:
                s = s + jnp.concatenate([bias_ref[b], bias_ref[b]], axis=1)
            elif (kb + 1) * bq > L - 384:
                kk = kb * bq + lax.broadcasted_iota(jnp.int32, (bq, 1), 0)
                s = s + jnp.where(kk < limit, 0.0, NEGATIVE)
            p = jnp.exp(s - lse)
            ds = (p * (dot_nt(v_ref[ks, :], dboth) - inner)).astype(bf16)
            tv = dot(p.astype(bf16), dboth)
            tk = dot(ds, both)
            if kb == b:
                dva_ref[ks, :] = tv
                dka_ref[ks, :] = tk
            else:
                dva_ref[ks, :] += tv
                dka_ref[ks, :] += tk
            for h in range(2):
                t = dot(kT[64 * h:64 * h + 64, ks], ds[:, h * bq:(h + 1) * bq])
                dq[h] = t if dq[h] is None else dq[h] + t
        d_ref[0, start:stop, :] = (jnp.transpose(jnp.concatenate(dq, axis=0)) * 0.125).astype(bf16)
    d_ref[1] = dka_ref[...].astype(bf16)
    d_ref[2] = dva_ref[...].astype(bf16)
    small_ref[0:1, :] = jnp.sum(d_ref[0].astype(f32), axis=0, keepdims=True)
    small_ref[1:2, :] = jnp.sum(d_ref[2].astype(f32), axis=0, keepdims=True)

def attend_back(prefix, padding, qkv, dctx, ctx, lse, first, count, width, earlier=(), bq=256):
    L = qkv.shape[0]
    D = dctx.shape[1]
    n = D // 128
    at = first % (width // 128)
    smem = pl.BlockSpec(memory_space=pltpu.SMEM)
    col = lambda off: pl.BlockSpec((L, 128), lambda j: (0, j + off))
    return pl.pallas_call(
        functools.partial(attend_back_kernel, bq=bq, first=first), grid=(count,),
        in_specs=[smem, smem, col(first), col(n + first), col(2 * n + first), col(first), col(first), pl.BlockSpec((2 * n, L), lambda j: (0, 0))]
        + [pl.BlockSpec(memory_space=pl.ANY)] * len(earlier),
        out_specs=[pl.BlockSpec((3, L, 128), lambda j: (0, 0, j + at)), pl.BlockSpec((8, 128), lambda j: (0, j + at))],
        out_shape=[jax.ShapeDtypeStruct((3, L, width), bf16), jax.ShapeDtypeStruct((8, width), f32)],
        scratch_shapes=[pltpu.VMEM((L, 128), f32), pltpu.VMEM((L, 128), f32), pltpu.VMEM((L // bq, bq, bq), f32)],
        input_output_aliases={8 + i: i for i in range(len(earlier))},
        compiler_params=cp(), name="attend_back",
        cost_estimate=HINT,
    )(prefix, padding, qkv, qkv, qkv, dctx, ctx, lse, *earlier)

def weight_grad_kernel(pos_ref, left_ref, d_ref, *refs, each, other, extra):
    refs = list(refs)
    if other:
        low_ref, second_in = refs[:2]
        refs = refs[2:]
    if extra:
        small_ref = refs.pop(0)
    keep_ref, send_ref, stage_ref, stage_sem = refs[:4]
    refs = refs[4:]
    if other:
        second_ref, second_sem = refs[:2]
        refs = refs[2:]
    if extra:
        extra_ref, extra_sem = refs
    step = pl.program_id(0)
    steps = 3 * each + other
    _, shards, rows, tn = stage_ref.shape
    half = shards // 2
    slot = lax.rem(step, 2)

    def copies(slot, step):
        high = pl.ds(pl.multiple_of(lax.div(step, each) * rows, rows), rows)
        cols = pl.ds(pl.multiple_of(lax.rem(step, each) * tn, tn), tn)
        return [pltpu.make_async_copy(stage_ref.at[slot, pl.ds(k * half, half)], out.at[:, high, cols], stage_sem.at[slot, k]) for k, out in enumerate((keep_ref, send_ref))]

    if extra:
        behind = [pltpu.make_async_copy(extra_ref.at[pl.ds(k * half, half)], out.at[:, pl.ds(3 * rows, extra), :], extra_sem.at[k]) for k, out in enumerate((keep_ref, send_ref))]
    if other:
        second = pltpu.make_async_copy(second_in, second_ref, second_sem.at[0])

    @pl.when(step == 0)
    def _():
        if other:
            second.start()
        if extra:
            for i in range(shards):
                extra_ref[pos_ref[i]] = jnp.broadcast_to(small_ref[i:i + 1, :], extra_ref.shape[1:]).astype(bf16)
            for c in behind:
                c.start()

    @pl.when(step >= 2)
    def _():
        for c in copies(slot, step - 2):
            c.wait()

    def put(value):
        for i in range(shards):
            stage_ref[slot, pos_ref[i]] = value[i * rows:(i + 1) * rows].astype(bf16)

    if other:
        @pl.when(step == 3 * each)
        def _():
            second.wait()

        @pl.when(step >= 3 * each)
        def _():
            put(dot_tn(second_ref[...], low_ref[...]))

        @pl.when(step < 3 * each)
        def _():
            put(dot_tn(left_ref[...], d_ref[0]))
    else:
        put(dot_tn(left_ref[...], d_ref[0]))
    for c in copies(slot, step):
        c.start()

    @pl.when(step == steps - 1)
    def _():
        for c in copies(1 - slot, step - 1) + copies(slot, step) + (behind if extra else []):
            c.wait()

def weight_grad(pos, left, d, second=None, low=None, small=None, tn=512):
    R, D = left.shape
    _, _, width = d.shape
    shards = pos.shape[0]
    rows = D // shards
    each = width // tn
    other = D // tn if second is not None else 0
    extra = min(rows, 16) if small is not None else 0
    high = (3 * each + other) // each * rows + extra
    half = jax.ShapeDtypeStruct((shards // 2, high, width), bf16)
    hbm = pl.BlockSpec(memory_space=pl.ANY)
    specs = [pl.BlockSpec(memory_space=pltpu.SMEM), pl.BlockSpec((R, D), lambda j: (0, 0)),
             pl.BlockSpec((1, R, tn), lambda j: (jnp.minimum(lax.div(j, each), 2), 0, jnp.where(j < 3 * each, lax.rem(j, each), each - 1)))]
    args = [pos, left, d]
    scratch = [pltpu.VMEM((2, shards, rows, tn), bf16), pltpu.SemaphoreType.DMA((2, 2))]
    if other:
        specs = specs + [pl.BlockSpec((R, tn), lambda j: (0, jnp.maximum(j - 3 * each, 0))), hbm]
        args = args + [low, second]
        scratch = scratch + [pltpu.VMEM((R, D), bf16), pltpu.SemaphoreType.DMA((1,))]
    if extra:
        specs = specs + [pl.BlockSpec((shards, width), lambda j: (0, 0))]
        args = args + [small]
        scratch = scratch + [pltpu.VMEM((shards, extra, width), bf16), pltpu.SemaphoreType.DMA((2,))]
    return pl.pallas_call(
        functools.partial(weight_grad_kernel, each=each, other=other, extra=extra), grid=(3 * each + other,),
        in_specs=specs, out_specs=[hbm, hbm], out_shape=[half, half], scratch_shapes=scratch,
        compiler_params=cp(), name="weight_grad", cost_estimate=HINT,
    )(*args)

def cotangent_kernel(order_ref, d_ref, *refs, count, final, tm):
    pieces, refs = refs[:count], refs[count:]
    step = pl.program_id(0)
    if final:
        stat_ref, vec_ref, earlier_in, tokens_in, low_in, out_ref, small_ref, weight_ref, acc_ref, earlier_ref, tokens_ref, low_ref, result_ref, in_sem, out_sem = refs
        loads = [pltpu.make_async_copy(a, b, in_sem.at[k]) for k, (a, b) in enumerate(((earlier_in, earlier_ref), (tokens_in, tokens_ref), (low_in, low_ref)))]
        @pl.when(step == 0)
        def _():
            for c in loads:
                c.start()
    else:
        out_ref, weight_ref, acc_ref = refs
    in_order(order_ref, pieces, weight_ref)
    term = dot_nt(d_ref[0], weight_ref[...])
    @pl.when(step == 0)
    def _():
        acc_ref[...] = term
    @pl.when(step > 0)
    def _():
        acc_ref[...] += term

    @pl.when(step == 2)
    def _():
        if not final:
            out_ref[...] = acc_ref[...].astype(bf16)
        else:
            for c in loads:
                c.wait()
            small_ref[...] = jnp.zeros_like(small_ref)
            gain = row_of(vec_ref, GAIN1)
            def store(i):
                at = pl.ds(pl.multiple_of(i * tm, tm), tm)
                return pltpu.make_async_copy(result_ref.at[at], out_ref.at[at], out_sem.at[i])

            def tile(i, carry):
                at = pl.ds(pl.multiple_of(i * tm, tm), tm)
                dn = acc_ref[at, :] + earlier_ref[at, :].astype(f32)
                r = stat_ref[at, 1:2]
                nhat = (tokens_ref[at, :].astype(f32) - stat_ref[at, 0:1]) * r
                e = dn * gain
                d = low_ref[at, :].astype(f32) + r * (e - jnp.mean(e, axis=-1, keepdims=True) - nhat * jnp.mean(e * nhat, axis=-1, keepdims=True))
                result_ref[at, :] = d.astype(bf16)
                small_ref[0:1, :] += jnp.sum(dn * nhat, axis=0, keepdims=True)
                small_ref[1:2, :] += jnp.sum(dn, axis=0, keepdims=True)
                store(i).start()
                return carry

            tiles = acc_ref.shape[0] // tm
            lax.fori_loop(0, tiles, tile, 0)
            for i in range(tiles):
                store(i).wait()

def cotangent(order, d, pieces, number, earlier=None, stats=None, vecs=None, tokens=None, low=None, tm=256):
    _, R, width = d.shape
    n, rows, _ = pieces[0].shape
    D = rows * n * len(pieces)
    per = D // width
    final = earlier is not None
    hbm = pl.BlockSpec(memory_space=pl.ANY)
    specs = [pl.BlockSpec(memory_space=pltpu.SMEM), pl.BlockSpec((1, R, width), lambda j: (j, 0, 0))]
    specs = specs + [pl.BlockSpec((n, rows, width), lambda j: (0, 0, j * per + number))] * len(pieces)
    scratch = [pltpu.VMEM((D, width), bf16), pltpu.VMEM((R, D), f32)]
    result = jax.ShapeDtypeStruct((R, D), bf16)
    more = ()
    if final:
        specs = specs + [pl.BlockSpec((R, 128), lambda j: (0, 0)), pl.BlockSpec(vecs.shape, lambda j: (0, 0)), hbm, hbm, hbm]
        more = (stats, vecs, earlier, tokens, low)
        outs, shapes = [hbm, pl.BlockSpec((8, D), lambda j: (0, 0))], [result, jax.ShapeDtypeStruct((8, D), f32)]
        scratch = scratch + [pltpu.VMEM((R, D), bf16)] * 4 + [pltpu.SemaphoreType.DMA((3,)), pltpu.SemaphoreType.DMA((R // tm,))]
    else:
        outs, shapes = pl.BlockSpec((R, D), lambda j: (0, 0)), result
    return pl.pallas_call(
        functools.partial(cotangent_kernel, count=len(pieces), final=final, tm=tm), grid=(3,),
        in_specs=specs, out_specs=outs, out_shape=shapes, scratch_shapes=scratch,
        compiler_params=cp(), name="cotangent", cost_estimate=HINT,
    )(order, d, *pieces, *more)

def owned_kernel(*refs, counts, rows, blocks, wide):
    parts, at = [], 0
    for c in counts:
        parts.append(sum(r[0].astype(f32) for r in refs[at:at + c]))
        at += c
    up_ref, down_ref = refs[at:]
    half = blocks // len(counts)
    D = down_ref.shape[1]
    for h, part in enumerate(parts):
        for b in range(half):
            down_ref[(h * half + b) * rows:(h * half + b + 1) * rows, :] = part[:, (half + b) * D:(half + b + 1) * D]
    per = D // rows
    group = blocks * rows
    lane = lax.broadcasted_iota(jnp.int32, (rows, 128), 1)
    for tile in range(blocks * D // 128):
        value = None
        for k in range(128 // rows):
            unit = (tile * 128 + k * rows) // rows
            shard, b = unit // blocks, unit % blocks
            source = (b % half) * D + shard * rows
            piece = parts[b // half][:, source // 128 * 128:source // 128 * 128 + 128]
            shift = (k * rows - source % 128) % 128
            if shift:
                piece = pltpu.roll(piece, shift, 1)
            value = piece if value is None else jnp.where(lane >= k * rows, piece, value)
        up_ref[:, tile * 128:(tile + 1) * 128] = value

def owned(groups, D, blocks):
    _, rows, width = groups[0][0].shape
    terms = [t for g in groups for t in g]
    return pl.pallas_call(
        functools.partial(owned_kernel, counts=[len(g) for g in groups], rows=rows, blocks=blocks, wide=width), grid=(1,),
        in_specs=[pl.BlockSpec((1, rows, width), lambda i: (0, 0, 0))] * len(terms),
        out_specs=[pl.BlockSpec((rows, blocks * D), lambda i: (0, 0)), pl.BlockSpec((blocks * rows, D), lambda i: (0, 0))],
        out_shape=[jax.ShapeDtypeStruct((rows, blocks * D), f32), jax.ShapeDtypeStruct((blocks * rows, D), f32)],
        compiler_params=cp(), name="owned", cost_estimate=HINT,
    )(*terms)


class Plan:
    def __init__(self, dp, fsdp):
        self.total = dp * fsdp
        bits = self.total.bit_length() - 1
        low = fsdp.bit_length() - 1
        if fsdp == 4:
            self.core, z, rest = low, list(range(low)), list(range(low + 1, bits))
        else:
            self.core, z, rest = 0, list(range(1, low)), list(range(low, bits))
        a, b = rest[:len(rest) // 2], rest[len(rest) // 2:]
        self.stages = [(a, b), (b, a), (z, z)]
        self.third = len(z) == low

    def masks(self, stage, core):
        bits = self.stages[stage][core]
        return [sum(1 << b for k, b in enumerate(bits) if j >> k & 1) for j in range(1 << len(bits))]

    def pairs(self, stage, j):
        return [(i, i ^ self.masks(stage, i >> self.core & 1)[j]) for i in range(self.total)]

    def size(self, stage):
        return 1 << len(self.stages[stage][0])

    def places(self, me, fixed=False):
        shard = lax.iota(jnp.int32, self.total)
        rel = shard ^ me
        core = (shard >> self.core) & 1
        pos = (rel >> self.core) & 1
        for k, (a, b) in enumerate(self.stages):
            pick = lambda bits, v: sum((((v >> bit) & 1) << k) for k, bit in enumerate(bits))
            own = pick(a, shard) if fixed and k == 2 else jnp.where(core == 0, pick(a, rel), pick(b, rel))
            pos = (pos << len(a)) + own
        return pos

AXES = ("dp", "fsdp")

def swap_core(plan, x):
    return lax.ppermute(x, AXES, [(i, i ^ (1 << plan.core)) for i in range(plan.total)])

def exchange(plan, x, stage, j):
    return lax.ppermute(x, AXES, plan.pairs(stage, j))

class Gathering:
    def __init__(self, plan, shard):
        self.plan, self.shard = plan, shard
        self.arrays = [exchange(plan, shard, 2, j) for j in range(1, plan.size(2))]

    def spread(self):
        column = jnp.stack([self.shard] + self.arrays)
        self.near = [exchange(self.plan, column, 1, j) for j in range(1, self.plan.size(1))]
        self.far = [exchange(self.plan, column, 0, j) for j in range(1, self.plan.size(0))]
        self.arrays = [column] + self.near + self.far

    def spread_again(self):
        n = self.plan.size(1)
        near, far = self.arrays[:n], self.arrays[n:]
        rest = [[exchange(self.plan, p, 0, j + 1) for p in near[1:]] for j in range(len(far))]
        other = [swap_core(self.plan, p) for p in self.arrays]
        self.first, self.other, self.arrays = self.arrays, other, [p for row in rest for p in row]

    def finish(self):
        n = self.plan.size(1)
        sides = (self.first, self.arrays), (self.other, [swap_core(self.plan, p) for p in self.arrays])
        pieces = []
        for first, rest in sides:
            pieces += first[:n]
            for j in range(self.plan.size(0) - 1):
                pieces += [first[n + j]] + rest[j * (n - 1):(j + 1) * (n - 1)]
        return pieces

def step(x, after, *reductions):
    x, _ = tie(x, after, *reductions)
    reductions = [r for r in reductions if r.stage < 3]
    if reductions:
        for r in reductions:
            r.add()
        x, = tie(x, *reductions)
        for r in reductions:
            r.go()
    return x

class Reduction:
    def __init__(self, plan, keep, send, one=False):
        self.plan, self.stage, self.size, self.one = plan, 0, keep.shape[0], one and plan.third
        self.terms = [keep, swap_core(plan, send)]
        self.sent = []

    def add(self):
        n = self.plan.size(self.stage)
        part = self.size // n
        if self.one and self.stage == 2:
            self.sent = [sum(t[:n].astype(f32) for t in self.terms).astype(self.terms[0].dtype)]
            return
        self.sent = [sum(t[j * part:(j + 1) * part].astype(f32) for t in self.terms).astype(self.terms[0].dtype) for j in range(1, n)]

    def go(self):
        if self.one and self.stage == 2:
            self.terms = [lax.psum_scatter(self.sent[0], AXES[1], scatter_dimension=0, tiled=False)[None]]
        else:
            self.terms = self.terms + [exchange(self.plan, s, self.stage, j + 1) for j, s in enumerate(self.sent)]
        self.sent = []
        self.size //= self.plan.size(self.stage)
        self.stage += 1

    def finish(self):
        while self.stage < 3:
            self.add()
            self.go()
        return sum(t[0].astype(f32) for t in self.terms)

def tie(*trees):
    flat = []
    for t in trees:
        flat += t.terms + t.sent if isinstance(t, Reduction) else t.arrays if isinstance(t, Gathering) else [t]
    flat = list(lax.optimization_barrier(tuple(flat)))
    out = []
    for t in trees:
        if isinstance(t, Reduction):
            t.terms = [flat.pop(0) for _ in t.terms]
            t.sent = [flat.pop(0) for _ in t.sent]
        elif isinstance(t, Gathering):
            t.arrays = [flat.pop(0) for _ in t.arrays]
        else:
            out.append(flat.pop(0))
    return out

def body(plan, tokens, prefix_len, padding_len, first_gain, first_shift, inproj_weight, query_bias, value_bias,
         outproj_weight, outproj_bias, second_gain, second_shift, up_weight, up_bias, down_weight, down_bias, grad_out):
    total = plan.total
    R, D = tokens.shape
    F = up_weight.shape[1]
    rows = D // total
    blocks = F // D
    me = lax.axis_index(AXES)
    pos = plan.places(me)
    pos_one = plan.places(me, plan.third)
    shard = lax.iota(jnp.int32, total)
    order = jnp.sum(jnp.where(pos[None, :] == shard[:, None], shard[None, :], 0), axis=1)
    n = first_gain.shape[0]
    half = blocks // 2
    up_local = up_weight.reshape(rows, total, blocks, rows).transpose(0, 2, 1, 3).reshape(rows, F)
    down_local = [down_weight[b * rows:(b + 1) * rows] for b in range(blocks)]
    small = jnp.concatenate([first_gain, first_shift, query_bias, value_bias, outproj_bias, second_gain, second_shift, down_bias, up_bias])
    small = jnp.pad(small.reshape(8 + blocks, rows).T, ((0, 0), (0, 128 - 8 - blocks)))
    inward = Gathering(plan, jnp.concatenate([inproj_weight, outproj_weight, small], axis=1))
    wide = lax.all_gather(jnp.concatenate([up_local] + down_local, axis=1), AXES, axis=0, tiled=True)
    stats = norm(tokens)
    stats, = tie(stats, inward)
    inward.spread()
    stats, = tie(stats, inward)
    inward.spread_again()
    stats, *inward.other = tie(stats, *inward.other, inward)
    inward = inward.finish()
    n1, qkv, vecs = project(order, tokens, stats, inward)
    ctx, lse = attend(prefix_len, padding_len, qkv)
    resid, n2, w_out = branch(order, ctx, tokens, vecs, inward)
    cut = D // 2
    n_pairs = D // 128
    def back(first, x, earlier=()):
        return attend_back(prefix_len, padding_len, qkv, x, ctx, lse, first, n_pairs // 4, cut, earlier)
    out, low, dctx, keep1, send1, keep2, send2, ubias_grad, mid = ffn(pos_one, n2, grad_out, vecs, wide, resid, w_out)
    g1 = Reduction(plan, keep1, send1, True)
    g2 = Reduction(plan, keep2, send2, True)
    d1 = back(0, dctx)
    dctx = step(dctx, d1[0], g1)
    d1 = back(n_pairs // 4, dctx, d1)
    n1a = step(n1, d1[0], g2)
    g3 = Reduction(plan, *weight_grad(pos, n1a, d1[0], ctx, low))
    dctx, _ = tie(dctx, g3.terms[0])
    d2 = back(n_pairs // 2, dctx)
    dctx = step(dctx, d2[0], g1)
    d2 = back(n_pairs * 3 // 4, dctx, d2)
    n1b = step(n1, d2[0], g2, g1)
    per = lambda v: v.reshape(total, -1)
    att = jnp.concatenate([d1[1], d2[1]], axis=1)
    ubg = ubias_grad.reshape(blocks, total, rows).transpose(1, 0, 2).reshape(total, -1)
    early = jnp.concatenate([per(att[0]), per(att[1]), per(mid[2]), per(mid[0]), per(mid[1]), per(mid[3]), ubg], axis=1)
    early = jnp.pad(early, ((0, 0), (0, cut - early.shape[1])))
    g4 = Reduction(plan, *weight_grad(pos, n1b, d2[0], small=early))
    da = step(d1[0], g4.terms[0], g3, g2)
    part = cotangent(order, da, inward, 0)
    part = step(part, part, g4)
    tokens_grad, end = cotangent(order, d2[0], inward, 1, part, stats, vecs, tokens, low)
    bits = [plan.core] + [bit for bit in range(total.bit_length() - 1) if bit != plan.core]
    swap = lambda v, bit: lax.ppermute(v, AXES, [(i, i ^ (1 << bit)) for i in range(total)])
    end = step(end[:2], end, g4)
    other = swap(end, bits[0])
    end = step(end, end, g3, g1)
    end, other = tie(end, other, g4)
    g4.add()
    g4.go()
    arriving = plan.size(2) - 1
    for k, bit in enumerate(bits[1:]):
        end = end + other
        other = swap(end, bit)
        if k < arriving:
            at = k - arriving
            other, g4.terms[at] = tie(other, g4.terms[at])
        if k == 0:
            other = step(other, other, g3)
    late = lax.dynamic_slice_in_dim(end + other, me * n, n, axis=1)
    in1, in2 = g3.finish(), g4.finish()
    up_grad, down_grad = owned([g1.terms, g2.terms], D, blocks)
    out_grad = jnp.concatenate([in1[3 * rows:4 * rows], in1[4 * rows:]], axis=1)
    in_grad = jnp.concatenate([g[k * rows:(k + 1) * rows] for k in range(3) for g in (in1, in2)], axis=1)
    early = in2[3 * rows]
    e = [early[i * n:(i + 1) * n] for i in range(6)]
    return (out, tokens_grad, late[0], late[1], in_grad, e[0], e[1], out_grad, e[2], e[3], e[4], up_grad, early[6 * n:6 * n + F // total], down_grad, e[5])

def solution(mesh):
    plan = Plan(mesh.shape["dp"], mesh.shape["fsdp"])
    rows, flat = P(AXES, None), P(AXES)
    ins = (rows, flat, flat, flat, flat, rows, flat, flat, rows, flat, flat, flat, rows, flat, rows, flat, rows)
    outs = (rows, rows, flat, flat, rows, flat, flat, rows, flat, flat, flat, rows, flat, rows, flat)
    return jax.shard_map(functools.partial(body, plan), mesh=mesh, in_specs=ins, out_specs=outs, check_vma=False)
```

```python
import functools, math
import jax, jax.numpy as jnp
from jax import lax
from jax.sharding import PartitionSpec as P
from jax.experimental import pallas as pl
from jax.experimental.pallas import tpu as pltpu
HEADS=16
EPSILON = 1e-05
NEGATIVE = -1000000000.0
bf16=jnp.bfloat16; f32=jnp.float32
VMEM_LIMIT=60*1024*1024
HINT=pl.CostEstimate(flops=1000, bytes_accessed=1000, transcendentals=0)
def cp(n=1): return pltpu.CompilerParams(dimension_semantics=("arbitrary",)*n, vmem_limit_bytes=VMEM_LIMIT)
def dot(a,b): return lax.dot_general(a,b,(((1,),(0,)),((),())),preferred_element_type=f32)
def dot_nt(a,b): return lax.dot_general(a,b,(((1,),(1,)),((),())),preferred_element_type=f32)
def dot_tn(a,b): return lax.dot_general(a,b,(((0,),(0,)),((),())),preferred_element_type=f32)

GAIN1, SHIFT1, QBIAS, VBIAS, OBIAS, GAIN2, SHIFT2, DBIAS, UBIAS = range(9)

def row_of(ref, k):
    return ref[k:k + 1, :]

def norm_kernel(tokens_ref, out_ref):
    x = tokens_ref[...].astype(f32)
    mean = jnp.mean(x, axis=-1, keepdims=True)
    center = x - mean
    r = lax.rsqrt(jnp.mean(center * center, axis=-1, keepdims=True) + EPSILON)
    lane = lax.broadcasted_iota(jnp.int32, out_ref.shape, 1)
    out_ref[...] = jnp.where(lane == 0, mean, r)

def norm(tokens, tm=256):
    R, D = tokens.shape
    return pl.pallas_call(
        norm_kernel, grid=(R // tm,), in_specs=[pl.BlockSpec((tm, D), lambda i: (i, 0))], out_specs=pl.BlockSpec((tm, 128), lambda i: (i, 0)),
        out_shape=jax.ShapeDtypeStruct((R, 128), f32), compiler_params=cp(), name="norm", cost_estimate=HINT,
    )(tokens)

def in_order(order_ref, pieces, whole_ref):
    n, rows, _ = pieces[0].shape
    for p, piece in enumerate(pieces):
        for i in range(n):
            whole_ref[pl.ds(pl.multiple_of(order_ref[p * n + i] * rows, rows), rows), :] = piece[i]

def project_kernel(order_ref, tokens_ref, stat_ref, *refs, count):
    pieces, sides = refs[:count], refs[count:2 * count]
    normed_ref, out_ref, vec_ref, weight_ref, side_ref, all_ref = refs[2 * count:]
    step = pl.program_id(0)
    @pl.when(step == 0)
    def _():
        in_order(order_ref, sides, side_ref)
        all_ref[...] = jnp.transpose(side_ref[...].astype(f32))
        vec_ref[...] = all_ref[:16, :]
        xhat = (tokens_ref[...].astype(f32) - stat_ref[:, 0:1]) * stat_ref[:, 1:2]
        normed_ref[...] = (xhat * all_ref[GAIN1:GAIN1 + 1, :] + all_ref[SHIFT1:SHIFT1 + 1, :]).astype(bf16)
    in_order(order_ref, pieces, weight_ref)
    D = normed_ref.shape[1]
    tn = out_ref.shape[1]
    third = pl.num_programs(0) // 3
    at = pl.ds(pl.multiple_of(lax.rem(step, D // tn) * tn, tn), tn)
    bias = jnp.where(step < third, all_ref[QBIAS:QBIAS + 1, at], jnp.where(step < 2 * third, 0.0, all_ref[VBIAS:VBIAS + 1, at]))
    factor = jnp.where(step < third, 0.125, 1.0)
    out = dot(normed_ref[...], weight_ref[...]) + bias
    out_ref[...] = (out * factor).astype(bf16)

def project(order, tokens, stats, pieces, tn=512):
    R, D = tokens.shape
    n, rows, width = pieces[0].shape
    N = 3 * D
    full = pl.BlockSpec((R, D), lambda j: (0, 0))
    return pl.pallas_call(
        functools.partial(project_kernel, count=len(pieces)), grid=(N // tn,),
        in_specs=[pl.BlockSpec(memory_space=pltpu.SMEM), full, pl.BlockSpec((R, 128), lambda j: (0, 0))]
        + [pl.BlockSpec((n, rows, tn), lambda j: (0, 0, j))] * len(pieces)
        + [pl.BlockSpec((n, rows, 128), lambda j: (0, 0, width // 128 - 1))] * len(pieces),
        out_specs=[full, pl.BlockSpec((R, tn), lambda j: (0, j)), pl.BlockSpec((16, D), lambda j: (0, 0))],
        out_shape=[jax.ShapeDtypeStruct((R, D), bf16), jax.ShapeDtypeStruct((R, N), bf16), jax.ShapeDtypeStruct((16, D), f32)],
        scratch_shapes=[pltpu.VMEM((D, tn), bf16), pltpu.VMEM((D, 128), bf16), pltpu.VMEM((128, D), f32)],
        compiler_params=cp(), name="project", cost_estimate=HINT,
    )(order, tokens, stats, *pieces, *pieces)

def key_bias(prefix, limit, lo, q0, bq, transposed, diagonal):
    shape = (bq, bq)
    kd = 0 if transposed else 1
    k = lo + lax.broadcasted_iota(jnp.int32, shape, kd)
    ok = k < limit
    if diagonal:
        q = q0 + lax.broadcasted_iota(jnp.int32, shape, 1 - kd)
        ok = ok & ((k < prefix) | (k <= q))
    return jnp.where(ok, 0.0, NEGATIVE)

def attend_kernel(prefix_ref, padding_ref, q_ref, k_ref, v_ref, out_ref, lse_ref, bias_ref, *, bq):
    L = q_ref.shape[0]
    step = pl.program_id(0)
    prefix = prefix_ref[0]
    limit = L - padding_ref[0]
    n = L // bq
    lane = lax.broadcasted_iota(jnp.int32, (1, 128), 1)
    @pl.when(step == 0)
    def _():
        for b in range(n):
            bias_ref[b] = key_bias(prefix, limit, b * bq, b * bq, bq, True, True)
    vT = jnp.transpose(v_ref[...])
    ones = jnp.ones((16, L), bf16)
    values = [jnp.concatenate([vT[64 * h:64 * h + 64], ones], axis=0) for h in range(2)]
    for b in range(n):
        start, stop = b * bq, (b + 1) * bq
        q = q_ref[start:stop, :]
        both = jnp.concatenate([jnp.where(lane < 64, q, 0), jnp.where(lane >= 64, q, 0)], axis=0).astype(bf16)
        s = []
        for kb in range(b + 1):
            t = dot_nt(k_ref[kb * bq:(kb + 1) * bq, :], both)
            if kb == b:
                t = t + jnp.concatenate([bias_ref[b], bias_ref[b]], axis=1)
            elif (kb + 1) * bq > L - 384:
                kk = kb * bq + lax.broadcasted_iota(jnp.int32, (bq, 1), 0)
                t = t + jnp.where(kk < limit, 0.0, NEGATIVE)
            s.append(t)
        m = functools.reduce(jnp.maximum, [jnp.max(t, axis=0, keepdims=True) for t in s])
        acc = [None, None]
        for kb in range(b + 1):
            e = jnp.exp(s[kb] - m).astype(bf16)
            for h in range(2):
                t = dot(values[h][:, kb * bq:(kb + 1) * bq], e[:, h * bq:(h + 1) * bq])
                acc[h] = t if acc[h] is None else acc[h] + t
        ctx = [a[:64] * (1.0 / a[64:65]) for a in acc]
        out_ref[start:stop, :] = jnp.transpose(jnp.concatenate(ctx, axis=0)).astype(bf16)
        for h in range(2):
            lse_ref[pl.ds(2 * step + h, 1), start:stop] = m[:, h * bq:(h + 1) * bq] + jnp.log(acc[h][64:65])

def attend(prefix, padding, qkv, bq=256):
    L = qkv.shape[0]
    D = qkv.shape[1] // 3
    n = D // 128
    smem = pl.BlockSpec(memory_space=pltpu.SMEM)
    col = lambda off: pl.BlockSpec((L, 128), lambda j: (0, j + off))
    return pl.pallas_call(
        functools.partial(attend_kernel, bq=bq), grid=(n,),
        in_specs=[smem, smem, col(0), col(n), col(2 * n)],
        out_specs=[col(0), pl.BlockSpec((2 * n, L), lambda j: (0, 0))],
        out_shape=[jax.ShapeDtypeStruct((L, D), bf16), jax.ShapeDtypeStruct((2 * n, L), f32)],
        scratch_shapes=[pltpu.VMEM((L // bq, bq, bq), f32)],
        compiler_params=cp(), name="attend",
        cost_estimate=HINT,
    )(prefix, padding, qkv, qkv, qkv)

def branch_kernel(order_ref, ctx_ref, tokens_ref, vec_ref, *refs):
    *pieces, resid_ref, normed_ref, weight_ref = refs
    @pl.when(pl.program_id(0) == 0)
    def _():
        in_order(order_ref, pieces, weight_ref)
    resid = tokens_ref[...].astype(f32) + (dot(ctx_ref[...], weight_ref[...]) + row_of(vec_ref, OBIAS))
    center = resid - jnp.mean(resid, axis=-1, keepdims=True)
    spread = jnp.mean(center * center, axis=-1, keepdims=True)
    normed = center * lax.rsqrt(spread + EPSILON) * row_of(vec_ref, GAIN2) + row_of(vec_ref, SHIFT2)
    resid_ref[...] = resid
    normed_ref[...] = normed.astype(bf16)

def branch(order, ctx, tokens, vecs, pieces, tm=256):
    R, D = ctx.shape
    n, high, _ = pieces[0].shape
    rows = pl.BlockSpec((tm, D), lambda i: (i, 0))
    return pl.pallas_call(
        branch_kernel, grid=(R // tm,),
        in_specs=[pl.BlockSpec(memory_space=pltpu.SMEM), rows, rows, pl.BlockSpec(vecs.shape, lambda i: (0, 0))]
        + [pl.BlockSpec((n, high, D), lambda i: (0, 0, 3))] * len(pieces),
        out_specs=[rows, rows, pl.BlockSpec((D, D), lambda i: (0, 0))],
        out_shape=[jax.ShapeDtypeStruct((R, D), f32), jax.ShapeDtypeStruct((R, D), bf16), jax.ShapeDtypeStruct((D, D), bf16)],
        compiler_params=cp(), name="branch", cost_estimate=HINT,
    )(order, ctx, tokens, vecs, *pieces)

def ffn_kernel(pos_ref, normed_ref, grad_ref, vec_ref, rows_ref, up_ref, down_ref, resid_in, weight_in,
               result_out, low_out, dctx_out, keep1_ref, send1_ref, keep2_ref, send2_ref, biasg_ref, small_ref,
               out_ref, dn_ref, ups_ref, dns_ref, resid_ref, weight_ref, result_ref, low_ref, dctx_ref, up_sem, dn_sem, in_sem, out_sem, *, shards, per, blocks, tm):
    step = pl.program_id(0)
    last = pl.num_programs(0) - 1
    D = normed_ref.shape[1]
    tf = ups_ref.shape[3]
    half = shards // 2
    rows = D // shards
    each = blocks // 2
    slot = lax.rem(step, 2)
    block = lax.div(step, per)
    bslot = lax.rem(block, 2)
    groups = ((keep1_ref, send1_ref), (keep2_ref, send2_ref))

    def up_copies(slot, step, group):
        cols = pl.ds(pl.multiple_of(step * tf - group * each * D, tf), tf)
        return [pltpu.make_async_copy(ups_ref.at[slot, pl.ds(k * half, half)], groups[group][k].at[:, :, cols], up_sem.at[slot, k]) for k in range(2)]

    def down_copies(bslot, block, group):
        cols = pl.ds(pl.multiple_of((each + block - group * each) * D, D), D)
        return [pltpu.make_async_copy(dns_ref.at[bslot, pl.ds(k * half, half)], groups[group][k].at[:, :, cols], dn_sem.at[bslot, k]) for k in range(2)]

    def each_group(block, do):
        for group in range(2):
            pl.when((block >= group * each) & (block < (group + 1) * each))(functools.partial(do, group))

    def start_up(group):
        for c in up_copies(slot, step, group):
            c.start()

    def wait_up(slot, step):
        def do(group):
            for c in up_copies(slot, step, group):
                c.wait()
        each_group(lax.div(step, per), do)

    def start_down(group):
        for c in down_copies(bslot, block, group):
            c.start()

    def wait_down(bslot, block):
        def do(group):
            for c in down_copies(bslot, block, group):
                c.wait()
        each_group(block, do)

    loads = [pltpu.make_async_copy(resid_in, resid_ref, in_sem.at[0]), pltpu.make_async_copy(weight_in, weight_ref, in_sem.at[1])]

    @pl.when(step == 0)
    def _():
        for c in loads:
            c.start()
        out_ref[...] = jnp.zeros_like(out_ref)
        dn_ref[...] = jnp.zeros_like(dn_ref)

    @pl.when(step >= 2)
    def _():
        wait_up(slot, step - 2)

    @pl.when((step >= 2 * per) & (lax.rem(step, per) == 0))
    def _():
        wait_down(bslot, block - 2)

    n2 = normed_ref[...]
    go = grad_ref[...]
    up = up_ref[...]
    down = down_ref[...]
    bias = row_of(vec_ref, UBIAS)
    for k in range(1, blocks):
        bias = jnp.where(block == k, row_of(vec_ref, UBIAS + k), bias)
    u = dot(n2, up) + bias
    cdf = 0.5 * (1.0 + lax.erf(u * math.sqrt(0.5)))
    a = (u * cdf).astype(bf16)
    slope = cdf + u * (jnp.exp(-0.5 * u * u) * (1.0 / math.sqrt(2 * math.pi)))
    du = (dot_nt(go, down) * slope).astype(bf16)
    out_ref[...] += dot(a, down)
    dn_ref[...] += dot_nt(du, up)
    biasg_ref[...] = jnp.sum(du.astype(f32), axis=0, keepdims=True)
    upg = dot_tn(n2, du).astype(bf16)
    for i in range(shards):
        ups_ref[slot, pos_ref[i]] = upg[i * rows:(i + 1) * rows]
    downg = dot_tn(a, go).astype(bf16)
    here = tf // rows
    at = lax.rem(step, per) * here
    for i in range(here):
        dns_ref[bslot, pos_ref[at + i]] = downg[i * rows:(i + 1) * rows]
    each_group(block, start_up)

    @pl.when(lax.rem(step, per) == per - 1)
    def _():
        each_group(block, start_down)

    @pl.when(step == last)
    def _():
        for c in loads:
            c.wait()
        small_ref[...] = jnp.zeros_like(small_ref)
        pairs = ((result_ref, result_out), (low_ref, low_out), (dctx_ref, dctx_out))

        def stores(i):
            at = pl.ds(pl.multiple_of(i * tm, tm), tm)
            return [pltpu.make_async_copy(here.at[at], there.at[at], out_sem.at[i, k]) for k, (here, there) in enumerate(pairs)]

        def tile(i, carry):
            at = pl.ds(pl.multiple_of(i * tm, tm), tm)
            resid = resid_ref[at, :]
            result_ref[at, :] = (resid + out_ref[at, :] + row_of(rows_ref, DBIAS)).astype(bf16)
            center = resid - jnp.mean(resid, axis=-1, keepdims=True)
            r = lax.rsqrt(jnp.mean(center * center, axis=-1, keepdims=True) + EPSILON)
            nhat = center * r
            dn = dn_ref[at, :]
            go = grad_ref[at, :].astype(f32)
            e = dn * row_of(rows_ref, GAIN2)
            low = (go + r * (e - jnp.mean(e, axis=-1, keepdims=True) - nhat * jnp.mean(e * nhat, axis=-1, keepdims=True))).astype(bf16)
            low_ref[at, :] = low
            dctx_ref[at, :] = dot_nt(low, weight_ref[...]).astype(bf16)
            small_ref[0:1, :] += jnp.sum(dn * nhat, axis=0, keepdims=True)
            small_ref[1:2, :] += jnp.sum(dn, axis=0, keepdims=True)
            small_ref[2:3, :] += jnp.sum(low.astype(f32), axis=0, keepdims=True)
            small_ref[3:4, :] += jnp.sum(go, axis=0, keepdims=True)
            for c in stores(i):
                c.start()
            return carry

        tiles = resid_ref.shape[0] // tm
        lax.fori_loop(0, tiles, tile, 0)
        for i in range(tiles):
            for c in stores(i):
                c.wait()
        for c in up_copies(1 - slot, step - 1, 1) + up_copies(slot, step, 1) + down_copies(1 - bslot, block - 1, 1) + down_copies(bslot, block, 1):
            c.wait()

def ffn(pos, normed, grad, vecs, wide, resid, weight, tf=512, tm=256):
    R, D = normed.shape
    blocks = wide.shape[1] // D // 2
    F = blocks * D
    shards = pos.shape[0]
    rows = D // shards
    per = D // tf
    full = pl.BlockSpec((R, D), lambda j: (0, 0))
    hbm = pl.BlockSpec(memory_space=pl.ANY)
    part = jax.ShapeDtypeStruct((shards // 2, rows, F), bf16)
    low = jax.ShapeDtypeStruct((R, D), bf16)
    return pl.pallas_call(
        functools.partial(ffn_kernel, shards=shards, per=per, blocks=blocks, tm=tm), grid=(F // tf,),
        in_specs=[pl.BlockSpec(memory_space=pltpu.SMEM), full, full, pl.BlockSpec((16, tf), lambda j: (0, lax.rem(j, per))), pl.BlockSpec((16, D), lambda j: (0, 0)),
                  pl.BlockSpec((D, tf), lambda j: (0, j)), pl.BlockSpec((tf, D), lambda j: (lax.rem(j, per), blocks + lax.div(j, per))), hbm, hbm],
        out_specs=[hbm] * 7 + [pl.BlockSpec((1, tf), lambda j: (0, j)), pl.BlockSpec((8, D), lambda j: (0, 0))],
        out_shape=[low, low, low, part, part, part, part, jax.ShapeDtypeStruct((1, F), f32), jax.ShapeDtypeStruct((8, D), f32)],
        scratch_shapes=[pltpu.VMEM((R, D), f32), pltpu.VMEM((R, D), f32), pltpu.VMEM((2, shards, rows, tf), bf16), pltpu.VMEM((2, shards, rows, D), bf16),
                        pltpu.VMEM((R, D), f32), pltpu.VMEM((D, D), bf16), pltpu.VMEM((R, D), bf16), pltpu.VMEM((R, D), bf16), pltpu.VMEM((R, D), bf16),
                        pltpu.SemaphoreType.DMA((2, 2)), pltpu.SemaphoreType.DMA((2, 2)), pltpu.SemaphoreType.DMA((2,)), pltpu.SemaphoreType.DMA((R // tm, 3))],
        compiler_params=cp(), name="ffn", cost_estimate=HINT,
    )(pos, normed, grad, vecs, vecs, wide, wide, resid, weight)

def attend_back_kernel(prefix_ref, padding_ref, q_ref, k_ref, v_ref, do_ref, o_ref, lse_ref, *refs, bq, first):
    d_ref, small_ref, dka_ref, dva_ref, bias_ref = refs[-5:]
    L = q_ref.shape[0]
    step = pl.program_id(0) + first
    prefix = prefix_ref[0]
    limit = L - padding_ref[0]
    n = L // bq
    lane = lax.broadcasted_iota(jnp.int32, (1, 128), 1)
    @pl.when(pl.program_id(0) == 0)
    def _():
        for b in range(n):
            bias_ref[b] = key_bias(prefix, limit, b * bq, b * bq, bq, True, True)
    kT = jnp.transpose(k_ref[...])
    prod = do_ref[...].astype(f32) * o_ref[...].astype(f32)
    row = lax.broadcasted_iota(jnp.int32, (8, 128), 0)
    col = lax.broadcasted_iota(jnp.int32, (8, 128), 1)
    pick = jnp.where((col // 64) == row, 1.0, 0.0)
    delta = lax.dot_general(pick, prod, (((1,), (1,)), ((), ())), precision=lax.Precision.HIGHEST, preferred_element_type=f32)
    for b in range(n):
        start, stop = b * bq, (b + 1) * bq
        q = q_ref[start:stop, :]
        do = do_ref[start:stop, :]
        both = jnp.concatenate([jnp.where(lane < 64, q, 0), jnp.where(lane >= 64, q, 0)], axis=0).astype(bf16)
        dboth = jnp.concatenate([jnp.where(lane < 64, do, 0), jnp.where(lane >= 64, do, 0)], axis=0).astype(bf16)
        lse = jnp.concatenate([lse_ref[pl.ds(2 * step, 1), start:stop], lse_ref[pl.ds(2 * step + 1, 1), start:stop]], axis=1)
        inner = jnp.concatenate([delta[0:1, start:stop], delta[1:2, start:stop]], axis=1)
        dq = [None, None]
        for kb in range(b + 1):
            ks = slice(kb * bq, (kb + 1) * bq)
            s = dot_nt(k_ref[ks, :], both)
            if kb == b:
                s = s + jnp.concatenate([bias_ref[b], bias_ref[b]], axis=1)
            elif (kb + 1) * bq > L - 384:
                kk = kb * bq + lax.broadcasted_iota(jnp.int32, (bq, 1), 0)
                s = s + jnp.where(kk < limit, 0.0, NEGATIVE)
            p = jnp.exp(s - lse)
            ds = (p * (dot_nt(v_ref[ks, :], dboth) - inner)).astype(bf16)
            tv = dot(p.astype(bf16), dboth)
            tk = dot(ds, both)
            if kb == b:
                dva_ref[ks, :] = tv
                dka_ref[ks, :] = tk
            else:
                dva_ref[ks, :] += tv
                dka_ref[ks, :] += tk
            for h in range(2):
                t = dot(kT[64 * h:64 * h + 64, ks], ds[:, h * bq:(h + 1) * bq])
                dq[h] = t if dq[h] is None else dq[h] + t
        d_ref[0, start:stop, :] = (jnp.transpose(jnp.concatenate(dq, axis=0)) * 0.125).astype(bf16)
    d_ref[1] = dka_ref[...].astype(bf16)
    d_ref[2] = dva_ref[...].astype(bf16)
    small_ref[0:1, :] = jnp.sum(d_ref[0].astype(f32), axis=0, keepdims=True)
    small_ref[1:2, :] = jnp.sum(d_ref[2].astype(f32), axis=0, keepdims=True)

def attend_back(prefix, padding, qkv, dctx, ctx, lse, first, count, width, earlier=(), bq=256):
    L = qkv.shape[0]
    D = dctx.shape[1]
    n = D // 128
    at = first % (width // 128)
    smem = pl.BlockSpec(memory_space=pltpu.SMEM)
    col = lambda off: pl.BlockSpec((L, 128), lambda j: (0, j + off))
    return pl.pallas_call(
        functools.partial(attend_back_kernel, bq=bq, first=first), grid=(count,),
        in_specs=[smem, smem, col(first), col(n + first), col(2 * n + first), col(first), col(first), pl.BlockSpec((2 * n, L), lambda j: (0, 0))]
        + [pl.BlockSpec(memory_space=pl.ANY)] * len(earlier),
        out_specs=[pl.BlockSpec((3, L, 128), lambda j: (0, 0, j + at)), pl.BlockSpec((8, 128), lambda j: (0, j + at))],
        out_shape=[jax.ShapeDtypeStruct((3, L, width), bf16), jax.ShapeDtypeStruct((8, width), f32)],
        scratch_shapes=[pltpu.VMEM((L, 128), f32), pltpu.VMEM((L, 128), f32), pltpu.VMEM((L // bq, bq, bq), f32)],
        input_output_aliases={8 + i: i for i in range(len(earlier))},
        compiler_params=cp(), name="attend_back",
        cost_estimate=HINT,
    )(prefix, padding, qkv, qkv, qkv, dctx, ctx, lse, *earlier)

def weight_grad_kernel(pos_ref, left_ref, d_ref, *refs, each, other, extra):
    refs = list(refs)
    if other:
        low_ref, second_in = refs[:2]
        refs = refs[2:]
    if extra:
        small_ref = refs.pop(0)
    keep_ref, send_ref, stage_ref, stage_sem = refs[:4]
    refs = refs[4:]
    if other:
        second_ref, second_sem = refs[:2]
        refs = refs[2:]
    if extra:
        extra_ref, extra_sem = refs
    step = pl.program_id(0)
    steps = 3 * each + other
    _, shards, rows, tn = stage_ref.shape
    half = shards // 2
    slot = lax.rem(step, 2)

    def copies(slot, step):
        high = pl.ds(pl.multiple_of(lax.div(step, each) * rows, rows), rows)
        cols = pl.ds(pl.multiple_of(lax.rem(step, each) * tn, tn), tn)
        return [pltpu.make_async_copy(stage_ref.at[slot, pl.ds(k * half, half)], out.at[:, high, cols], stage_sem.at[slot, k]) for k, out in enumerate((keep_ref, send_ref))]

    if extra:
        behind = [pltpu.make_async_copy(extra_ref.at[pl.ds(k * half, half)], out.at[:, pl.ds(3 * rows, extra), :], extra_sem.at[k]) for k, out in enumerate((keep_ref, send_ref))]
    if other:
        second = pltpu.make_async_copy(second_in, second_ref, second_sem.at[0])

    @pl.when(step == 0)
    def _():
        if other:
            second.start()
        if extra:
            for i in range(shards):
                extra_ref[pos_ref[i]] = jnp.broadcast_to(small_ref[i:i + 1, :], extra_ref.shape[1:]).astype(bf16)
            for c in behind:
                c.start()

    @pl.when(step >= 2)
    def _():
        for c in copies(slot, step - 2):
            c.wait()

    def put(value):
        for i in range(shards):
            stage_ref[slot, pos_ref[i]] = value[i * rows:(i + 1) * rows].astype(bf16)

    if other:
        @pl.when(step == 3 * each)
        def _():
            second.wait()

        @pl.when(step >= 3 * each)
        def _():
            put(dot_tn(second_ref[...], low_ref[...]))

        @pl.when(step < 3 * each)
        def _():
            put(dot_tn(left_ref[...], d_ref[0]))
    else:
        put(dot_tn(left_ref[...], d_ref[0]))
    for c in copies(slot, step):
        c.start()

    @pl.when(step == steps - 1)
    def _():
        for c in copies(1 - slot, step - 1) + copies(slot, step) + (behind if extra else []):
            c.wait()

def weight_grad(pos, left, d, second=None, low=None, small=None, tn=512):
    R, D = left.shape
    _, _, width = d.shape
    shards = pos.shape[0]
    rows = D // shards
    each = width // tn
    other = D // tn if second is not None else 0
    extra = min(rows, 16) if small is not None else 0
    high = (3 * each + other) // each * rows + extra
    half = jax.ShapeDtypeStruct((shards // 2, high, width), bf16)
    hbm = pl.BlockSpec(memory_space=pl.ANY)
    specs = [pl.BlockSpec(memory_space=pltpu.SMEM), pl.BlockSpec((R, D), lambda j: (0, 0)),
             pl.BlockSpec((1, R, tn), lambda j: (jnp.minimum(lax.div(j, each), 2), 0, jnp.where(j < 3 * each, lax.rem(j, each), each - 1)))]
    args = [pos, left, d]
    scratch = [pltpu.VMEM((2, shards, rows, tn), bf16), pltpu.SemaphoreType.DMA((2, 2))]
    if other:
        specs = specs + [pl.BlockSpec((R, tn), lambda j: (0, jnp.maximum(j - 3 * each, 0))), hbm]
        args = args + [low, second]
        scratch = scratch + [pltpu.VMEM((R, D), bf16), pltpu.SemaphoreType.DMA((1,))]
    if extra:
        specs = specs + [pl.BlockSpec((shards, width), lambda j: (0, 0))]
        args = args + [small]
        scratch = scratch + [pltpu.VMEM((shards, extra, width), bf16), pltpu.SemaphoreType.DMA((2,))]
    return pl.pallas_call(
        functools.partial(weight_grad_kernel, each=each, other=other, extra=extra), grid=(3 * each + other,),
        in_specs=specs, out_specs=[hbm, hbm], out_shape=[half, half], scratch_shapes=scratch,
        compiler_params=cp(), name="weight_grad", cost_estimate=HINT,
    )(*args)

def cotangent_kernel(order_ref, d_ref, *refs, count, final, tm):
    pieces, refs = refs[:count], refs[count:]
    step = pl.program_id(0)
    if final:
        stat_ref, vec_ref, earlier_in, tokens_in, low_in, out_ref, small_ref, weight_ref, acc_ref, earlier_ref, tokens_ref, low_ref, result_ref, in_sem, out_sem = refs
        loads = [pltpu.make_async_copy(a, b, in_sem.at[k]) for k, (a, b) in enumerate(((earlier_in, earlier_ref), (tokens_in, tokens_ref), (low_in, low_ref)))]
        @pl.when(step == 0)
        def _():
            for c in loads:
                c.start()
    else:
        out_ref, weight_ref, acc_ref = refs
    in_order(order_ref, pieces, weight_ref)
    term = dot_nt(d_ref[0], weight_ref[...])
    @pl.when(step == 0)
    def _():
        acc_ref[...] = term
    @pl.when(step > 0)
    def _():
        acc_ref[...] += term

    @pl.when(step == 2)
    def _():
        if not final:
            out_ref[...] = acc_ref[...].astype(bf16)
        else:
            for c in loads:
                c.wait()
            small_ref[...] = jnp.zeros_like(small_ref)
            gain = row_of(vec_ref, GAIN1)
            def store(i):
                at = pl.ds(pl.multiple_of(i * tm, tm), tm)
                return pltpu.make_async_copy(result_ref.at[at], out_ref.at[at], out_sem.at[i])

            def tile(i, carry):
                at = pl.ds(pl.multiple_of(i * tm, tm), tm)
                dn = acc_ref[at, :] + earlier_ref[at, :].astype(f32)
                r = stat_ref[at, 1:2]
                nhat = (tokens_ref[at, :].astype(f32) - stat_ref[at, 0:1]) * r
                e = dn * gain
                d = low_ref[at, :].astype(f32) + r * (e - jnp.mean(e, axis=-1, keepdims=True) - nhat * jnp.mean(e * nhat, axis=-1, keepdims=True))
                result_ref[at, :] = d.astype(bf16)
                small_ref[0:1, :] += jnp.sum(dn * nhat, axis=0, keepdims=True)
                small_ref[1:2, :] += jnp.sum(dn, axis=0, keepdims=True)
                store(i).start()
                return carry

            tiles = acc_ref.shape[0] // tm
            lax.fori_loop(0, tiles, tile, 0)
            for i in range(tiles):
                store(i).wait()

def cotangent(order, d, pieces, number, earlier=None, stats=None, vecs=None, tokens=None, low=None, tm=256):
    _, R, width = d.shape
    n, rows, _ = pieces[0].shape
    D = rows * n * len(pieces)
    per = D // width
    final = earlier is not None
    hbm = pl.BlockSpec(memory_space=pl.ANY)
    specs = [pl.BlockSpec(memory_space=pltpu.SMEM), pl.BlockSpec((1, R, width), lambda j: (j, 0, 0))]
    specs = specs + [pl.BlockSpec((n, rows, width), lambda j: (0, 0, j * per + number))] * len(pieces)
    scratch = [pltpu.VMEM((D, width), bf16), pltpu.VMEM((R, D), f32)]
    result = jax.ShapeDtypeStruct((R, D), bf16)
    more = ()
    if final:
        specs = specs + [pl.BlockSpec((R, 128), lambda j: (0, 0)), pl.BlockSpec(vecs.shape, lambda j: (0, 0)), hbm, hbm, hbm]
        more = (stats, vecs, earlier, tokens, low)
        outs, shapes = [hbm, pl.BlockSpec((8, D), lambda j: (0, 0))], [result, jax.ShapeDtypeStruct((8, D), f32)]
        scratch = scratch + [pltpu.VMEM((R, D), bf16)] * 4 + [pltpu.SemaphoreType.DMA((3,)), pltpu.SemaphoreType.DMA((R // tm,))]
    else:
        outs, shapes = pl.BlockSpec((R, D), lambda j: (0, 0)), result
    return pl.pallas_call(
        functools.partial(cotangent_kernel, count=len(pieces), final=final, tm=tm), grid=(3,),
        in_specs=specs, out_specs=outs, out_shape=shapes, scratch_shapes=scratch,
        compiler_params=cp(), name="cotangent", cost_estimate=HINT,
    )(order, d, *pieces, *more)

def owned_kernel(*refs, counts, rows, blocks, wide):
    parts, at = [], 0
    for c in counts:
        parts.append(sum(r[0].astype(f32) for r in refs[at:at + c]))
        at += c
    up_ref, down_ref = refs[at:]
    half = blocks // len(counts)
    D = down_ref.shape[1]
    for h, part in enumerate(parts):
        for b in range(half):
            down_ref[(h * half + b) * rows:(h * half + b + 1) * rows, :] = part[:, (half + b) * D:(half + b + 1) * D]
    per = D // rows
    group = blocks * rows
    lane = lax.broadcasted_iota(jnp.int32, (rows, 128), 1)
    for tile in range(blocks * D // 128):
        value = None
        for k in range(128 // rows):
            unit = (tile * 128 + k * rows) // rows
            shard, b = unit // blocks, unit % blocks
            source = (b % half) * D + shard * rows
            piece = parts[b // half][:, source // 128 * 128:source // 128 * 128 + 128]
            shift = (k * rows - source % 128) % 128
            if shift:
                piece = pltpu.roll(piece, shift, 1)
            value = piece if value is None else jnp.where(lane >= k * rows, piece, value)
        up_ref[:, tile * 128:(tile + 1) * 128] = value

def owned(groups, D, blocks):
    _, rows, width = groups[0][0].shape
    terms = [t for g in groups for t in g]
    return pl.pallas_call(
        functools.partial(owned_kernel, counts=[len(g) for g in groups], rows=rows, blocks=blocks, wide=width), grid=(1,),
        in_specs=[pl.BlockSpec((1, rows, width), lambda i: (0, 0, 0))] * len(terms),
        out_specs=[pl.BlockSpec((rows, blocks * D), lambda i: (0, 0)), pl.BlockSpec((blocks * rows, D), lambda i: (0, 0))],
        out_shape=[jax.ShapeDtypeStruct((rows, blocks * D), f32), jax.ShapeDtypeStruct((blocks * rows, D), f32)],
        compiler_params=cp(), name="owned", cost_estimate=HINT,
    )(*terms)


class Plan:
    def __init__(self, dp, fsdp):
        self.total = dp * fsdp
        bits = self.total.bit_length() - 1
        low = fsdp.bit_length() - 1
        if fsdp == 4:
            self.core, z, rest = low, list(range(low)), list(range(low + 1, bits))
        else:
            self.core, z, rest = 0, list(range(1, low)), list(range(low, bits))
        a, b = rest[:len(rest) // 2], rest[len(rest) // 2:]
        self.stages = [(a, b), (b, a), (z, z)]
        self.third = len(z) == low

    def masks(self, stage, core):
        bits = self.stages[stage][core]
        return [sum(1 << b for k, b in enumerate(bits) if j >> k & 1) for j in range(1 << len(bits))]

    def pairs(self, stage, j):
        return [(i, i ^ self.masks(stage, i >> self.core & 1)[j]) for i in range(self.total)]

    def size(self, stage):
        return 1 << len(self.stages[stage][0])

    def places(self, me, fixed=False):
        shard = lax.iota(jnp.int32, self.total)
        rel = shard ^ me
        core = (shard >> self.core) & 1
        pos = (rel >> self.core) & 1
        for k, (a, b) in enumerate(self.stages):
            pick = lambda bits, v: sum((((v >> bit) & 1) << k) for k, bit in enumerate(bits))
            own = pick(a, shard) if fixed and k == 2 else jnp.where(core == 0, pick(a, rel), pick(b, rel))
            pos = (pos << len(a)) + own
        return pos

AXES = ("dp", "fsdp")

def swap_core(plan, x):
    return lax.ppermute(x, AXES, [(i, i ^ (1 << plan.core)) for i in range(plan.total)])

def exchange(plan, x, stage, j):
    return lax.ppermute(x, AXES, plan.pairs(stage, j))

class Gathering:
    def __init__(self, plan, shard):
        self.plan, self.shard = plan, shard
        self.arrays = [exchange(plan, shard, 2, j) for j in range(1, plan.size(2))]

    def spread(self):
        column = jnp.stack([self.shard] + self.arrays)
        self.near = [exchange(self.plan, column, 1, j) for j in range(1, self.plan.size(1))]
        self.far = [exchange(self.plan, column, 0, j) for j in range(1, self.plan.size(0))]
        self.arrays = [column] + self.near + self.far

    def spread_again(self):
        n = self.plan.size(1)
        near, far = self.arrays[:n], self.arrays[n:]
        rest = [[exchange(self.plan, p, 0, j + 1) for p in near[1:]] for j in range(len(far))]
        other = [swap_core(self.plan, p) for p in self.arrays]
        self.first, self.other, self.arrays = self.arrays, other, [p for row in rest for p in row]

    def finish(self):
        n = self.plan.size(1)
        sides = (self.first, self.arrays), (self.other, [swap_core(self.plan, p) for p in self.arrays])
        pieces = []
        for first, rest in sides:
            pieces += first[:n]
            for j in range(self.plan.size(0) - 1):
                pieces += [first[n + j]] + rest[j * (n - 1):(j + 1) * (n - 1)]
        return pieces

def step(x, after, *reductions):
    x, _ = tie(x, after, *reductions)
    reductions = [r for r in reductions if r.stage < 3]
    if reductions:
        for r in reductions:
            r.add()
        x, = tie(x, *reductions)
        for r in reductions:
            r.go()
    return x

class Reduction:
    def __init__(self, plan, keep, send, one=False):
        self.plan, self.stage, self.size, self.one = plan, 0, keep.shape[0], one and plan.third
        self.terms = [keep, swap_core(plan, send)]
        self.sent = []

    def add(self):
        n = self.plan.size(self.stage)
        part = self.size // n
        if self.one and self.stage == 2:
            self.sent = [sum(t[:n].astype(f32) for t in self.terms).astype(self.terms[0].dtype)]
            return
        self.sent = [sum(t[j * part:(j + 1) * part].astype(f32) for t in self.terms).astype(self.terms[0].dtype) for j in range(1, n)]

    def go(self):
        if self.one and self.stage == 2:
            self.terms = [lax.psum_scatter(self.sent[0], AXES[1], scatter_dimension=0, tiled=False)[None]]
        else:
            self.terms = self.terms + [exchange(self.plan, s, self.stage, j + 1) for j, s in enumerate(self.sent)]
        self.sent = []
        self.size //= self.plan.size(self.stage)
        self.stage += 1

    def finish(self):
        while self.stage < 3:
            self.add()
            self.go()
        return sum(t[0].astype(f32) for t in self.terms)

def tie(*trees):
    flat = []
    for t in trees:
        flat += t.terms + t.sent if isinstance(t, Reduction) else t.arrays if isinstance(t, Gathering) else [t]
    flat = list(lax.optimization_barrier(tuple(flat)))
    out = []
    for t in trees:
        if isinstance(t, Reduction):
            t.terms = [flat.pop(0) for _ in t.terms]
            t.sent = [flat.pop(0) for _ in t.sent]
        elif isinstance(t, Gathering):
            t.arrays = [flat.pop(0) for _ in t.arrays]
        else:
            out.append(flat.pop(0))
    return out

def body(plan, tokens, prefix_len, padding_len, first_gain, first_shift, inproj_weight, query_bias, value_bias,
         outproj_weight, outproj_bias, second_gain, second_shift, up_weight, up_bias, down_weight, down_bias, grad_out):
    total = plan.total
    R, D = tokens.shape
    F = up_weight.shape[1]
    rows = D // total
    blocks = F // D
    me = lax.axis_index(AXES)
    pos = plan.places(me)
    pos_one = plan.places(me, plan.third)
    shard = lax.iota(jnp.int32, total)
    order = jnp.sum(jnp.where(pos[None, :] == shard[:, None], shard[None, :], 0), axis=1)
    n = first_gain.shape[0]
    half = blocks // 2
    up_local = up_weight.reshape(rows, total, blocks, rows).transpose(0, 2, 1, 3).reshape(rows, F)
    down_local = [down_weight[b * rows:(b + 1) * rows] for b in range(blocks)]
    small = jnp.concatenate([first_gain, first_shift, query_bias, value_bias, outproj_bias, second_gain, second_shift, down_bias, up_bias])
    small = jnp.pad(small.reshape(8 + blocks, rows).T, ((0, 0), (0, 128 - 8 - blocks)))
    inward = Gathering(plan, jnp.concatenate([inproj_weight, outproj_weight, small], axis=1))
    wide = lax.all_gather(jnp.concatenate([up_local] + down_local, axis=1), AXES, axis=0, tiled=True)
    stats = norm(tokens)
    stats, = tie(stats, inward)
    inward.spread()
    stats, = tie(stats, inward)
    inward.spread_again()
    stats, *inward.other = tie(stats, *inward.other, inward)
    inward = inward.finish()
    n1, qkv, vecs = project(order, tokens, stats, inward)
    ctx, lse = attend(prefix_len, padding_len, qkv)
    resid, n2, w_out = branch(order, ctx, tokens, vecs, inward)
    cut = D // 2
    n_pairs = D // 128
    def back(first, x, earlier=()):
        return attend_back(prefix_len, padding_len, qkv, x, ctx, lse, first, n_pairs // 4, cut, earlier)
    out, low, dctx, keep1, send1, keep2, send2, ubias_grad, mid = ffn(pos_one, n2, grad_out, vecs, wide, resid, w_out)
    g1 = Reduction(plan, keep1, send1, True)
    g2 = Reduction(plan, keep2, send2, True)
    d1 = back(0, dctx)
    dctx = step(dctx, d1[0], g1)
    d1 = back(n_pairs // 4, dctx, d1)
    n1a = step(n1, d1[0], g2)
    g3 = Reduction(plan, *weight_grad(pos, n1a, d1[0], ctx, low))
    dctx, _ = tie(dctx, g3.terms[0])
    d2 = back(n_pairs // 2, dctx)
    dctx = step(dctx, d2[0], g1)
    d2 = back(n_pairs * 3 // 4, dctx, d2)
    n1b = step(n1, d2[0], g2, g1)
    per = lambda v: v.reshape(total, -1)
    att = jnp.concatenate([d1[1], d2[1]], axis=1)
    ubg = ubias_grad.reshape(blocks, total, rows).transpose(1, 0, 2).reshape(total, -1)
    early = jnp.concatenate([per(att[0]), per(att[1]), per(mid[2]), per(mid[0]), per(mid[1]), per(mid[3]), ubg], axis=1)
    early = jnp.pad(early, ((0, 0), (0, cut - early.shape[1])))
    g4 = Reduction(plan, *weight_grad(pos, n1b, d2[0], small=early))
    da = step(d1[0], g4.terms[0], g3, g2)
    part = cotangent(order, da, inward, 0)
    part = step(part, part, g4, g1)
    tokens_grad, end = cotangent(order, d2[0], inward, 1, part, stats, vecs, tokens, low)
    bits = [plan.core] + [bit for bit in range(total.bit_length() - 1) if bit != plan.core]
    swap = lambda v, bit: lax.ppermute(v, AXES, [(i, i ^ (1 << bit)) for i in range(total)])
    end = step(end[:2], end, g4)
    other = swap(end, bits[0])
    end = step(end, end, g3)
    end, other = tie(end, other, g4)
    g4.add()
    g4.go()
    arriving = plan.size(2) - 1
    for k, bit in enumerate(bits[1:]):
        end = end + other
        other = swap(end, bit)
        if k < arriving:
            at = k - arriving
            other, g4.terms[at] = tie(other, g4.terms[at])
        if k == 0:
            other = step(other, other, g3, g2)
    late = lax.dynamic_slice_in_dim(end + other, me * n, n, axis=1)
    in1, in2 = g3.finish(), g4.finish()
    up_grad, down_grad = owned([g1.terms, g2.terms], D, blocks)
    out_grad = jnp.concatenate([in1[3 * rows:4 * rows], in1[4 * rows:]], axis=1)
    in_grad = jnp.concatenate([g[k * rows:(k + 1) * rows] for k in range(3) for g in (in1, in2)], axis=1)
    early = in2[3 * rows]
    e = [early[i * n:(i + 1) * n] for i in range(6)]
    return (out, tokens_grad, late[0], late[1], in_grad, e[0], e[1], out_grad, e[2], e[3], e[4], up_grad, early[6 * n:6 * n + F // total], down_grad, e[5])

def solution(mesh):
    plan = Plan(mesh.shape["dp"], mesh.shape["fsdp"])
    rows, flat = P(AXES, None), P(AXES)
    ins = (rows, flat, flat, flat, flat, rows, flat, flat, rows, flat, flat, flat, rows, flat, rows, flat, rows)
    outs = (rows, rows, flat, flat, rows, flat, flat, rows, flat, flat, flat, rows, flat, rows, flat)
    return jax.shard_map(functools.partial(body, plan), mesh=mesh, in_specs=ins, out_specs=outs, check_vma=False)
```

```python
import functools, math
import jax, jax.numpy as jnp
from jax import lax
from jax.sharding import PartitionSpec as P
from jax.experimental import pallas as pl
from jax.experimental.pallas import tpu as pltpu
HEADS=16
EPSILON = 1e-05
NEGATIVE = -1000000000.0
bf16=jnp.bfloat16; f32=jnp.float32
VMEM_LIMIT=60*1024*1024
HINT=pl.CostEstimate(flops=1000, bytes_accessed=1000, transcendentals=0)
def cp(n=1): return pltpu.CompilerParams(dimension_semantics=("arbitrary",)*n, vmem_limit_bytes=VMEM_LIMIT)
def dot(a,b): return lax.dot_general(a,b,(((1,),(0,)),((),())),preferred_element_type=f32)
def dot_nt(a,b): return lax.dot_general(a,b,(((1,),(1,)),((),())),preferred_element_type=f32)
def dot_tn(a,b): return lax.dot_general(a,b,(((0,),(0,)),((),())),preferred_element_type=f32)

GAIN1, SHIFT1, QBIAS, VBIAS, OBIAS, GAIN2, SHIFT2, DBIAS, UBIAS = range(9)

def row_of(ref, k):
    return ref[k:k + 1, :]

def norm_kernel(tokens_ref, out_ref):
    x = tokens_ref[...].astype(f32)
    mean = jnp.mean(x, axis=-1, keepdims=True)
    center = x - mean
    r = lax.rsqrt(jnp.mean(center * center, axis=-1, keepdims=True) + EPSILON)
    lane = lax.broadcasted_iota(jnp.int32, out_ref.shape, 1)
    out_ref[...] = jnp.where(lane == 0, mean, r)

def norm(tokens, tm=256):
    R, D = tokens.shape
    return pl.pallas_call(
        norm_kernel, grid=(R // tm,), in_specs=[pl.BlockSpec((tm, D), lambda i: (i, 0))], out_specs=pl.BlockSpec((tm, 128), lambda i: (i, 0)),
        out_shape=jax.ShapeDtypeStruct((R, 128), f32), compiler_params=cp(), name="norm", cost_estimate=HINT,
    )(tokens)

def in_order(order_ref, pieces, whole_ref):
    n, rows, _ = pieces[0].shape
    for p, piece in enumerate(pieces):
        for i in range(n):
            whole_ref[pl.ds(pl.multiple_of(order_ref[p * n + i] * rows, rows), rows), :] = piece[i]

def project_kernel(order_ref, tokens_ref, stat_ref, *refs, count):
    pieces, sides = refs[:count], refs[count:2 * count]
    normed_ref, out_ref, vec_ref, weight_ref, side_ref, all_ref = refs[2 * count:]
    step = pl.program_id(0)
    @pl.when(step == 0)
    def _():
        in_order(order_ref, sides, side_ref)
        all_ref[...] = jnp.transpose(side_ref[...].astype(f32))
        vec_ref[...] = all_ref[:16, :]
        xhat = (tokens_ref[...].astype(f32) - stat_ref[:, 0:1]) * stat_ref[:, 1:2]
        normed_ref[...] = (xhat * all_ref[GAIN1:GAIN1 + 1, :] + all_ref[SHIFT1:SHIFT1 + 1, :]).astype(bf16)
    in_order(order_ref, pieces, weight_ref)
    D = normed_ref.shape[1]
    tn = out_ref.shape[1]
    third = pl.num_programs(0) // 3
    at = pl.ds(pl.multiple_of(lax.rem(step, D // tn) * tn, tn), tn)
    bias = jnp.where(step < third, all_ref[QBIAS:QBIAS + 1, at], jnp.where(step < 2 * third, 0.0, all_ref[VBIAS:VBIAS + 1, at]))
    factor = jnp.where(step < third, 0.125, 1.0)
    out = dot(normed_ref[...], weight_ref[...]) + bias
    out_ref[...] = (out * factor).astype(bf16)

def project(order, tokens, stats, pieces, tn=512):
    R, D = tokens.shape
    n, rows, width = pieces[0].shape
    N = 3 * D
    full = pl.BlockSpec((R, D), lambda j: (0, 0))
    return pl.pallas_call(
        functools.partial(project_kernel, count=len(pieces)), grid=(N // tn,),
        in_specs=[pl.BlockSpec(memory_space=pltpu.SMEM), full, pl.BlockSpec((R, 128), lambda j: (0, 0))]
        + [pl.BlockSpec((n, rows, tn), lambda j: (0, 0, j))] * len(pieces)
        + [pl.BlockSpec((n, rows, 128), lambda j: (0, 0, width // 128 - 1))] * len(pieces),
        out_specs=[full, pl.BlockSpec((R, tn), lambda j: (0, j)), pl.BlockSpec((16, D), lambda j: (0, 0))],
        out_shape=[jax.ShapeDtypeStruct((R, D), bf16), jax.ShapeDtypeStruct((R, N), bf16), jax.ShapeDtypeStruct((16, D), f32)],
        scratch_shapes=[pltpu.VMEM((D, tn), bf16), pltpu.VMEM((D, 128), bf16), pltpu.VMEM((128, D), f32)],
        compiler_params=cp(), name="project", cost_estimate=HINT,
    )(order, tokens, stats, *pieces, *pieces)

def key_bias(prefix, limit, lo, q0, bq, transposed, diagonal):
    shape = (bq, bq)
    kd = 0 if transposed else 1
    k = lo + lax.broadcasted_iota(jnp.int32, shape, kd)
    ok = k < limit
    if diagonal:
        q = q0 + lax.broadcasted_iota(jnp.int32, shape, 1 - kd)
        ok = ok & ((k < prefix) | (k <= q))
    return jnp.where(ok, 0.0, NEGATIVE)

def attend_kernel(prefix_ref, padding_ref, q_ref, k_ref, v_ref, out_ref, lse_ref, bias_ref, *, bq):
    L = q_ref.shape[0]
    step = pl.program_id(0)
    prefix = prefix_ref[0]
    limit = L - padding_ref[0]
    n = L // bq
    lane = lax.broadcasted_iota(jnp.int32, (1, 128), 1)
    @pl.when(step == 0)
    def _():
        for b in range(n):
            bias_ref[b] = key_bias(prefix, limit, b * bq, b * bq, bq, True, True)
    vT = jnp.transpose(v_ref[...])
    ones = jnp.ones((16, L), bf16)
    values = [jnp.concatenate([vT[64 * h:64 * h + 64], ones], axis=0) for h in range(2)]
    for b in range(n):
        start, stop = b * bq, (b + 1) * bq
        q = q_ref[start:stop, :]
        both = jnp.concatenate([jnp.where(lane < 64, q, 0), jnp.where(lane >= 64, q, 0)], axis=0).astype(bf16)
        s = []
        for kb in range(b + 1):
            t = dot_nt(k_ref[kb * bq:(kb + 1) * bq, :], both)
            if kb == b:
                t = t + jnp.concatenate([bias_ref[b], bias_ref[b]], axis=1)
            elif (kb + 1) * bq > L - 384:
                kk = kb * bq + lax.broadcasted_iota(jnp.int32, (bq, 1), 0)
                t = t + jnp.where(kk < limit, 0.0, NEGATIVE)
            s.append(t)
        m = functools.reduce(jnp.maximum, [jnp.max(t, axis=0, keepdims=True) for t in s])
        acc = [None, None]
        for kb in range(b + 1):
            e = jnp.exp(s[kb] - m).astype(bf16)
            for h in range(2):
                t = dot(values[h][:, kb * bq:(kb + 1) * bq], e[:, h * bq:(h + 1) * bq])
                acc[h] = t if acc[h] is None else acc[h] + t
        ctx = [a[:64] * (1.0 / a[64:65]) for a in acc]
        out_ref[start:stop, :] = jnp.transpose(jnp.concatenate(ctx, axis=0)).astype(bf16)
        for h in range(2):
            lse_ref[pl.ds(2 * step + h, 1), start:stop] = m[:, h * bq:(h + 1) * bq] + jnp.log(acc[h][64:65])

def attend(prefix, padding, qkv, bq=256):
    L = qkv.shape[0]
    D = qkv.shape[1] // 3
    n = D // 128
    smem = pl.BlockSpec(memory_space=pltpu.SMEM)
    col = lambda off: pl.BlockSpec((L, 128), lambda j: (0, j + off))
    return pl.pallas_call(
        functools.partial(attend_kernel, bq=bq), grid=(n,),
        in_specs=[smem, smem, col(0), col(n), col(2 * n)],
        out_specs=[col(0), pl.BlockSpec((2 * n, L), lambda j: (0, 0))],
        out_shape=[jax.ShapeDtypeStruct((L, D), bf16), jax.ShapeDtypeStruct((2 * n, L), f32)],
        scratch_shapes=[pltpu.VMEM((L // bq, bq, bq), f32)],
        compiler_params=cp(), name="attend",
        cost_estimate=HINT,
    )(prefix, padding, qkv, qkv, qkv)

def branch_kernel(order_ref, ctx_ref, tokens_ref, vec_ref, *refs):
    *pieces, resid_ref, normed_ref, weight_ref = refs
    @pl.when(pl.program_id(0) == 0)
    def _():
        in_order(order_ref, pieces, weight_ref)
    resid = tokens_ref[...].astype(f32) + (dot(ctx_ref[...], weight_ref[...]) + row_of(vec_ref, OBIAS))
    center = resid - jnp.mean(resid, axis=-1, keepdims=True)
    spread = jnp.mean(center * center, axis=-1, keepdims=True)
    normed = center * lax.rsqrt(spread + EPSILON) * row_of(vec_ref, GAIN2) + row_of(vec_ref, SHIFT2)
    resid_ref[...] = resid
    normed_ref[...] = normed.astype(bf16)

def branch(order, ctx, tokens, vecs, pieces, tm=256):
    R, D = ctx.shape
    n, high, _ = pieces[0].shape
    rows = pl.BlockSpec((tm, D), lambda i: (i, 0))
    return pl.pallas_call(
        branch_kernel, grid=(R // tm,),
        in_specs=[pl.BlockSpec(memory_space=pltpu.SMEM), rows, rows, pl.BlockSpec(vecs.shape, lambda i: (0, 0))]
        + [pl.BlockSpec((n, high, D), lambda i: (0, 0, 3))] * len(pieces),
        out_specs=[rows, rows, pl.BlockSpec((D, D), lambda i: (0, 0))],
        out_shape=[jax.ShapeDtypeStruct((R, D), f32), jax.ShapeDtypeStruct((R, D), bf16), jax.ShapeDtypeStruct((D, D), bf16)],
        compiler_params=cp(), name="branch", cost_estimate=HINT,
    )(order, ctx, tokens, vecs, *pieces)

def ffn_kernel(pos_ref, normed_ref, grad_ref, vec_ref, rows_ref, up_ref, down_ref, resid_in, weight_in,
               result_out, low_out, dctx_out, keep1_ref, send1_ref, keep2_ref, send2_ref, biasg_ref, small_ref,
               out_ref, dn_ref, ups_ref, dns_ref, resid_ref, weight_ref, result_ref, low_ref, dctx_ref, up_sem, dn_sem, in_sem, out_sem, *, shards, per, blocks, tm):
    step = pl.program_id(0)
    last = pl.num_programs(0) - 1
    D = normed_ref.shape[1]
    tf = ups_ref.shape[3]
    half = shards // 2
    rows = D // shards
    each = blocks // 2
    slot = lax.rem(step, 2)
    block = lax.div(step, per)
    bslot = lax.rem(block, 2)
    groups = ((keep1_ref, send1_ref), (keep2_ref, send2_ref))

    def up_copies(slot, step, group):
        cols = pl.ds(pl.multiple_of(step * tf - group * each * D, tf), tf)
        return [pltpu.make_async_copy(ups_ref.at[slot, pl.ds(k * half, half)], groups[group][k].at[:, :, cols], up_sem.at[slot, k]) for k in range(2)]

    def down_copies(bslot, block, group):
        cols = pl.ds(pl.multiple_of((each + block - group * each) * D, D), D)
        return [pltpu.make_async_copy(dns_ref.at[bslot, pl.ds(k * half, half)], groups[group][k].at[:, :, cols], dn_sem.at[bslot, k]) for k in range(2)]

    def each_group(block, do):
        for group in range(2):
            pl.when((block >= group * each) & (block < (group + 1) * each))(functools.partial(do, group))

    def start_up(group):
        for c in up_copies(slot, step, group):
            c.start()

    def wait_up(slot, step):
        def do(group):
            for c in up_copies(slot, step, group):
                c.wait()
        each_group(lax.div(step, per), do)

    def start_down(group):
        for c in down_copies(bslot, block, group):
            c.start()

    def wait_down(bslot, block):
        def do(group):
            for c in down_copies(bslot, block, group):
                c.wait()
        each_group(block, do)

    loads = [pltpu.make_async_copy(resid_in, resid_ref, in_sem.at[0]), pltpu.make_async_copy(weight_in, weight_ref, in_sem.at[1])]

    @pl.when(step == 0)
    def _():
        for c in loads:
            c.start()
        out_ref[...] = jnp.zeros_like(out_ref)
        dn_ref[...] = jnp.zeros_like(dn_ref)

    @pl.when(step >= 2)
    def _():
        wait_up(slot, step - 2)

    @pl.when((step >= 2 * per) & (lax.rem(step, per) == 0))
    def _():
        wait_down(bslot, block - 2)

    n2 = normed_ref[...]
    go = grad_ref[...]
    up = up_ref[...]
    down = down_ref[...]
    bias = row_of(vec_ref, UBIAS)
    for k in range(1, blocks):
        bias = jnp.where(block == k, row_of(vec_ref, UBIAS + k), bias)
    u = dot(n2, up) + bias
    cdf = 0.5 * (1.0 + lax.erf(u * math.sqrt(0.5)))
    a = (u * cdf).astype(bf16)
    slope = cdf + u * (jnp.exp(-0.5 * u * u) * (1.0 / math.sqrt(2 * math.pi)))
    du = (dot_nt(go, down) * slope).astype(bf16)
    out_ref[...] += dot(a, down)
    dn_ref[...] += dot_nt(du, up)
    biasg_ref[...] = jnp.sum(du.astype(f32), axis=0, keepdims=True)
    upg = dot_tn(n2, du).astype(bf16)
    for i in range(shards):
        ups_ref[slot, pos_ref[i]] = upg[i * rows:(i + 1) * rows]
    downg = dot_tn(a, go).astype(bf16)
    here = tf // rows
    at = lax.rem(step, per) * here
    for i in range(here):
        dns_ref[bslot, pos_ref[at + i]] = downg[i * rows:(i + 1) * rows]
    each_group(block, start_up)

    @pl.when(lax.rem(step, per) == per - 1)
    def _():
        each_group(block, start_down)

    @pl.when(step == last)
    def _():
        for c in loads:
            c.wait()
        small_ref[...] = jnp.zeros_like(small_ref)
        pairs = ((result_ref, result_out), (low_ref, low_out), (dctx_ref, dctx_out))

        def stores(i):
            at = pl.ds(pl.multiple_of(i * tm, tm), tm)
            return [pltpu.make_async_copy(here.at[at], there.at[at], out_sem.at[i, k]) for k, (here, there) in enumerate(pairs)]

        def tile(i, carry):
            at = pl.ds(pl.multiple_of(i * tm, tm), tm)
            resid = resid_ref[at, :]
            result_ref[at, :] = (resid + out_ref[at, :] + row_of(rows_ref, DBIAS)).astype(bf16)
            center = resid - jnp.mean(resid, axis=-1, keepdims=True)
            r = lax.rsqrt(jnp.mean(center * center, axis=-1, keepdims=True) + EPSILON)
            nhat = center * r
            dn = dn_ref[at, :]
            go = grad_ref[at, :].astype(f32)
            e = dn * row_of(rows_ref, GAIN2)
            low = (go + r * (e - jnp.mean(e, axis=-1, keepdims=True) - nhat * jnp.mean(e * nhat, axis=-1, keepdims=True))).astype(bf16)
            low_ref[at, :] = low
            dctx_ref[at, :] = dot_nt(low, weight_ref[...]).astype(bf16)
            small_ref[0:1, :] += jnp.sum(dn * nhat, axis=0, keepdims=True)
            small_ref[1:2, :] += jnp.sum(dn, axis=0, keepdims=True)
            small_ref[2:3, :] += jnp.sum(low.astype(f32), axis=0, keepdims=True)
            small_ref[3:4, :] += jnp.sum(go, axis=0, keepdims=True)
            for c in stores(i):
                c.start()
            return carry

        tiles = resid_ref.shape[0] // tm
        lax.fori_loop(0, tiles, tile, 0)
        for i in range(tiles):
            for c in stores(i):
                c.wait()
        for c in up_copies(1 - slot, step - 1, 1) + up_copies(slot, step, 1) + down_copies(1 - bslot, block - 1, 1) + down_copies(bslot, block, 1):
            c.wait()

def ffn(pos, normed, grad, vecs, wide, resid, weight, tf=512, tm=256):
    R, D = normed.shape
    blocks = wide.shape[1] // D // 2
    F = blocks * D
    shards = pos.shape[0]
    rows = D // shards
    per = D // tf
    full = pl.BlockSpec((R, D), lambda j: (0, 0))
    hbm = pl.BlockSpec(memory_space=pl.ANY)
    part = jax.ShapeDtypeStruct((shards // 2, rows, F), bf16)
    low = jax.ShapeDtypeStruct((R, D), bf16)
    return pl.pallas_call(
        functools.partial(ffn_kernel, shards=shards, per=per, blocks=blocks, tm=tm), grid=(F // tf,),
        in_specs=[pl.BlockSpec(memory_space=pltpu.SMEM), full, full, pl.BlockSpec((16, tf), lambda j: (0, lax.rem(j, per))), pl.BlockSpec((16, D), lambda j: (0, 0)),
                  pl.BlockSpec((D, tf), lambda j: (0, j)), pl.BlockSpec((tf, D), lambda j: (lax.rem(j, per), blocks + lax.div(j, per))), hbm, hbm],
        out_specs=[hbm] * 7 + [pl.BlockSpec((1, tf), lambda j: (0, j)), pl.BlockSpec((8, D), lambda j: (0, 0))],
        out_shape=[low, low, low, part, part, part, part, jax.ShapeDtypeStruct((1, F), f32), jax.ShapeDtypeStruct((8, D), f32)],
        scratch_shapes=[pltpu.VMEM((R, D), f32), pltpu.VMEM((R, D), f32), pltpu.VMEM((2, shards, rows, tf), bf16), pltpu.VMEM((2, shards, rows, D), bf16),
                        pltpu.VMEM((R, D), f32), pltpu.VMEM((D, D), bf16), pltpu.VMEM((R, D), bf16), pltpu.VMEM((R, D), bf16), pltpu.VMEM((R, D), bf16),
                        pltpu.SemaphoreType.DMA((2, 2)), pltpu.SemaphoreType.DMA((2, 2)), pltpu.SemaphoreType.DMA((2,)), pltpu.SemaphoreType.DMA((R // tm, 3))],
        compiler_params=cp(), name="ffn", cost_estimate=HINT,
    )(pos, normed, grad, vecs, vecs, wide, wide, resid, weight)

def attend_back_kernel(prefix_ref, padding_ref, q_ref, k_ref, v_ref, do_ref, o_ref, lse_ref, *refs, bq, first):
    d_ref, small_ref, dka_ref, dva_ref, bias_ref = refs[-5:]
    L = q_ref.shape[0]
    step = pl.program_id(0) + first
    prefix = prefix_ref[0]
    limit = L - padding_ref[0]
    n = L // bq
    lane = lax.broadcasted_iota(jnp.int32, (1, 128), 1)
    @pl.when(pl.program_id(0) == 0)
    def _():
        for b in range(n):
            bias_ref[b] = key_bias(prefix, limit, b * bq, b * bq, bq, True, True)
    kT = jnp.transpose(k_ref[...])
    prod = do_ref[...].astype(f32) * o_ref[...].astype(f32)
    row = lax.broadcasted_iota(jnp.int32, (8, 128), 0)
    col = lax.broadcasted_iota(jnp.int32, (8, 128), 1)
    pick = jnp.where((col // 64) == row, 1.0, 0.0)
    delta = lax.dot_general(pick, prod, (((1,), (1,)), ((), ())), precision=lax.Precision.HIGHEST, preferred_element_type=f32)
    for b in range(n):
        start, stop = b * bq, (b + 1) * bq
        q = q_ref[start:stop, :]
        do = do_ref[start:stop, :]
        both = jnp.concatenate([jnp.where(lane < 64, q, 0), jnp.where(lane >= 64, q, 0)], axis=0).astype(bf16)
        dboth = jnp.concatenate([jnp.where(lane < 64, do, 0), jnp.where(lane >= 64, do, 0)], axis=0).astype(bf16)
        lse = jnp.concatenate([lse_ref[pl.ds(2 * step, 1), start:stop], lse_ref[pl.ds(2 * step + 1, 1), start:stop]], axis=1)
        inner = jnp.concatenate([delta[0:1, start:stop], delta[1:2, start:stop]], axis=1)
        dq = [None, None]
        for kb in range(b + 1):
            ks = slice(kb * bq, (kb + 1) * bq)
            s = dot_nt(k_ref[ks, :], both)
            if kb == b:
                s = s + jnp.concatenate([bias_ref[b], bias_ref[b]], axis=1)
            elif (kb + 1) * bq > L - 384:
                kk = kb * bq + lax.broadcasted_iota(jnp.int32, (bq, 1), 0)
                s = s + jnp.where(kk < limit, 0.0, NEGATIVE)
            p = jnp.exp(s - lse)
            ds = (p * (dot_nt(v_ref[ks, :], dboth) - inner)).astype(bf16)
            tv = dot(p.astype(bf16), dboth)
            tk = dot(ds, both)
            if kb == b:
                dva_ref[ks, :] = tv
                dka_ref[ks, :] = tk
            else:
                dva_ref[ks, :] += tv
                dka_ref[ks, :] += tk
            for h in range(2):
                t = dot(kT[64 * h:64 * h + 64, ks], ds[:, h * bq:(h + 1) * bq])
                dq[h] = t if dq[h] is None else dq[h] + t
        d_ref[0, start:stop, :] = (jnp.transpose(jnp.concatenate(dq, axis=0)) * 0.125).astype(bf16)
    d_ref[1] = dka_ref[...].astype(bf16)
    d_ref[2] = dva_ref[...].astype(bf16)
    small_ref[0:1, :] = jnp.sum(d_ref[0].astype(f32), axis=0, keepdims=True)
    small_ref[1:2, :] = jnp.sum(d_ref[2].astype(f32), axis=0, keepdims=True)

def attend_back(prefix, padding, qkv, dctx, ctx, lse, first, count, width, earlier=(), bq=256):
    L = qkv.shape[0]
    D = dctx.shape[1]
    n = D // 128
    at = first % (width // 128)
    smem = pl.BlockSpec(memory_space=pltpu.SMEM)
    col = lambda off: pl.BlockSpec((L, 128), lambda j: (0, j + off))
    return pl.pallas_call(
        functools.partial(attend_back_kernel, bq=bq, first=first), grid=(count,),
        in_specs=[smem, smem, col(first), col(n + first), col(2 * n + first), col(first), col(first), pl.BlockSpec((2 * n, L), lambda j: (0, 0))]
        + [pl.BlockSpec(memory_space=pl.ANY)] * len(earlier),
        out_specs=[pl.BlockSpec((3, L, 128), lambda j: (0, 0, j + at)), pl.BlockSpec((8, 128), lambda j: (0, j + at))],
        out_shape=[jax.ShapeDtypeStruct((3, L, width), bf16), jax.ShapeDtypeStruct((8, width), f32)],
        scratch_shapes=[pltpu.VMEM((L, 128), f32), pltpu.VMEM((L, 128), f32), pltpu.VMEM((L // bq, bq, bq), f32)],
        input_output_aliases={8 + i: i for i in range(len(earlier))},
        compiler_params=cp(), name="attend_back",
        cost_estimate=HINT,
    )(prefix, padding, qkv, qkv, qkv, dctx, ctx, lse, *earlier)

def weight_grad_kernel(pos_ref, left_ref, d_ref, *refs, each, other, extra):
    refs = list(refs)
    if other:
        low_ref, second_in = refs[:2]
        refs = refs[2:]
    if extra:
        small_ref = refs.pop(0)
    keep_ref, send_ref, stage_ref, stage_sem = refs[:4]
    refs = refs[4:]
    if other:
        second_ref, second_sem = refs[:2]
        refs = refs[2:]
    if extra:
        extra_ref, extra_sem = refs
    step = pl.program_id(0)
    steps = 3 * each + other
    _, shards, rows, tn = stage_ref.shape
    half = shards // 2
    slot = lax.rem(step, 2)

    def copies(slot, step):
        high = pl.ds(pl.multiple_of(lax.div(step, each) * rows, rows), rows)
        cols = pl.ds(pl.multiple_of(lax.rem(step, each) * tn, tn), tn)
        return [pltpu.make_async_copy(stage_ref.at[slot, pl.ds(k * half, half)], out.at[:, high, cols], stage_sem.at[slot, k]) for k, out in enumerate((keep_ref, send_ref))]

    if extra:
        behind = [pltpu.make_async_copy(extra_ref.at[pl.ds(k * half, half)], out.at[:, pl.ds(3 * rows, extra), :], extra_sem.at[k]) for k, out in enumerate((keep_ref, send_ref))]
    if other:
        second = pltpu.make_async_copy(second_in, second_ref, second_sem.at[0])

    @pl.when(step == 0)
    def _():
        if other:
            second.start()
        if extra:
            for i in range(shards):
                extra_ref[pos_ref[i]] = jnp.broadcast_to(small_ref[i:i + 1, :], extra_ref.shape[1:]).astype(bf16)
            for c in behind:
                c.start()

    @pl.when(step >= 2)
    def _():
        for c in copies(slot, step - 2):
            c.wait()

    def put(value):
        for i in range(shards):
            stage_ref[slot, pos_ref[i]] = value[i * rows:(i + 1) * rows].astype(bf16)

    if other:
        @pl.when(step == 3 * each)
        def _():
            second.wait()

        @pl.when(step >= 3 * each)
        def _():
            put(dot_tn(second_ref[...], low_ref[...]))

        @pl.when(step < 3 * each)
        def _():
            put(dot_tn(left_ref[...], d_ref[0]))
    else:
        put(dot_tn(left_ref[...], d_ref[0]))
    for c in copies(slot, step):
        c.start()

    @pl.when(step == steps - 1)
    def _():
        for c in copies(1 - slot, step - 1) + copies(slot, step) + (behind if extra else []):
            c.wait()

def weight_grad(pos, left, d, second=None, low=None, small=None, tn=512):
    R, D = left.shape
    _, _, width = d.shape
    shards = pos.shape[0]
    rows = D // shards
    each = width // tn
    other = D // tn if second is not None else 0
    extra = min(rows, 16) if small is not None else 0
    high = (3 * each + other) // each * rows + extra
    half = jax.ShapeDtypeStruct((shards // 2, high, width), bf16)
    hbm = pl.BlockSpec(memory_space=pl.ANY)
    specs = [pl.BlockSpec(memory_space=pltpu.SMEM), pl.BlockSpec((R, D), lambda j: (0, 0)),
             pl.BlockSpec((1, R, tn), lambda j: (jnp.minimum(lax.div(j, each), 2), 0, jnp.where(j < 3 * each, lax.rem(j, each), each - 1)))]
    args = [pos, left, d]
    scratch = [pltpu.VMEM((2, shards, rows, tn), bf16), pltpu.SemaphoreType.DMA((2, 2))]
    if other:
        specs = specs + [pl.BlockSpec((R, tn), lambda j: (0, jnp.maximum(j - 3 * each, 0))), hbm]
        args = args + [low, second]
        scratch = scratch + [pltpu.VMEM((R, D), bf16), pltpu.SemaphoreType.DMA((1,))]
    if extra:
        specs = specs + [pl.BlockSpec((shards, width), lambda j: (0, 0))]
        args = args + [small]
        scratch = scratch + [pltpu.VMEM((shards, extra, width), bf16), pltpu.SemaphoreType.DMA((2,))]
    return pl.pallas_call(
        functools.partial(weight_grad_kernel, each=each, other=other, extra=extra), grid=(3 * each + other,),
        in_specs=specs, out_specs=[hbm, hbm], out_shape=[half, half], scratch_shapes=scratch,
        compiler_params=cp(), name="weight_grad", cost_estimate=HINT,
    )(*args)

def cotangent_kernel(order_ref, d_ref, *refs, count, final, tm):
    pieces, refs = refs[:count], refs[count:]
    step = pl.program_id(0)
    if final:
        stat_ref, vec_ref, earlier_in, tokens_in, low_in, out_ref, small_ref, weight_ref, acc_ref, earlier_ref, tokens_ref, low_ref, result_ref, in_sem, out_sem = refs
        loads = [pltpu.make_async_copy(a, b, in_sem.at[k]) for k, (a, b) in enumerate(((earlier_in, earlier_ref), (tokens_in, tokens_ref), (low_in, low_ref)))]
        @pl.when(step == 0)
        def _():
            for c in loads:
                c.start()
    else:
        out_ref, weight_ref, acc_ref = refs
    in_order(order_ref, pieces, weight_ref)
    term = dot_nt(d_ref[0], weight_ref[...])
    @pl.when(step == 0)
    def _():
        acc_ref[...] = term
    @pl.when(step > 0)
    def _():
        acc_ref[...] += term

    @pl.when(step == 2)
    def _():
        if not final:
            out_ref[...] = acc_ref[...].astype(bf16)
        else:
            for c in loads:
                c.wait()
            small_ref[...] = jnp.zeros_like(small_ref)
            gain = row_of(vec_ref, GAIN1)
            def store(i):
                at = pl.ds(pl.multiple_of(i * tm, tm), tm)
                return pltpu.make_async_copy(result_ref.at[at], out_ref.at[at], out_sem.at[i])

            def tile(i, carry):
                at = pl.ds(pl.multiple_of(i * tm, tm), tm)
                dn = acc_ref[at, :] + earlier_ref[at, :].astype(f32)
                r = stat_ref[at, 1:2]
                nhat = (tokens_ref[at, :].astype(f32) - stat_ref[at, 0:1]) * r
                e = dn * gain
                d = low_ref[at, :].astype(f32) + r * (e - jnp.mean(e, axis=-1, keepdims=True) - nhat * jnp.mean(e * nhat, axis=-1, keepdims=True))
                result_ref[at, :] = d.astype(bf16)
                small_ref[0:1, :] += jnp.sum(dn * nhat, axis=0, keepdims=True)
                small_ref[1:2, :] += jnp.sum(dn, axis=0, keepdims=True)
                store(i).start()
                return carry

            tiles = acc_ref.shape[0] // tm
            lax.fori_loop(0, tiles, tile, 0)
            for i in range(tiles):
                store(i).wait()

def cotangent(order, d, pieces, number, earlier=None, stats=None, vecs=None, tokens=None, low=None, tm=256):
    _, R, width = d.shape
    n, rows, _ = pieces[0].shape
    D = rows * n * len(pieces)
    per = D // width
    final = earlier is not None
    hbm = pl.BlockSpec(memory_space=pl.ANY)
    specs = [pl.BlockSpec(memory_space=pltpu.SMEM), pl.BlockSpec((1, R, width), lambda j: (j, 0, 0))]
    specs = specs + [pl.BlockSpec((n, rows, width), lambda j: (0, 0, j * per + number))] * len(pieces)
    scratch = [pltpu.VMEM((D, width), bf16), pltpu.VMEM((R, D), f32)]
    result = jax.ShapeDtypeStruct((R, D), bf16)
    more = ()
    if final:
        specs = specs + [pl.BlockSpec((R, 128), lambda j: (0, 0)), pl.BlockSpec(vecs.shape, lambda j: (0, 0)), hbm, hbm, hbm]
        more = (stats, vecs, earlier, tokens, low)
        outs, shapes = [hbm, pl.BlockSpec((2, D), lambda j: (0, 0))], [result, jax.ShapeDtypeStruct((2, D), f32)]
        scratch = scratch + [pltpu.VMEM((R, D), bf16)] * 4 + [pltpu.SemaphoreType.DMA((3,)), pltpu.SemaphoreType.DMA((R // tm,))]
    else:
        outs, shapes = pl.BlockSpec((R, D), lambda j: (0, 0)), result
    return pl.pallas_call(
        functools.partial(cotangent_kernel, count=len(pieces), final=final, tm=tm), grid=(3,),
        in_specs=specs, out_specs=outs, out_shape=shapes, scratch_shapes=scratch,
        compiler_params=cp(), name="cotangent", cost_estimate=HINT,
    )(order, d, *pieces, *more)

def owned_kernel(*refs, counts, rows, blocks, wide):
    parts, at = [], 0
    for c in counts:
        parts.append(sum(r[0].astype(f32) for r in refs[at:at + c]))
        at += c
    up_ref, down_ref = refs[at:]
    half = blocks // len(counts)
    D = down_ref.shape[1]
    for h, part in enumerate(parts):
        for b in range(half):
            down_ref[(h * half + b) * rows:(h * half + b + 1) * rows, :] = part[:, (half + b) * D:(half + b + 1) * D]
    per = D // rows
    group = blocks * rows
    lane = lax.broadcasted_iota(jnp.int32, (rows, 128), 1)
    for tile in range(blocks * D // 128):
        value = None
        for k in range(128 // rows):
            unit = (tile * 128 + k * rows) // rows
            shard, b = unit // blocks, unit % blocks
            source = (b % half) * D + shard * rows
            piece = parts[b // half][:, source // 128 * 128:source // 128 * 128 + 128]
            shift = (k * rows - source % 128) % 128
            if shift:
                piece = pltpu.roll(piece, shift, 1)
            value = piece if value is None else jnp.where(lane >= k * rows, piece, value)
        up_ref[:, tile * 128:(tile + 1) * 128] = value

def owned(groups, D, blocks):
    _, rows, width = groups[0][0].shape
    terms = [t for g in groups for t in g]
    return pl.pallas_call(
        functools.partial(owned_kernel, counts=[len(g) for g in groups], rows=rows, blocks=blocks, wide=width), grid=(1,),
        in_specs=[pl.BlockSpec((1, rows, width), lambda i: (0, 0, 0))] * len(terms),
        out_specs=[pl.BlockSpec((rows, blocks * D), lambda i: (0, 0)), pl.BlockSpec((blocks * rows, D), lambda i: (0, 0))],
        out_shape=[jax.ShapeDtypeStruct((rows, blocks * D), f32), jax.ShapeDtypeStruct((blocks * rows, D), f32)],
        compiler_params=cp(), name="owned", cost_estimate=HINT,
    )(*terms)


class Plan:
    def __init__(self, dp, fsdp):
        self.total = dp * fsdp
        bits = self.total.bit_length() - 1
        low = fsdp.bit_length() - 1
        if fsdp == 4:
            self.core, z, rest = low, list(range(low)), list(range(low + 1, bits))
        else:
            self.core, z, rest = 0, list(range(1, low)), list(range(low, bits))
        a, b = rest[:len(rest) // 2], rest[len(rest) // 2:]
        self.stages = [(a, b), (b, a), (z, z)]
        self.third = len(z) == low

    def masks(self, stage, core):
        bits = self.stages[stage][core]
        return [sum(1 << b for k, b in enumerate(bits) if j >> k & 1) for j in range(1 << len(bits))]

    def pairs(self, stage, j):
        return [(i, i ^ self.masks(stage, i >> self.core & 1)[j]) for i in range(self.total)]

    def size(self, stage):
        return 1 << len(self.stages[stage][0])

    def places(self, me, fixed=False):
        shard = lax.iota(jnp.int32, self.total)
        rel = shard ^ me
        core = (shard >> self.core) & 1
        pos = (rel >> self.core) & 1
        for k, (a, b) in enumerate(self.stages):
            pick = lambda bits, v: sum((((v >> bit) & 1) << k) for k, bit in enumerate(bits))
            own = pick(a, shard) if fixed and k == 2 else jnp.where(core == 0, pick(a, rel), pick(b, rel))
            pos = (pos << len(a)) + own
        return pos

AXES = ("dp", "fsdp")

def swap_core(plan, x):
    return lax.ppermute(x, AXES, [(i, i ^ (1 << plan.core)) for i in range(plan.total)])

def exchange(plan, x, stage, j):
    return lax.ppermute(x, AXES, plan.pairs(stage, j))

class Gathering:
    def __init__(self, plan, shard):
        self.plan, self.shard = plan, shard
        self.arrays = [exchange(plan, shard, 2, j) for j in range(1, plan.size(2))]

    def spread(self):
        column = jnp.stack([self.shard] + self.arrays)
        self.near = [exchange(self.plan, column, 1, j) for j in range(1, self.plan.size(1))]
        self.far = [exchange(self.plan, column, 0, j) for j in range(1, self.plan.size(0))]
        self.arrays = [column] + self.near + self.far

    def spread_again(self):
        n = self.plan.size(1)
        near, far = self.arrays[:n], self.arrays[n:]
        rest = [[exchange(self.plan, p, 0, j + 1) for p in near[1:]] for j in range(len(far))]
        other = [swap_core(self.plan, p) for p in self.arrays]
        self.first, self.other, self.arrays = self.arrays, other, [p for row in rest for p in row]

    def finish(self):
        n = self.plan.size(1)
        sides = (self.first, self.arrays), (self.other, [swap_core(self.plan, p) for p in self.arrays])
        pieces = []
        for first, rest in sides:
            pieces += first[:n]
            for j in range(self.plan.size(0) - 1):
                pieces += [first[n + j]] + rest[j * (n - 1):(j + 1) * (n - 1)]
        return pieces

def step(x, after, *reductions):
    x, _ = tie(x, after, *reductions)
    reductions = [r for r in reductions if r.stage < 3]
    if reductions:
        for r in reductions:
            r.add()
        x, = tie(x, *reductions)
        for r in reductions:
            r.go()
    return x

class Reduction:
    def __init__(self, plan, keep, send, one=False):
        self.plan, self.stage, self.size, self.one = plan, 0, keep.shape[0], one and plan.third
        self.terms = [keep, swap_core(plan, send)]
        self.sent = []

    def add(self):
        n = self.plan.size(self.stage)
        part = self.size // n
        if self.one and self.stage == 2:
            self.sent = [sum(t[:n].astype(f32) for t in self.terms).astype(self.terms[0].dtype)]
            return
        self.sent = [sum(t[j * part:(j + 1) * part].astype(f32) for t in self.terms).astype(self.terms[0].dtype) for j in range(1, n)]

    def go(self):
        if self.one and self.stage == 2:
            self.terms = [lax.psum_scatter(self.sent[0], AXES[1], scatter_dimension=0, tiled=False)[None]]
        else:
            self.terms = self.terms + [exchange(self.plan, s, self.stage, j + 1) for j, s in enumerate(self.sent)]
        self.sent = []
        self.size //= self.plan.size(self.stage)
        self.stage += 1

    def finish(self):
        while self.stage < 3:
            self.add()
            self.go()
        return sum(t[0].astype(f32) for t in self.terms)

def tie(*trees):
    flat = []
    for t in trees:
        flat += t.terms + t.sent if isinstance(t, Reduction) else t.arrays if isinstance(t, Gathering) else [t]
    flat = list(lax.optimization_barrier(tuple(flat)))
    out = []
    for t in trees:
        if isinstance(t, Reduction):
            t.terms = [flat.pop(0) for _ in t.terms]
            t.sent = [flat.pop(0) for _ in t.sent]
        elif isinstance(t, Gathering):
            t.arrays = [flat.pop(0) for _ in t.arrays]
        else:
            out.append(flat.pop(0))
    return out

def body(plan, tokens, prefix_len, padding_len, first_gain, first_shift, inproj_weight, query_bias, value_bias,
         outproj_weight, outproj_bias, second_gain, second_shift, up_weight, up_bias, down_weight, down_bias, grad_out):
    total = plan.total
    R, D = tokens.shape
    F = up_weight.shape[1]
    rows = D // total
    blocks = F // D
    me = lax.axis_index(AXES)
    pos = plan.places(me)
    pos_one = plan.places(me, plan.third)
    shard = lax.iota(jnp.int32, total)
    order = jnp.sum(jnp.where(pos[None, :] == shard[:, None], shard[None, :], 0), axis=1)
    n = first_gain.shape[0]
    half = blocks // 2
    up_local = up_weight.reshape(rows, total, blocks, rows).transpose(0, 2, 1, 3).reshape(rows, F)
    down_local = [down_weight[b * rows:(b + 1) * rows] for b in range(blocks)]
    small = jnp.concatenate([first_gain, first_shift, query_bias, value_bias, outproj_bias, second_gain, second_shift, down_bias, up_bias])
    small = jnp.pad(small.reshape(8 + blocks, rows).T, ((0, 0), (0, 128 - 8 - blocks)))
    inward = Gathering(plan, jnp.concatenate([inproj_weight, outproj_weight, small], axis=1))
    wide = lax.all_gather(jnp.concatenate([up_local] + down_local, axis=1), AXES, axis=0, tiled=True)
    stats = norm(tokens)
    stats, = tie(stats, inward)
    inward.spread()
    stats, = tie(stats, inward)
    inward.spread_again()
    stats, *inward.other = tie(stats, *inward.other, inward)
    inward = inward.finish()
    n1, qkv, vecs = project(order, tokens, stats, inward)
    ctx, lse = attend(prefix_len, padding_len, qkv)
    resid, n2, w_out = branch(order, ctx, tokens, vecs, inward)
    cut = D // 2
    n_pairs = D // 128
    def back(first, x, earlier=()):
        return attend_back(prefix_len, padding_len, qkv, x, ctx, lse, first, n_pairs // 4, cut, earlier)
    out, low, dctx, keep1, send1, keep2, send2, ubias_grad, mid = ffn(pos_one, n2, grad_out, vecs, wide, resid, w_out)
    g1 = Reduction(plan, keep1, send1, True)
    g2 = Reduction(plan, keep2, send2, True)
    d1 = back(0, dctx)
    dctx = step(dctx, d1[0], g1)
    d1 = back(n_pairs // 4, dctx, d1)
    n1a = step(n1, d1[0], g2)
    g3 = Reduction(plan, *weight_grad(pos, n1a, d1[0], ctx, low))
    dctx, _ = tie(dctx, g3.terms[0])
    d2 = back(n_pairs // 2, dctx)
    dctx = step(dctx, d2[0], g1)
    d2 = back(n_pairs * 3 // 4, dctx, d2)
    n1b = step(n1, d2[0], g2, g1)
    per = lambda v: v.reshape(total, -1)
    att = jnp.concatenate([d1[1], d2[1]], axis=1)
    ubg = ubias_grad.reshape(blocks, total, rows).transpose(1, 0, 2).reshape(total, -1)
    early = jnp.concatenate([per(att[0]), per(att[1]), per(mid[2]), per(mid[0]), per(mid[1]), per(mid[3]), ubg], axis=1)
    early = jnp.pad(early, ((0, 0), (0, cut - early.shape[1])))
    g4 = Reduction(plan, *weight_grad(pos, n1b, d2[0], small=early))
    da = step(d1[0], g4.terms[0], g3, g2)
    part = cotangent(order, da, inward, 0)
    part = step(part, part, g4, g1)
    tokens_grad, end = cotangent(order, d2[0], inward, 1, part, stats, vecs, tokens, low)
    bits = [plan.core] + [bit for bit in range(total.bit_length() - 1) if bit != plan.core]
    swap = lambda v, bit: lax.ppermute(v, AXES, [(i, i ^ (1 << bit)) for i in range(total)])
    end = step(end, end, g4)
    other = swap(end, bits[0])
    end = step(end, end, g3)
    end, other = tie(end, other, g4)
    g4.add()
    g4.go()
    arriving = plan.size(2) - 1
    for k, bit in enumerate(bits[1:]):
        end = end + other
        other = swap(end, bit)
        if k < arriving:
            at = k - arriving
            other, g4.terms[at] = tie(other, g4.terms[at])
        if k == 0:
            other = step(other, other, g3, g2)
    late = lax.dynamic_slice_in_dim(end + other, me * n, n, axis=1)
    in1, in2 = g3.finish(), g4.finish()
    up_grad, down_grad = owned([g1.terms, g2.terms], D, blocks)
    out_grad = jnp.concatenate([in1[3 * rows:4 * rows], in1[4 * rows:]], axis=1)
    in_grad = jnp.concatenate([g[k * rows:(k + 1) * rows] for k in range(3) for g in (in1, in2)], axis=1)
    early = in2[3 * rows]
    e = [early[i * n:(i + 1) * n] for i in range(6)]
    return (out, tokens_grad, late[0], late[1], in_grad, e[0], e[1], out_grad, e[2], e[3], e[4], up_grad, early[6 * n:6 * n + F // total], down_grad, e[5])

def solution(mesh):
    plan = Plan(mesh.shape["dp"], mesh.shape["fsdp"])
    rows, flat = P(AXES, None), P(AXES)
    ins = (rows, flat, flat, flat, flat, rows, flat, flat, rows, flat, flat, flat, rows, flat, rows, flat, rows)
    outs = (rows, rows, flat, flat, rows, flat, flat, rows, flat, flat, flat, rows, flat, rows, flat)
    return jax.shard_map(functools.partial(body, plan), mesh=mesh, in_specs=ins, out_specs=outs, check_vma=False)
```
